32 devices in a mesh: rt: 8 (over y, x, core), ct: 4 (over z).
Axes of the slice: x: 2, y: 2, z: 4, core: 2. Of those that a mesh axis runs over, the one named last changes fastest.
Arguments:
- factor_rows: float32 [48, 2, 1024, 1024], P('rt', None, 'ct'), as said below
- slot_row: int32 [48], replicated, may hold values from -1 to 31, as said below
- known: float32 [48, 1024, 256], P('rt', 'ct'), may hold values from -6 to 6
- rhs: float32 [2, 1024, 256], P(None, 'ct', 'rt'), may hold values from -6 to 6
Outputs:
- solved: float32 [2, 1024, 256], P(None, 'ct', 'rt')
The draws below stay inside these ranges and needn't reach their ends.
Inputs may be any that keep to these rules, and one draw needn't show every extreme that they name: `slot_row`: each row tile 0 to 31 stands in exactly one slot; the other slots hold -1. The slots of one index of rt are the 6 consecutive ones; at most 6 are live, and some index of rt has all 6 live. `factor_rows`: diagonal tiles L[0, 0] and L[1, 1] are lower triangular with diagonal entries from 1 to 2; the entry block (0, 1) is zero; entries of empty slots are arbitrary.
All inputs are finite; a program needn't handle non-finite values.
Results may differ from the reference program's by a relative error of at most 0.0003.
Values sent between devices are 32-bit elements; how exact they have to be, the bound alone decides.
No kernel may reach another device: no remote copies, remote signals or barrier semaphores. Data moves between devices by JAX's collectives and lax.ppermute only.
A program may use at most 64 MiB of HBM per device.

```python
import jax
import jax.numpy as jnp
from jax import lax

B = 1024
R = 256
CAP = 6
ROWTILES = 32
SLOTS = 48
N_RT = 8


def slot_layout(key):
    total_slots = N_RT * CAP
    key_full, key_weight, key_score, key_perm = jax.random.split(key, 4)
    chosen = jax.random.randint(key_full, (), 0, N_RT)
    weight = jax.random.randint(key_weight, (N_RT,), 1, 5)
    position = jnp.arange(total_slots, dtype=jnp.int32)
    owner = position // CAP
    base = jax.random.randint(key_score, (total_slots,), 0, 4096)
    score = base * weight[owner] * total_slots + position
    score = jnp.where(owner == chosen, 2 ** 30 + position, score)
    order = jnp.argsort(-score)
    perm = jax.random.permutation(key_perm, ROWTILES).astype(jnp.int32)
    ranked = jnp.concatenate([perm, -jnp.ones((total_slots - ROWTILES,), jnp.int32)])
    return jnp.zeros((total_slots,), jnp.int32).at[order].set(ranked)


def draw_slot_row(key, part):
    return slot_layout(jax.random.fold_in(key, 101))


def draw_factor_rows(key, part):
    rows = slot_layout(jax.random.fold_in(key, 101))
    base_key = jax.random.fold_in(key, 202)
    scale_off = (B * ROWTILES) ** (-0.5)
    row_index = jnp.arange(B)[:, None]
    col_index = jnp.arange(B)[None, :]
    strict = (row_index > col_index).astype(jnp.float32)
    equal = (row_index == col_index).astype(jnp.float32)

    def one_slot(index):
        slot_key = jax.random.fold_in(base_key, index)
        key_off, key_low, key_diag = jax.random.split(slot_key, 3)
        shape = (2, B, B)
        noise = jax.random.normal(key_off, shape, jnp.float32)
        off = noise * scale_off
        lower = jax.random.normal(key_low, shape, jnp.float32) * (0.6 / B ** 0.5)
        diag_vals = jax.random.uniform(key_diag, shape, jnp.float32, 1.0, 2.0)
        tile = strict * lower + equal * diag_vals
        row = rows[index]
        column = jnp.arange(2)[:, None, None]
        is_diag = row == column
        is_zero = (row == 0) & (column == 1)
        return jnp.where(is_diag, tile, jnp.where(is_zero, jnp.zeros_like(off), off))
    return lax.map(one_slot, jnp.arange(N_RT * CAP))


def steps_of(own_key, extent, pieces, least, high):
    def one(dim, shards_of):
        draws = jax.random.uniform(jax.random.fold_in(jax.random.fold_in(own_key, 6), dim), (shards_of,), jnp.float32, least / len(pieces), high / len(pieces))
        return jnp.repeat(jnp.exp(draws), extent[dim] // shards_of).reshape((-1,) + (1,) * (len(extent) - dim - 1))

    gain = one(*pieces[0])
    for cut in pieces[1:]:
        gain = gain * one(*cut)
    return gain


def scatter_about(own_key, extent, deviation, reach, shards=(), kind=jnp.bfloat16):
    result = jax.random.normal(own_key, extent, jnp.float32) * deviation
    if len(shards) > 0:
        result = steps_of(own_key, extent, shards, -0.22, 0.18) * result
    return jnp.clip(result, min=-reach, max=reach).astype(kind)


def setup_inputs(seed: int = 0) -> dict:
    keys = jax.random.split(jax.random.key(seed), 5)
    return {
        "factor_rows": draw_factor_rows(jax.random.fold_in(keys[4], 71), 0),
        "slot_row": draw_slot_row(jax.random.fold_in(keys[4], 71), 0),
        "known": scatter_about(keys[2], (SLOTS, B, R), 1.0, 6.0, ((0, 8), (1, 4)), jnp.float32),
        "rhs": scatter_about(keys[3], (2, B, R), 1.0, 6.0, ((1, 4), (2, 8)), jnp.float32),
    }


def reference(factor_rows, slot_row, known, rhs):
    high = lax.Precision.HIGHEST

    def accumulate(total, item):
        tiles, values, row = item
        term = jnp.einsum('cka,kr->car', tiles, values, precision=high)
        return (total + jnp.where(row >= 2, term, jnp.zeros_like(term)), None)
    start = jnp.zeros((2, B, R), jnp.float32)
    partial_value, unused = lax.scan(accumulate, start, (factor_rows, known, slot_row))
    residual = rhs - partial_value
    first_slot = jnp.argmax(slot_row == 0).astype(jnp.int32)
    second_slot = jnp.argmax(slot_row == 1).astype(jnp.int32)
    diag_zero = factor_rows[first_slot, 0]
    diag_one = factor_rows[second_slot, 1]
    lower_one = factor_rows[second_slot, 0]
    solved_one = lax.linalg.triangular_solve(diag_one, residual[1], left_side=True, lower=True, transpose_a=True)
    coupling = jnp.einsum('ka,kr->ar', lower_one, solved_one, precision=high)
    solved_zero = lax.linalg.triangular_solve(diag_zero, residual[0] - coupling, left_side=True, lower=True, transpose_a=True)
    return jnp.stack([solved_zero, solved_one])
```

```python
import functools

import jax
import jax.numpy as jnp
from jax import lax
from jax.experimental import pallas as pl
from jax.experimental.pallas import tpu as pltpu
from jax.sharding import PartitionSpec as P

F32 = jnp.float32
BF16 = jnp.bfloat16
VMEM = pltpu.MemorySpace.VMEM
SMEM = pltpu.MemorySpace.SMEM


def split(value):
    high = value.astype(BF16)
    return high, (value - high.astype(F32)).astype(BF16)


def dot_split(a, b, dims):
    (ah, al), (bh, bl) = a, b

    def one(u, v):
        return lax.dot_general(u, v, (dims, ((), ())), preferred_element_type=F32)

    return one(al, bh) + one(ah, bl) + one(ah, bh)


def dot3(a, b):
    return dot_split(split(a), split(b), ((1,), (0,)))


def partial_kernel(rows_ref, order_ref, factor_ref, known_ref, out_ref, acc_ref, *, columns, groups):
    step = pl.program_id(0)

    @pl.when(step == 0)
    def _():
        acc_ref[...] = jnp.zeros_like(acc_ref)

    @pl.when(rows_ref[step] >= 2)
    def _():
        acc_ref[...] += dot_split(split(known_ref[0]), split(factor_ref[0, 0]), ((0,), (0,)))

    @pl.when(step == pl.num_programs(0) - 1)
    def _():
        for place in range(groups):
            start = pl.multiple_of(order_ref[place] * columns, columns)
            out_ref[place] = acc_ref[pl.ds(start, columns), :]


def partial_product(local_rows, order, factor_rows, known, column, columns):
    slots, _, band, width = factor_rows.shape
    total = known.shape[2]
    groups = total // columns
    return pl.pallas_call(
        functools.partial(partial_kernel, columns=columns, groups=groups),
        out_shape=jax.ShapeDtypeStruct((groups, columns, width), F32),
        grid_spec=pltpu.PrefetchScalarGridSpec(
            num_scalar_prefetch=2,
            grid=(slots,),
            in_specs=[
                pl.BlockSpec((1, 1, band, width), lambda s, r, o: (s, column, 0, 0)),
                pl.BlockSpec((1, band, total), lambda s, r, o: (s, 0, 0)),
            ],
            out_specs=pl.BlockSpec((groups, columns, width), lambda s, r, o: (0, 0, 0)),
            scratch_shapes=[pltpu.VMEM((total, width), F32)],
        ),
        compiler_params=pltpu.CompilerParams(vmem_limit_bytes=32 << 20),
        name="partial",
    )(local_rows, order, factor_rows, known)


def invert_kernel(block_ref, out_ref):
    size = block_ref.shape[0]
    block = block_ref[...]
    row = lax.broadcasted_iota(jnp.int32, (size, size), 0)
    col = lax.broadcasted_iota(jnp.int32, (size, size), 1)
    diag = jnp.where(row == col, block, 0.0)
    recip_row = 1.0 / jnp.sum(diag, axis=0, keepdims=True)
    recip_col = 1.0 / jnp.sum(diag, axis=1, keepdims=True)
    pair = (row - col == 1) & (lax.rem(row, 2) == 1)
    inverse = jnp.where(row == col, recip_row, jnp.where(pair, -(block * recip_row) * recip_col, 0.0))
    step = 2
    while step < size:
        half = lax.div(row, step)
        below = (half - lax.div(col, step) == 1) & (lax.rem(half, 2) == 1)
        lower = jnp.where(below, block, 0.0)
        parts = split(inverse)
        middle = dot_split(split(lower), parts, ((1,), (0,)))
        inverse = inverse - dot_split(parts, split(middle), ((1,), (0,)))
        step *= 2
    out_ref[...] = inverse


def invert(block):
    return pl.pallas_call(
        invert_kernel,
        out_shape=jax.ShapeDtypeStruct(block.shape, F32),
        in_specs=[pl.BlockSpec(memory_space=VMEM)],
        out_specs=pl.BlockSpec(memory_space=VMEM),
        compiler_params=pltpu.CompilerParams(vmem_limit_bytes=32 << 20),
        name="invert",
    )(block)


def stage_kernel(place_ref, base_ref, inverse_ref, tile_ref, add_ref, message_ref, held_ref, solved_ref, update_ref, *, stage):
    band = base_ref.shape[1]

    @pl.when(place_ref[0] == stage)
    def _():
        message = message_ref[...]
        right = base_ref[...] - message[:, stage * band :]
        solved = dot3(right, inverse_ref[...])
        solved_ref[...] = solved
        if stage > 0:
            update = message[:, : stage * band] + dot3(solved, tile_ref[:, : stage * band])
            update_ref[...] = update + add_ref[:, : stage * band]

    @pl.when(place_ref[0] != stage)
    def _():
        solved_ref[...] = held_ref[...]


def run_stage(place, base, inverse, tile, add, message, held, stage):
    columns, band = base.shape
    width = max(stage, 1) * band
    vmem = pl.BlockSpec(memory_space=VMEM)
    return pl.pallas_call(
        functools.partial(stage_kernel, stage=stage),
        out_shape=(jax.ShapeDtypeStruct((columns, band), F32), jax.ShapeDtypeStruct((columns, width), F32)),
        in_specs=[pl.BlockSpec(memory_space=SMEM)] + [vmem] * 6,
        out_specs=(vmem, vmem),
        compiler_params=pltpu.CompilerParams(vmem_limit_bytes=32 << 20),
        name="stage",
    )(place, base, inverse, tile, add, message, held)


def run_stage_plain(place, base, inverse, tile, add, message, held, stage):
    high = lax.Precision.HIGHEST
    band = base.shape[1]
    right = base - message[:, stage * band :]
    solved = jnp.dot(right, inverse, precision=high)
    active = place[0] == stage
    width = max(stage, 1) * band
    update = jnp.dot(solved, tile[:, :width], precision=high) + add[:, :width]
    if stage > 0:
        update = update + message[:, :width]
    return jnp.where(active, solved, held), update


def sweep(place, base, inverse, tile, add, bands):
    columns, band = base.shape
    run = run_stage if band % 128 == 0 else run_stage_plain
    message = jnp.zeros((columns, bands * band), F32)
    held = jnp.zeros((columns, band), F32)
    for stage in range(bands - 1, -1, -1):
        held, update = run(place, base, inverse, tile, add, message, held, stage)
        if stage > 0:
            message = lax.ppermute(update, "ct", [(stage, stage - 1)])
    return held


def stage_orders(members):
    bits = members.bit_length() - 1
    first = list(range(1, bits))
    return first, first[::-1]


def core_pairs(members):
    return [(i, i ^ 1) for i in range(members)]


def stage_pairs(members, stage):
    orders = stage_orders(members)
    return [(i, i ^ (1 << orders[i & 1][stage])) for i in range(members)]


def send_order(members, me):
    orders = stage_orders(members)
    count = len(orders[0])
    tables = []
    for core in range(2):
        table = []
        for place in range(members):
            other = place >> count
            rest = place & ((1 << count) - 1)
            relative = other
            for stage in range(count):
                if (rest >> (count - 1 - stage)) & 1:
                    relative |= 1 << orders[core ^ other][stage]
            table.append(relative)
        tables.append(jnp.array(table, jnp.int32))
    return me ^ jnp.where((me & 1) == 0, tables[0], tables[1])


def reduce_rows(value, members):
    half = members // 2
    value = value[:half] + lax.ppermute(value[half:], "rt", core_pairs(members))
    stage = 0
    while half > 1:
        half //= 2
        value = value[:half] + lax.ppermute(value[half:], "rt", stage_pairs(members, stage))
        stage += 1
    return value[0]


def share_band(factor_rows, local_rows, row, column, members, core):
    slots, _, band, width = factor_rows.shape
    half = band // 2
    match = local_rows == row
    slot = jnp.argmax(match).astype(jnp.int32)
    mine = jnp.any(match)

    def part(which):
        piece = lax.dynamic_slice(factor_rows, (slot, column, which * half, 0), (1, 1, half, width))
        return jnp.where(mine, piece.reshape(half, width), 0.0)

    value = part(core) + lax.ppermute(part(1 - core), "rt", core_pairs(members))
    for stage in range(len(stage_orders(members)[0])):
        value = value + lax.ppermute(value, "rt", stage_pairs(members, stage))
    other = lax.ppermute(value, "rt", core_pairs(members))
    first = core == 0
    return jnp.concatenate([jnp.where(first, value, other), jnp.where(first, other, value)], 0)


def shards(factor_rows, slot_row, known, rhs, *, members, bands):
    slots, _, band, width = factor_rows.shape
    columns = rhs.shape[2]
    me = lax.axis_index("rt")
    place = lax.axis_index("ct")
    core = me & 1
    place_ref = place.astype(jnp.int32).reshape(1)
    local_rows = lax.dynamic_slice_in_dim(slot_row, me * slots, slots, 0)
    order = send_order(members, me).astype(jnp.int32)

    def own(value, where):
        return lax.dynamic_slice(value, (0, where * band), (value.shape[0], band))

    tile_one = share_band(factor_rows, local_rows, 1, 1, members, core)
    sum_one = reduce_rows(partial_product(local_rows, order, factor_rows, known, 1, columns), members)
    sum_zero = reduce_rows(partial_product(local_rows, order, factor_rows, known, 0, columns), members)
    tile_lower = share_band(factor_rows, local_rows, 1, 0, members, core)
    tile_zero = share_band(factor_rows, local_rows, 0, 0, members, core)
    inverse_one = invert(own(tile_one, place))
    inverse_zero = invert(own(tile_zero, place))

    base = rhs[1].T - own(sum_one, place)
    for shift in range(1, bands):
        piece = own(sum_one, jnp.minimum(place + shift, bands - 1))
        base = base - lax.ppermute(piece, "ct", [(i, i + shift) for i in range(bands - shift)])
    solved_one = sweep(place_ref, base, inverse_one, tile_one, sum_one, bands)

    coupling = sum_zero + jnp.dot(solved_one, tile_lower, precision=lax.Precision.HIGH)
    base = rhs[0].T - own(coupling, place)
    for mask in range(bands - 1, 0, -1):
        piece = own(coupling, place ^ mask)
        base = base - lax.ppermute(piece, "ct", [(i, i ^ mask) for i in range(bands)])
    nothing = jnp.zeros((columns, width), F32)
    solved_zero = sweep(place_ref, base, inverse_zero, tile_zero, nothing, bands)
    return jnp.stack([solved_zero.T, solved_one.T])


def solution(mesh):
    members, bands = mesh.shape["rt"], mesh.shape["ct"]
    in_specs = (P("rt", None, "ct", None), P(), P("rt", "ct", None), P(None, "ct", "rt"))
    out_specs = P(None, "ct", "rt")
    body = functools.partial(shards, members=members, bands=bands)
    return jax.shard_map(body, mesh=mesh, in_specs=in_specs, out_specs=out_specs, check_vma=False)
```

```python
import functools

import jax
import jax.numpy as jnp
from jax import lax
from jax.experimental import pallas as pl
from jax.experimental.pallas import tpu as pltpu
from jax.sharding import PartitionSpec as P

F32 = jnp.float32
BF16 = jnp.bfloat16
VMEM = pltpu.MemorySpace.VMEM
SMEM = pltpu.MemorySpace.SMEM


def split(value):
    high = value.astype(BF16)
    return high, (value - high.astype(F32)).astype(BF16)


def dot_split(a, b, dims):
    (ah, al), (bh, bl) = a, b

    def one(u, v):
        return lax.dot_general(u, v, (dims, ((), ())), preferred_element_type=F32)

    return one(al, bh) + one(ah, bl) + one(ah, bh)


def dot3(a, b):
    return dot_split(split(a), split(b), ((1,), (0,)))


def send_tables(members):
    orders = stage_orders(members)
    count = len(orders[0])
    tables = []
    for core in range(2):
        table = []
        for place in range(members):
            other = place >> count
            rest = place & ((1 << count) - 1)
            relative = other
            for stage in range(count):
                if (rest >> (count - 1 - stage)) & 1:
                    relative |= 1 << orders[core ^ other][stage]
            table.append(relative)
        tables.append(table)
    return tables


def partial_kernel(where_ref, rows_ref, factor_ref, known_ref, keep_ref, send_ref, acc_ref, *, columns, tables):
    step = pl.program_id(0)
    slots = pl.num_programs(0)
    me = where_ref[0]

    @pl.when(step == 0)
    def _():
        acc_ref[...] = jnp.zeros_like(acc_ref)

    @pl.when(rows_ref[me * slots + step] >= 2)
    def _():
        acc_ref[...] += dot_split(split(known_ref[0]), split(factor_ref[0, 0]), ((0,), (0,)))

    @pl.when(step == slots - 1)
    def _():
        half = len(tables[0]) // 2
        for spot, (even, odd) in enumerate(zip(*tables)):
            group = me ^ jnp.where((me & 1) == 0, even, odd)
            rows = acc_ref[pl.ds(pl.multiple_of(group * columns, columns), columns), :]
            if spot < half:
                keep_ref[spot] = rows
            else:
                send_ref[spot - half] = rows


def partial_product(where, slot_row, factor_rows, known, column, columns):
    slots, _, band, width = factor_rows.shape
    total = known.shape[2]
    groups = total // columns
    shape = jax.ShapeDtypeStruct((groups // 2, columns, width), F32)
    whole = pl.BlockSpec(shape.shape, lambda s, w, r: (0, 0, 0))
    return pl.pallas_call(
        functools.partial(partial_kernel, columns=columns, tables=send_tables(groups)),
        out_shape=(shape, shape),
        grid_spec=pltpu.PrefetchScalarGridSpec(
            num_scalar_prefetch=2,
            grid=(slots,),
            in_specs=[
                pl.BlockSpec((1, 1, band, width), lambda s, w, r: (s, column, 0, 0)),
                pl.BlockSpec((1, band, total), lambda s, w, r: (s, 0, 0)),
            ],
            out_specs=(whole, whole),
            scratch_shapes=[pltpu.VMEM((total, width), F32)],
        ),
        compiler_params=pltpu.CompilerParams(vmem_limit_bytes=32 << 20),
        name="partial",
    )(where, slot_row, factor_rows, known)


def inverse_of(block):
    size = block.shape[0]
    row = lax.broadcasted_iota(jnp.int32, (size, size), 0)
    col = lax.broadcasted_iota(jnp.int32, (size, size), 1)
    diag = jnp.where(row == col, block, 0.0)
    recip_row = 1.0 / jnp.sum(diag, axis=0, keepdims=True)
    recip_col = 1.0 / jnp.sum(diag, axis=1, keepdims=True)
    pair = (row - col == 1) & (lax.rem(row, 2) == 1)
    inverse = jnp.where(row == col, recip_row, jnp.where(pair, -(block * recip_row) * recip_col, 0.0))
    step = 2
    while step < size:
        half = lax.div(row, step)
        below = (half - lax.div(col, step) == 1) & (lax.rem(half, 2) == 1)
        lower = jnp.where(below, block, 0.0)
        parts = split(inverse)
        middle = dot_split(split(lower), parts, ((1,), (0,)))
        inverse = inverse - dot_split(parts, split(middle), ((1,), (0,)))
        step *= 2
    return inverse


def invert_kernel(block_ref, out_ref):
    out_ref[...] = inverse_of(block_ref[...])


def invert(block):
    return pl.pallas_call(
        invert_kernel,
        out_shape=jax.ShapeDtypeStruct(block.shape, F32),
        in_specs=[pl.BlockSpec(memory_space=VMEM)],
        out_specs=pl.BlockSpec(memory_space=VMEM),
        compiler_params=pltpu.CompilerParams(vmem_limit_bytes=32 << 20),
        name="invert",
    )(block)


def band_kernel(where_ref, rows_ref, factor_ref, keep_ref, send_ref, sems, *, row, column, slots):
    half = keep_ref.shape[0]
    me = where_ref[0]
    core = me & 1
    slot = jnp.int32(-1)
    for s in range(slots):
        slot = jnp.where(rows_ref[me * slots + s] == row, s, slot)

    @pl.when(slot >= 0)
    def _():
        copies = []
        for index, (target, which) in enumerate(((send_ref, 1 - core), (keep_ref, core))):
            start = pl.multiple_of(which * half, half)
            source = factor_ref.at[slot, column, pl.ds(start, half), :]
            copies.append(pltpu.make_async_copy(source, target, sems.at[index]))
        for copy in copies:
            copy.start()
        for copy in copies:
            copy.wait()

    @pl.when(slot < 0)
    def _():
        keep_ref[...] = jnp.zeros_like(keep_ref)
        send_ref[...] = jnp.zeros_like(send_ref)


def inverted_band_kernel(where_ref, rows_ref, factor_ref, keep_ref, send_ref, tile_ref, sem, *, row, column, slots):
    half = keep_ref.shape[0]
    band = 2 * half
    me, place = where_ref[0], where_ref[1]
    core = me & 1
    slot = jnp.int32(-1)
    for s in range(slots):
        slot = jnp.where(rows_ref[me * slots + s] == row, s, slot)

    @pl.when(slot >= 0)
    def _():
        copy = pltpu.make_async_copy(factor_ref.at[slot, column], tile_ref, sem)
        copy.start()
        copy.wait()
        for spot in range(tile_ref.shape[1] // band):

            @pl.when(place == spot)
            def _():
                here = slice(spot * band, (spot + 1) * band)
                tile_ref[:, here] = inverse_of(tile_ref[:, here])

        keep_ref[...] = tile_ref[pl.ds(pl.multiple_of(core * half, half), half), :]
        send_ref[...] = tile_ref[pl.ds(pl.multiple_of((1 - core) * half, half), half), :]

    @pl.when(slot < 0)
    def _():
        keep_ref[...] = jnp.zeros_like(keep_ref)
        send_ref[...] = jnp.zeros_like(send_ref)


def owned_band(where, slot_row, factor_rows, row, column, inverted):
    slots, _, band, width = factor_rows.shape
    shape = jax.ShapeDtypeStruct((band // 2, width), F32)
    vmem = pl.BlockSpec(memory_space=VMEM)
    smem = pl.BlockSpec(memory_space=SMEM)
    if inverted:
        body = inverted_band_kernel
        scratch = [pltpu.VMEM((band, width), F32), pltpu.SemaphoreType.DMA(())]
    else:
        body = band_kernel
        scratch = [pltpu.SemaphoreType.DMA((2,))]
    return pl.pallas_call(
        functools.partial(body, row=row, column=column, slots=slots),
        out_shape=(shape, shape),
        in_specs=[smem, smem, pl.BlockSpec(memory_space=pl.ANY)],
        out_specs=(vmem, vmem),
        scratch_shapes=scratch,
        compiler_params=pltpu.CompilerParams(vmem_limit_bytes=32 << 20),
        name="band",
    )(where, slot_row, factor_rows)


def stage_kernel(place_ref, base_ref, inverse_ref, tile_ref, add_ref, message_ref, held_ref, solved_ref, update_ref, *, stage):
    band = base_ref.shape[1]

    @pl.when(place_ref[0] == stage)
    def _():
        message = message_ref[...]
        right = base_ref[...] - message[:, stage * band :]
        solved = dot3(right, inverse_ref[...])
        solved_ref[...] = solved
        if stage > 0:
            update = message[:, : stage * band] + dot3(solved, tile_ref[:, : stage * band])
            update_ref[...] = update + add_ref[:, : stage * band]

    @pl.when(place_ref[0] != stage)
    def _():
        solved_ref[...] = held_ref[...]


def run_stage(place, base, inverse, tile, add, message, held, stage):
    columns, band = base.shape
    width = max(stage, 1) * band
    vmem = pl.BlockSpec(memory_space=VMEM)
    return pl.pallas_call(
        functools.partial(stage_kernel, stage=stage),
        out_shape=(jax.ShapeDtypeStruct((columns, band), F32), jax.ShapeDtypeStruct((columns, width), F32)),
        in_specs=[pl.BlockSpec(memory_space=SMEM)] + [vmem] * 6,
        out_specs=(vmem, vmem),
        compiler_params=pltpu.CompilerParams(vmem_limit_bytes=32 << 20),
        name="stage",
    )(place, base, inverse, tile, add, message, held)


def run_stage_plain(place, base, inverse, tile, add, message, held, stage):
    high = lax.Precision.HIGHEST
    band = base.shape[1]
    right = base - message[:, stage * band :]
    solved = jnp.dot(right, inverse, precision=high)
    active = place[0] == stage
    width = max(stage, 1) * band
    update = jnp.dot(solved, tile[:, :width], precision=high) + add[:, :width]
    if stage > 0:
        update = update + message[:, :width]
    return jnp.where(active, solved, held), update


def sweep(place, base, inverse, tile, add, bands):
    columns, band = base.shape
    run = run_stage if band % 128 == 0 else run_stage_plain
    message = jnp.zeros((columns, bands * band), F32)
    held = jnp.zeros((columns, band), F32)
    for stage in range(bands - 1, -1, -1):
        held, update = run(place, base, inverse, tile, add, message, held, stage)
        if stage > 0:
            message = lax.ppermute(update, "ct", [(stage, stage - 1)])
    return held


def stage_orders(members):
    bits = members.bit_length() - 1
    first = list(range(1, bits))
    return first, first[::-1]


def swap_core(value, members):
    return lax.ppermute(value, "rt", [(i, i ^ 1) for i in range(members)])


def swap_chip(value, members, stage):
    orders = stage_orders(members)
    return lax.ppermute(value, "rt", [(i, i ^ (1 << orders[i & 1][stage])) for i in range(members)])


def after(value, *others):
    return lax.optimization_barrier((value,) + others)[0]


def join_halves(value, members, core):
    other = swap_core(value, members)
    first = core == 0
    return jnp.concatenate([jnp.where(first, value, other), jnp.where(first, other, value)], 0)


def shards(factor_rows, slot_row, known, rhs, *, members, bands):
    slots, _, band, width = factor_rows.shape
    columns = rhs.shape[2]
    stages = len(stage_orders(members)[0])
    me = lax.axis_index("rt")
    place = lax.axis_index("ct")
    core = me & 1
    where = jnp.stack([me, place]).astype(jnp.int32)
    place_ref = where[1:]
    factor_rows = pltpu.with_memory_space_constraint(factor_rows, pltpu.HBM)
    known = pltpu.with_memory_space_constraint(known, pltpu.HBM)

    def own(value, spot):
        return lax.dynamic_slice(value, (0, spot * band), (value.shape[0], band))

    keep, send = owned_band(where, slot_row, factor_rows, 1, 1, False)
    tile_one = keep + swap_core(send, members)

    keep_one, send_one = partial_product(after(where, tile_one), slot_row, factor_rows, known, 1, columns)
    sum_one = keep_one + swap_core(send_one, members)
    later = after(where, sum_one)
    keep_zero, send_zero = partial_product(later, slot_row, factor_rows, known, 0, columns)
    keep_low, send_low = owned_band(later, slot_row, factor_rows, 1, 0, False)
    keep_top, send_top = owned_band(later, slot_row, factor_rows, 0, 0, True)

    def reduce_step(value, stage):
        half = value.shape[0] // 2
        return value[:half] + swap_chip(value[half:], members, stage)

    for stage in range(stages):
        sum_one = reduce_step(sum_one, stage)
        tile_one = tile_one + swap_chip(tile_one, members, stage)
    sum_one = sum_one[0]

    sum_zero = keep_zero + swap_core(send_zero, members)
    tile_lower = keep_low + swap_core(send_low, members)
    tile_zero = keep_top + swap_core(send_top, members)

    base = rhs[1].T - own(sum_one, place)
    for shift in range(1, bands):
        piece = own(sum_one, jnp.minimum(place + shift, bands - 1))
        base = base - lax.ppermute(piece, "ct", [(i, i + shift) for i in range(bands - shift)])

    tile_one = join_halves(tile_one, members, core)
    inverse_one = invert(own(tile_one, place))

    tile_lower = after(tile_lower, sum_one, tile_one)
    sum_zero = after(sum_zero, sum_one, tile_one)
    for stage in range(stages):
        sum_zero = reduce_step(sum_zero, stage)
        tile_lower = tile_lower + swap_chip(tile_lower, members, stage)
        tile_zero = after(tile_zero, tile_lower)
    sum_zero = sum_zero[0]
    for stage in range(stages):
        tile_zero = tile_zero + swap_chip(tile_zero, members, stage)
    tile_lower = join_halves(tile_lower, members, core)
    tile_zero = join_halves(tile_zero, members, core)
    inverse_zero = own(tile_zero, place)

    solved_one = sweep(place_ref, base, inverse_one, tile_one, sum_one, bands)

    coupling = sum_zero + jnp.dot(solved_one, tile_lower, precision=lax.Precision.HIGH)
    base = rhs[0].T - own(coupling, place)
    for mask in range(bands - 1, 0, -1):
        piece = own(coupling, place ^ mask)
        base = base - lax.ppermute(piece, "ct", [(i, i ^ mask) for i in range(bands)])
    nothing = jnp.zeros((columns, width), F32)
    solved_zero = sweep(place_ref, base, inverse_zero, tile_zero, nothing, bands)
    return jnp.stack([solved_zero.T, solved_one.T])


def solution(mesh):
    members, bands = mesh.shape["rt"], mesh.shape["ct"]
    in_specs = (P("rt", None, "ct", None), P(), P("rt", "ct", None), P(None, "ct", "rt"))
    out_specs = P(None, "ct", "rt")
    body = functools.partial(shards, members=members, bands=bands)
    return jax.shard_map(body, mesh=mesh, in_specs=in_specs, out_specs=out_specs, check_vma=False)
```

```python
import functools

import jax
import jax.numpy as jnp
from jax import lax
from jax.experimental import pallas as pl
from jax.experimental.pallas import tpu as pltpu
from jax.sharding import PartitionSpec as P

F32 = jnp.float32
BF16 = jnp.bfloat16
VMEM = pltpu.MemorySpace.VMEM
SMEM = pltpu.MemorySpace.SMEM


def split(value):
    high = value.astype(BF16)
    return high, (value - high.astype(F32)).astype(BF16)


def dot_split(a, b, dims):
    (ah, al), (bh, bl) = a, b

    def one(u, v):
        return lax.dot_general(u, v, (dims, ((), ())), preferred_element_type=F32)

    return one(al, bh) + one(ah, bl) + one(ah, bh)


def dot3(a, b):
    return dot_split(split(a), split(b), ((1,), (0,)))


def send_tables(members):
    orders = stage_orders(members)
    count = len(orders[0])
    tables = []
    for core in range(2):
        table = []
        for place in range(members):
            other = place >> count
            rest = place & ((1 << count) - 1)
            relative = other
            for stage in range(count):
                if (rest >> (count - 1 - stage)) & 1:
                    relative |= 1 << orders[core ^ other][stage]
            table.append(relative)
        tables.append(table)
    return tables


def partial_kernel(
    where_ref, rows_ref, factor_ref, known_ref, keep_ref, send_ref, factor_buf, known_buf, acc_ref, sems, *, column, tables
):
    slots = factor_buf.shape[0]
    columns = keep_ref.shape[1]
    me = where_ref[0]

    def copies(slot):
        return (
            pltpu.make_async_copy(known_ref.at[slot], known_buf.at[slot], sems.at[0, slot]),
            pltpu.make_async_copy(factor_ref.at[slot, column], factor_buf.at[slot], sems.at[1, slot]),
        )

    for slot in range(slots):

        @pl.when(rows_ref[me * slots + slot] >= 2)
        def _():
            for copy in copies(slot):
                copy.start()

    acc_ref[...] = jnp.zeros_like(acc_ref)
    for slot in range(slots):

        @pl.when(rows_ref[me * slots + slot] >= 2)
        def _():
            for copy in copies(slot):
                copy.wait()
            acc_ref[...] += dot_split(split(known_buf[slot]), split(factor_buf[slot]), ((0,), (0,)))

    half = len(tables[0]) // 2
    for spot, (even, odd) in enumerate(zip(*tables)):
        group = me ^ jnp.where((me & 1) == 0, even, odd)
        rows = acc_ref[pl.ds(pl.multiple_of(group * columns, columns), columns), :]
        if spot < half:
            keep_ref[spot] = rows
        else:
            send_ref[spot - half] = rows


def partial_product(where, slot_row, factor_rows, known, column, columns):
    slots, _, band, width = factor_rows.shape
    total = known.shape[2]
    groups = total // columns
    shape = jax.ShapeDtypeStruct((groups // 2, columns, width), F32)
    vmem = pl.BlockSpec(memory_space=VMEM)
    smem = pl.BlockSpec(memory_space=SMEM)
    hbm = pl.BlockSpec(memory_space=pl.ANY)
    return pl.pallas_call(
        functools.partial(partial_kernel, column=column, tables=send_tables(groups)),
        out_shape=(shape, shape),
        in_specs=[smem, smem, hbm, hbm],
        out_specs=(vmem, vmem),
        scratch_shapes=[
            pltpu.VMEM((slots, band, width), F32),
            pltpu.VMEM((slots, band, total), F32),
            pltpu.VMEM((total, width), F32),
            pltpu.SemaphoreType.DMA((2, slots)),
        ],
        compiler_params=pltpu.CompilerParams(vmem_limit_bytes=40 << 20),
        name="partial",
    )(where, slot_row, factor_rows, known)


def inverse_of(block):
    size = block.shape[0]
    row = lax.broadcasted_iota(jnp.int32, (size, size), 0)
    col = lax.broadcasted_iota(jnp.int32, (size, size), 1)
    diag = jnp.where(row == col, block, 0.0)
    recip_row = 1.0 / jnp.sum(diag, axis=0, keepdims=True)
    recip_col = 1.0 / jnp.sum(diag, axis=1, keepdims=True)
    pair = (row - col == 1) & (lax.rem(row, 2) == 1)
    inverse = jnp.where(row == col, recip_row, jnp.where(pair, -(block * recip_row) * recip_col, 0.0))
    step = 2
    while step < size:
        half = lax.div(row, step)
        below = (half - lax.div(col, step) == 1) & (lax.rem(half, 2) == 1)
        lower = jnp.where(below, block, 0.0)
        parts = split(inverse)
        middle = dot_split(split(lower), parts, ((1,), (0,)))
        inverse = inverse - dot_split(parts, split(middle), ((1,), (0,)))
        step *= 2
    return inverse


def invert_diagonal(tile_ref, place, band):
    for spot in range(tile_ref.shape[1] // band):

        @pl.when(place == spot)
        def _():
            here = slice(spot * band, (spot + 1) * band)
            tile_ref[:, here] = inverse_of(tile_ref[:, here])


def join_kernel(where_ref, mine_ref, other_ref, tile_ref, *, inverted):
    half = mine_ref.shape[0]
    core = where_ref[0] & 1
    tile_ref[pl.ds(pl.multiple_of(core * half, half), half), :] = mine_ref[...]
    tile_ref[pl.ds(pl.multiple_of((1 - core) * half, half), half), :] = other_ref[...]
    if inverted:
        invert_diagonal(tile_ref, where_ref[1], 2 * half)


def join_halves(where, mine, other, inverted):
    half, width = mine.shape
    vmem = pl.BlockSpec(memory_space=VMEM)
    return pl.pallas_call(
        functools.partial(join_kernel, inverted=inverted),
        out_shape=jax.ShapeDtypeStruct((2 * half, width), F32),
        in_specs=[pl.BlockSpec(memory_space=SMEM), vmem, vmem],
        out_specs=vmem,
        compiler_params=pltpu.CompilerParams(vmem_limit_bytes=32 << 20),
        name="join",
    )(where, mine, other)


def band_kernel(where_ref, rows_ref, factor_ref, keep_ref, send_ref, sems, *, row, column, slots):
    half = keep_ref.shape[0]
    me = where_ref[0]
    core = me & 1
    slot = jnp.int32(-1)
    for s in range(slots):
        slot = jnp.where(rows_ref[me * slots + s] == row, s, slot)

    @pl.when(slot >= 0)
    def _():
        copies = []
        for index, (target, which) in enumerate(((send_ref, 1 - core), (keep_ref, core))):
            start = pl.multiple_of(which * half, half)
            source = factor_ref.at[slot, column, pl.ds(start, half), :]
            copies.append(pltpu.make_async_copy(source, target, sems.at[index]))
        for copy in copies:
            copy.start()
        for copy in copies:
            copy.wait()

    @pl.when(slot < 0)
    def _():
        keep_ref[...] = jnp.zeros_like(keep_ref)
        send_ref[...] = jnp.zeros_like(send_ref)


def inverted_band_kernel(where_ref, rows_ref, factor_ref, keep_ref, send_ref, tile_ref, sem, *, row, column, slots):
    half = keep_ref.shape[0]
    band = 2 * half
    me, place = where_ref[0], where_ref[1]
    core = me & 1
    slot = jnp.int32(-1)
    for s in range(slots):
        slot = jnp.where(rows_ref[me * slots + s] == row, s, slot)

    @pl.when(slot >= 0)
    def _():
        copy = pltpu.make_async_copy(factor_ref.at[slot, column], tile_ref, sem)
        copy.start()
        copy.wait()
        invert_diagonal(tile_ref, place, band)
        keep_ref[...] = tile_ref[pl.ds(pl.multiple_of(core * half, half), half), :]
        send_ref[...] = tile_ref[pl.ds(pl.multiple_of((1 - core) * half, half), half), :]

    @pl.when(slot < 0)
    def _():
        keep_ref[...] = jnp.zeros_like(keep_ref)
        send_ref[...] = jnp.zeros_like(send_ref)


def owned_band(where, slot_row, factor_rows, row, column, inverted):
    slots, _, band, width = factor_rows.shape
    shape = jax.ShapeDtypeStruct((band // 2, width), F32)
    vmem = pl.BlockSpec(memory_space=VMEM)
    smem = pl.BlockSpec(memory_space=SMEM)
    if inverted:
        body = inverted_band_kernel
        scratch = [pltpu.VMEM((band, width), F32), pltpu.SemaphoreType.DMA(())]
    else:
        body = band_kernel
        scratch = [pltpu.SemaphoreType.DMA((2,))]
    return pl.pallas_call(
        functools.partial(body, row=row, column=column, slots=slots),
        out_shape=(shape, shape),
        in_specs=[smem, smem, pl.BlockSpec(memory_space=pl.ANY)],
        out_specs=(vmem, vmem),
        scratch_shapes=scratch,
        compiler_params=pltpu.CompilerParams(vmem_limit_bytes=32 << 20),
        name="band",
    )(where, slot_row, factor_rows)


def stage_kernel(where_ref, base_ref, tile_ref, add_ref, message_ref, held_ref, solved_ref, update_ref, *, stage):
    band = base_ref.shape[1]
    left = stage * band

    @pl.when(where_ref[1] == stage)
    def _():
        message = message_ref[...]
        right = base_ref[...] - message[:, left:]
        solved = dot3(right, tile_ref[:, left : left + band])
        solved_ref[...] = solved
        if stage > 0:
            update_ref[...] = message[:, :left] + dot3(solved, tile_ref[:, :left]) + add_ref[:, :left]

    @pl.when(where_ref[1] != stage)
    def _():
        solved_ref[...] = held_ref[...]


def run_stage(where, base, tile, add, message, held, stage):
    columns, band = base.shape
    width = max(stage, 1) * band
    vmem = pl.BlockSpec(memory_space=VMEM)
    return pl.pallas_call(
        functools.partial(stage_kernel, stage=stage),
        out_shape=(jax.ShapeDtypeStruct((columns, band), F32), jax.ShapeDtypeStruct((columns, width), F32)),
        in_specs=[pl.BlockSpec(memory_space=SMEM)] + [vmem] * 5,
        out_specs=(vmem, vmem),
        compiler_params=pltpu.CompilerParams(vmem_limit_bytes=32 << 20),
        name="stage",
    )(where, base, tile, add, message, held)


def run_stage_plain(where, base, tile, add, message, held, stage):
    high = lax.Precision.HIGHEST
    band = base.shape[1]
    left = stage * band
    right = base - message[:, left:]
    solved = jnp.dot(right, tile[:, left : left + band], precision=high)
    width = max(left, band)
    update = jnp.dot(solved, tile[:, :width], precision=high) + add[:, :width]
    if stage > 0:
        update = update + message[:, :width]
    return jnp.where(where[1] == stage, solved, held), update


def first_message(columns, width, band):
    return jnp.zeros((columns, width), F32), jnp.zeros((columns, band), F32)


def hop(update, stage):
    return lax.ppermute(update, "ct", [(stage, stage - 1)])


def stage_orders(members):
    bits = members.bit_length() - 1
    first = list(range(1, bits))
    return first, first[::-1]


def swap_core(value, members):
    return lax.ppermute(value, "rt", [(i, i ^ 1) for i in range(members)])


def swap_chip(value, members, stage):
    orders = stage_orders(members)
    return lax.ppermute(value, "rt", [(i, i ^ (1 << orders[i & 1][stage])) for i in range(members)])


def after(value, *others):
    return lax.optimization_barrier((value,) + others)[0]


def shards(factor_rows, slot_row, known, rhs, *, members, bands):
    slots, _, band, width = factor_rows.shape
    columns = rhs.shape[2]
    stages = len(stage_orders(members)[0])
    run = run_stage if band % 128 == 0 else run_stage_plain
    me = lax.axis_index("rt")
    place = lax.axis_index("ct")
    where = jnp.stack([me, place]).astype(jnp.int32)
    factor_rows = pltpu.with_memory_space_constraint(factor_rows, pltpu.HBM)
    known = pltpu.with_memory_space_constraint(known, pltpu.HBM)

    def own(value, spot):
        return lax.dynamic_slice(value, (0, spot * band), (value.shape[0], band))

    def partial(ready, column):
        return partial_product(ready, slot_row, factor_rows, known, column, columns)

    def owned(ready, row, column, inverted):
        return owned_band(ready, slot_row, factor_rows, row, column, inverted)

    def chip_half(value, stage):
        return swap_chip(value[value.shape[0] // 2 :], members, stage)

    keep, send = owned(where, 1, 1, False)
    tile_one = keep + swap_core(send, members)
    got_tile = swap_chip(tile_one, members, 0)
    keep, send = partial(after(where, tile_one), 1)
    sum_one = keep + swap_core(send, members)
    keep_zero = send_zero = keep_low = send_low = keep_top = send_top = None
    for stage in range(stages):
        got_sum = chip_half(sum_one, stage)
        if stage == 0:
            later = after(where, sum_one)
            keep_zero, send_zero = partial(later, 0)
            keep_low, send_low = owned(after(where, keep_zero), 1, 0, False)
            got_tile, got_sum = after(got_tile, keep_zero, keep_low), after(got_sum, keep_zero, keep_low)
        tile_one = tile_one + got_tile
        if stage < stages - 1:
            got_tile = swap_chip(tile_one, members, stage + 1)
        half = sum_one.shape[0] // 2
        sum_one = sum_one[:half] + after(got_sum, tile_one)
        if stage == 0:
            keep_top, send_top = owned(after(where, sum_one), 0, 0, True)
    sum_one = after(sum_one, keep_top)[0]

    got_up = []
    for shift in range(1, bands):
        piece = own(sum_one, jnp.minimum(place + shift, bands - 1))
        got_up.append(lax.ppermute(piece, "ct", [(i, i + shift) for i in range(bands - shift)]))

    other = swap_core(tile_one, members)
    sum_zero = after(keep_zero, sum_one) + swap_core(after(send_zero, sum_one), members)
    tile_low = after(keep_low, sum_one) + swap_core(after(send_low, sum_one), members)
    tile_top = after(keep_top, sum_one) + swap_core(after(send_top, sum_one), members)
    got_low = swap_chip(after(tile_low, other), members, 0)
    got_zero = chip_half(after(sum_zero, other), 0)
    tile_one = join_halves(where, tile_one, other, True)
    got_top = swap_chip(after(tile_top, tile_low), members, 0)

    base = rhs[1].T - own(sum_one, place)
    for piece in got_up:
        base = base - after(piece, tile_one)

    message, held = first_message(columns, width, band)
    for stage in range(bands - 1, -1, -1):
        held, update = run(where, base, tile_one, sum_one, message, held, stage)
        if stage > 0:
            message = hop(update, stage)
        index = bands - 1 - stage
        if index < stages:
            gate = held
            tile_low = tile_low + after(got_low, gate)
            half = sum_zero.shape[0] // 2
            sum_zero = sum_zero[:half] + after(got_zero, gate)
            tile_top = tile_top + after(got_top, gate, tile_low)
            if index < stages - 1:
                got_low = swap_chip(tile_low, members, index + 1)
                got_zero = chip_half(sum_zero, index + 1)
                got_top = swap_chip(tile_top, members, index + 1)
        if index == stages - 1:
            tile_low = join_halves(where, tile_low, swap_core(tile_low, members), False)
            tile_top_other = swap_core(tile_top, members)
            message = after(message, tile_low, sum_zero)
    solved_one = held
    sum_zero = sum_zero[0]

    coupling = sum_zero + jnp.dot(solved_one, tile_low, precision=lax.Precision.HIGH)
    base = rhs[0].T - own(coupling, place)
    tile_top = join_halves(where, tile_top, tile_top_other, False)
    for mask in range(bands - 1, 0, -1):
        piece = own(coupling, place ^ mask)
        got = lax.ppermute(piece, "ct", [(i, i ^ mask) for i in range(bands)])
        base = base - after(got, tile_top)

    nothing = jnp.zeros((columns, width), F32)
    message, held = first_message(columns, width, band)
    for stage in range(bands - 1, -1, -1):
        held, update = run(where, base, tile_top, nothing, message, held, stage)
        if stage > 0:
            message = hop(update, stage)
    return jnp.stack([held.T, solved_one.T])


def solution(mesh):
    members, bands = mesh.shape["rt"], mesh.shape["ct"]
    in_specs = (P("rt", None, "ct", None), P(), P("rt", "ct", None), P(None, "ct", "rt"))
    out_specs = P(None, "ct", "rt")
    body = functools.partial(shards, members=members, bands=bands)
    return jax.shard_map(body, mesh=mesh, in_specs=in_specs, out_specs=out_specs, check_vma=False)
```

```python
import functools

import jax
import jax.numpy as jnp
from jax import lax
from jax.experimental import pallas as pl
from jax.experimental.pallas import tpu as pltpu
from jax.sharding import PartitionSpec as P

F32 = jnp.float32
BF16 = jnp.bfloat16
VMEM = pl.BlockSpec(memory_space=pltpu.MemorySpace.VMEM)
SMEM = pl.BlockSpec(memory_space=pltpu.MemorySpace.SMEM)
HBM = pl.BlockSpec(memory_space=pl.ANY)


def shape(*dims):
    return jax.ShapeDtypeStruct(dims, F32)


def call(body, out, specs, args, name, scratch=(), aliases=None, micros=1.0):
    multiple = isinstance(out, tuple)
    return pl.pallas_call(
        body,
        out_shape=out,
        in_specs=list(specs),
        out_specs=tuple(VMEM for _ in out) if multiple else VMEM,
        scratch_shapes=list(scratch),
        input_output_aliases=aliases or {},
        compiler_params=pltpu.CompilerParams(vmem_limit_bytes=40 << 20),
        cost_estimate=pl.CostEstimate(flops=0, transcendentals=0, bytes_accessed=int(micros * 3.0e6)),
        name=name,
    )(*args)


def split(value):
    high = value.astype(BF16)
    return high, (value - high.astype(F32)).astype(BF16)


def dot_split(a, b, dims):
    (ah, al), (bh, bl) = a, b

    def one(u, v):
        return lax.dot_general(u, v, (dims, ((), ())), preferred_element_type=F32)

    return one(al, bh) + one(ah, bl) + one(ah, bh)


def dot3(a, b):
    return dot_split(split(a), split(b), ((1,), (0,)))


def stage_orders(members):
    bits = members.bit_length() - 1
    first = list(range(1, bits))
    return first, first[::-1]


def swap_core(value, members):
    return lax.ppermute(value, "rt", [(i, i ^ 1) for i in range(members)])


def swap_chip(value, members, stage):
    orders = stage_orders(members)
    return lax.ppermute(value, "rt", [(i, i ^ (1 << orders[i & 1][stage])) for i in range(members)])


def send_tables(members):
    orders = stage_orders(members)
    count = len(orders[0])
    tables = []
    for core in range(2):
        table = []
        for place in range(members):
            other = place >> count
            rest = place & ((1 << count) - 1)
            relative = other
            for stage in range(count):
                if (rest >> (count - 1 - stage)) & 1:
                    relative |= 1 << orders[core ^ other][stage]
            table.append(relative)
        tables.append(table)
    return tables


def accumulate(where_ref, rows_ref, factor_ref, known_ref, factor_buf, known_buf, acc_ref, sems, column):
    slots = factor_buf.shape[0]
    depth = 2
    me = where_ref[0]

    def live(slot):
        return rows_ref[me * slots + slot] >= 2

    def copies(slot):
        return (
            pltpu.make_async_copy(known_ref.at[slot], known_buf.at[slot], sems.at[0, slot]),
            pltpu.make_async_copy(factor_ref.at[slot, column], factor_buf.at[slot], sems.at[1, slot]),
        )

    def start(slot):
        @pl.when(live(slot))
        def _():
            for copy in copies(slot):
                copy.start()

    for slot in range(min(depth, slots)):
        start(slot)
    acc_ref[...] = jnp.zeros_like(acc_ref)
    for slot in range(slots):

        @pl.when(live(slot))
        def _():
            for copy in copies(slot):
                copy.wait()

        if slot + depth < slots:
            start(slot + depth)

        @pl.when(live(slot))
        def _():
            acc_ref[...] += dot_split(split(known_buf[slot]), split(factor_buf[slot]), ((0,), (0,)))


def in_send_order(where_ref, acc_ref, keep_ref, send_ref, first, tables):
    count = len(tables[0])
    columns = acc_ref.shape[0] // count
    me = where_ref[0]
    for spot, (even, odd) in enumerate(zip(*tables)):
        group = me ^ jnp.where((me & 1) == 0, even, odd)
        rows = acc_ref[pl.ds(pl.multiple_of(group * columns, columns), columns), :]
        target, start = (keep_ref, spot) if spot < count // 2 else (send_ref, spot - count // 2)
        target[first + start * columns : first + (start + 1) * columns, :] = rows


def owned_slot(where_ref, rows_ref, row, slots):
    slot = jnp.int32(-1)
    for s in range(slots):
        slot = jnp.where(rows_ref[where_ref[0] * slots + s] == row, s, slot)
    return slot


def band_copies(where_ref, factor_ref, slot, column, keep_ref, send_ref, first, half, sems):
    core = where_ref[0] & 1
    copies = []
    for index, (target, which) in enumerate(((send_ref, 1 - core), (keep_ref, core))):
        start = pl.multiple_of(which * half, half)
        source = factor_ref.at[slot, column, pl.ds(start, half), :]
        copies.append(pltpu.make_async_copy(source, target.at[pl.ds(first, half), :], sems.at[index]))
    return copies


def put_band(where_ref, rows_ref, factor_ref, row, column, keep_ref, send_ref, first, half, sems):
    slot = owned_slot(where_ref, rows_ref, row, factor_ref.shape[0])

    @pl.when(slot >= 0)
    def _():
        for copy in band_copies(where_ref, factor_ref, slot, column, keep_ref, send_ref, first, half, sems):
            copy.start()

    @pl.when(slot < 0)
    def _():
        keep_ref[first : first + half, :] = jnp.zeros((half, keep_ref.shape[1]), F32)
        send_ref[first : first + half, :] = jnp.zeros((half, keep_ref.shape[1]), F32)

    def finish():
        @pl.when(slot >= 0)
        def _():
            for copy in band_copies(where_ref, factor_ref, slot, column, keep_ref, send_ref, first, half, sems):
                copy.wait()

    return finish


def partial_scratch(slots, band, width, total):
    return [
        pltpu.VMEM((slots, band, width), F32),
        pltpu.VMEM((slots, band, total), F32),
        pltpu.VMEM((total, width), F32),
        pltpu.SemaphoreType.DMA((2, slots)),
    ]


def first_band(where, slot_row, factor_rows):
    _, _, band, width = factor_rows.shape
    half = band // 2

    def body(where_ref, rows_ref, factor_ref, keep_ref, send_ref, sems):
        put_band(where_ref, rows_ref, factor_ref, 1, 1, keep_ref, send_ref, 0, half, sems)()

    out = (shape(half, width), shape(half, width))
    scratch = [pltpu.SemaphoreType.DMA((2,))]
    return call(body, out, (SMEM, SMEM, HBM), (where, slot_row, factor_rows), "first_band", scratch)


def partial_one(where, slot_row, factor_rows, known, members):
    slots, _, band, width = factor_rows.shape
    total = known.shape[2]
    tables = send_tables(members)

    def body(where_ref, rows_ref, factor_ref, known_ref, keep_ref, send_ref, factor_buf, known_buf, acc_ref, sems):
        accumulate(where_ref, rows_ref, factor_ref, known_ref, factor_buf, known_buf, acc_ref, sems, 1)
        in_send_order(where_ref, acc_ref, keep_ref, send_ref, 0, tables)

    out = (shape(total // 2, width), shape(total // 2, width))
    scratch = partial_scratch(slots, band, width, total)
    args = (where, slot_row, factor_rows, known)
    return call(body, out, (SMEM, SMEM, HBM, HBM), args, "partial_one", scratch, micros=5.0)


def pack_rest(where, slot_row, factor_rows, known, members):
    slots, _, band, width = factor_rows.shape
    half, total = band // 2, known.shape[2]
    tables = send_tables(members)

    def body(where_ref, rows_ref, factor_ref, known_ref, keep_ref, send_ref, factor_buf, known_buf, acc_ref, sems, low, top):
        finish_low = put_band(where_ref, rows_ref, factor_ref, 1, 0, keep_ref, send_ref, 0, half, low)
        finish_top = put_band(where_ref, rows_ref, factor_ref, 0, 0, keep_ref, send_ref, half, half, top)
        accumulate(where_ref, rows_ref, factor_ref, known_ref, factor_buf, known_buf, acc_ref, sems, 0)
        in_send_order(where_ref, acc_ref, keep_ref, send_ref, band, tables)
        finish_low()
        finish_top()

    rows = band + total // 2
    out = (shape(rows, width), shape(rows, width))
    scratch = partial_scratch(slots, band, width, total) + [pltpu.SemaphoreType.DMA((2,))] * 2
    args = (where, slot_row, factor_rows, known)
    return call(body, out, (SMEM, SMEM, HBM, HBM), args, "pack_rest", scratch, micros=6.0)


def after(value, *others):
    return lax.optimization_barrier((value,) + others)[0]


def pack_parts(sums, skip, got, tile_rows, final):
    width = got.shape[1]
    count = got.shape[0] - tile_rows
    go = count if final else count // 2

    def add(tiles_ref, sums_ref, got_ref, out_ref, keep_ref):
        out_ref[:tile_rows, :] = tiles_ref[:tile_rows, :] + got_ref[:tile_rows, :]
        keep_ref[...] = sums_ref[skip : skip + go, :] + got_ref[tile_rows : tile_rows + go, :]
        if not final:
            out_ref[tile_rows:, :] = sums_ref[skip + go : skip + count, :] + got_ref[tile_rows + go :, :]

    return add, (shape(tile_rows + count - go, width), shape(go, width))


def pack_step(tiles, sums, skip, got, tile_rows, final):
    add, out = pack_parts(sums, skip, got, tile_rows, final)
    return call(add, out, (VMEM,) * 3, (tiles, sums, got), "pack_step")


def inverse_of(block):
    size = block.shape[0]
    row = lax.broadcasted_iota(jnp.int32, (size, size), 0)
    col = lax.broadcasted_iota(jnp.int32, (size, size), 1)
    diag = jnp.where(row == col, block, 0.0)
    recip_row = 1.0 / jnp.sum(diag, axis=0, keepdims=True)
    recip_col = 1.0 / jnp.sum(diag, axis=1, keepdims=True)
    pair = (row - col == 1) & (lax.rem(row, 2) == 1)
    inverse = jnp.where(row == col, recip_row, jnp.where(pair, -(block * recip_row) * recip_col, 0.0))
    step = 2
    while step < size:
        half = lax.div(row, step)
        below = (half - lax.div(col, step) == 1) & (lax.rem(half, 2) == 1)
        lower = jnp.where(below, block, 0.0)
        parts = split(inverse)
        middle = dot_split(split(lower), parts, ((1,), (0,)))
        inverse = inverse - dot_split(parts, split(middle), ((1,), (0,)))
        step *= 2
    return inverse


def invert_diagonal(tile_ref, place, chosen, band):
    for spot in chosen:

        @pl.when(place == spot)
        def _():
            here = slice(spot * band, (spot + 1) * band)
            tile_ref[:, here] = inverse_of(tile_ref[:, here])


def join_halves(where, mine, other, first, half, chosen):
    width = mine.shape[1]

    def body(where_ref, mine_ref, other_ref, tile_ref):
        core = where_ref[0] & 1
        tile_ref[pl.ds(pl.multiple_of(core * half, half), half), :] = mine_ref[first : first + half, :]
        tile_ref[pl.ds(pl.multiple_of((1 - core) * half, half), half), :] = other_ref[first : first + half, :]
        invert_diagonal(tile_ref, where_ref[1], chosen, 2 * half)

    return call(body, shape(2 * half, width), (SMEM, VMEM, VMEM), (where, mine, other), "join", micros=5.0)


def invert_late(where, tile, chosen):
    band = tile.shape[0]

    def body(where_ref, old_ref, tile_ref):
        invert_diagonal(tile_ref, where_ref[1], chosen, band)

    return call(body, shape(*tile.shape), (SMEM, VMEM), (where, tile), "invert_late", aliases={1: 0}, micros=4.0)


def run_stage(where, base, tile, add, near, far, held, stage, pack=None):
    columns, band = base.shape
    left = stage * band
    last = max(left - band, 0)
    more = () if pack is None else pack[:2] + (pack[3],)
    add_pack, out_pack = (None, ()) if pack is None else pack_parts(*pack[1:])

    def body(where_ref, base_ref, tile_ref, add_ref, near_ref, far_ref, held_ref, *refs):
        solved_ref, update_ref = refs[len(more) : len(more) + 2]

        @pl.when(where_ref[1] == stage)
        def _():
            right = base_ref[...] - near_ref[...] - far_ref[:, left : left + band]
            solved = dot3(right, tile_ref[:, left : left + band])
            solved_ref[...] = solved
            if stage > 0:
                here = slice(last, left)
                update_ref[...] = far_ref[:, here] + add_ref[:, here] + dot3(solved, tile_ref[:, here])

        @pl.when(where_ref[1] != stage)
        def _():
            solved_ref[...] = held_ref[...]

        if more:
            add_pack(*refs[: len(more)], *refs[len(more) + 2 :])

    out = (shape(columns, band), shape(columns, band)) + out_pack
    specs = (SMEM,) + (VMEM,) * (6 + len(more))
    return call(body, out, specs, (where, base, tile, add, near, far, held) + more, "stage")


def run_rest(where, tile, add, far, solved, stage):
    columns, band = solved.shape
    last = (stage - 1) * band

    def body(where_ref, tile_ref, add_ref, far_ref, solved_ref, rest_ref):
        @pl.when(where_ref[1] == stage)
        def _():
            rest_ref[...] = far_ref[:, :last] + add_ref[:, :last] + dot3(solved_ref[...], tile_ref[:, :last])

    return call(body, shape(columns, last), (SMEM,) + (VMEM,) * 4, (where, tile, add, far, solved), "rest", micros=3.0)


def run_stage_plain(where, base, tile, add, near, far, held, stage, pack=None):
    high = lax.Precision.HIGHEST
    band = base.shape[1]
    left = stage * band
    here = slice(max(left - band, 0), max(left, band))
    solved = jnp.dot(base - near - far[:, left : left + band], tile[:, left : left + band], precision=high)
    update = jnp.dot(solved, tile[:, here], precision=high) + add[:, here] + far[:, here]
    more = () if pack is None else tuple(pack_step(*pack))
    return (jnp.where(where[1] == stage, solved, held), update) + more


def run_rest_plain(where, tile, add, far, solved, stage):
    last = (stage - 1) * solved.shape[1]
    return far[:, :last] + add[:, :last] + jnp.dot(solved, tile[:, :last], precision=lax.Precision.HIGHEST)


def sweep(where, base, tile, add, bands, packs=None):
    columns, band = base.shape
    aligned = band % 128 == 0
    stage_of, rest_of = (run_stage, run_rest) if aligned else (run_stage_plain, run_rest_plain)
    near = jnp.zeros((columns, band), F32)
    held = jnp.zeros((columns, band), F32)
    fars = [jnp.zeros((columns, bands * band), F32)] * 2
    for stage in range(bands - 1, -1, -1):
        far = fars.pop(0)
        pack = packs.take(stage) if packs else None
        held, update, *more = stage_of(where, base, tile, add, near, far, held, stage, pack)
        if stage > 0:
            near = lax.ppermute(update, "ct", [(stage, stage - 1)])
        if stage > 1:
            rest = rest_of(where, tile, add, far, held, stage)
            fars.append(lax.ppermute(rest, "ct", [(stage, stage - 2)]))
        if more:
            packs.put(*more)
    return held


class Packs:
    def __init__(self, tiles, sums, got, band, steps, at, members):
        self.tiles, self.sums, self.got, self.band = tiles, sums, got, band
        self.step, self.steps, self.at, self.members = 0, steps, at, members

    def take(self, stage):
        if self.step == self.steps or stage != self.at[self.step]:
            return None
        return (self.tiles, self.sums, 0, self.got, self.band, self.step == self.steps - 1)

    def put(self, tiles, sums):
        self.tiles, self.sums, self.step = tiles, sums, self.step + 1
        if self.step < self.steps:
            self.got = swap_chip(tiles, self.members, self.step)
        else:
            self.got = swap_core(tiles, self.members)


def couple(where, sums, solved, tile, bands):
    columns, band = solved.shape

    def body(where_ref, sums_ref, solved_ref, tile_ref, out_ref, whole_ref):
        whole_ref[...] = sums_ref[...] + dot3(solved_ref[...], tile_ref[...])
        for mask in range(bands):
            start = pl.multiple_of((where_ref[1] ^ mask) * band, band)
            out_ref[mask] = whole_ref[:, pl.ds(start, band)]

    scratch = [pltpu.VMEM((columns, bands * band), F32)]
    return call(body, shape(bands, columns, band), (SMEM,) + (VMEM,) * 3, (where, sums, solved, tile), "couple", scratch)


def couple_plain(where, sums, solved, tile, bands):
    band = solved.shape[1]
    whole = sums + jnp.dot(solved, tile, precision=lax.Precision.HIGHEST)
    return jnp.stack([own_band(whole, where[1] ^ mask, band) for mask in range(bands)])


def own_band(value, spot, band):
    return lax.dynamic_slice(value, (0, spot * band), (value.shape[0], band))


def shards(factor_rows, slot_row, known, rhs, *, members, bands):
    slots, _, band, width = factor_rows.shape
    half = band // 2
    columns = rhs.shape[2]
    stages = len(stage_orders(members)[0])
    aligned = band % 128 == 0
    place = lax.axis_index("ct")
    where = jnp.stack([lax.axis_index("rt"), place]).astype(jnp.int32)
    factor_rows = pltpu.with_memory_space_constraint(factor_rows, pltpu.HBM)
    known = pltpu.with_memory_space_constraint(known, pltpu.HBM)

    keep, send = first_band(where, slot_row, factor_rows)
    tile_one = keep + swap_core(send, members)
    got_tile = swap_chip(tile_one, members, 0)
    keep, send = partial_one(after(where, tile_one), slot_row, factor_rows, known, members)
    got_sum = swap_core(send, members)
    tile_one = tile_one + after(got_tile, keep)
    got_tile = swap_chip(tile_one, members, 1) if stages > 1 else None
    sum_one = keep + after(got_sum, tile_one)
    keep = send = None
    for stage in range(stages):
        rows = sum_one.shape[0] // 2
        got_sum = swap_chip(sum_one[rows:], members, stage)
        if stage == 0:
            keep, send = pack_rest(after(where, sum_one), slot_row, factor_rows, known, members)
        if stage < stages - 1:
            tile_one = tile_one + after(got_tile, keep)
            got_tile = swap_chip(tile_one, members, stage + 2) if stage < stages - 2 else None
        sum_one = sum_one[:rows] + after(got_sum, tile_one)
        if stage == 0:
            second = sum_one

    got_up = []
    for shift in range(1, bands):
        piece = own_band(sum_one, jnp.minimum(place + shift, bands - 1), band)
        got_up.append(lax.ppermute(piece, "ct", [(i, i + shift) for i in range(bands - shift)]))

    got = swap_core(after(send, second), members)
    tiles, sums = pack_step(keep, keep, band, after(got, sum_one), band, False)
    got_pack = swap_chip(tiles, members, 0)

    other = swap_core(tile_one, members)
    tile_one = join_halves(after(where, sum_one), tile_one, other, 0, half, range(bands))
    base = rhs[1].T - own_band(sum_one, place, band)
    for piece in got_up:
        base = base - after(piece, tile_one)

    at = [2 * (stages - 1 - step) for step in range(stages)]
    packs = Packs(tiles, sums, got_pack, band, stages, at, members)
    solved_one = sweep(where, base, tile_one, sum_one, bands, packs)
    tile_low = join_halves(where, packs.tiles, packs.got, 0, half, ())
    tile_zero = join_halves(where, packs.tiles, packs.got, half, half, range(1, bands))

    pieces = (couple if aligned else couple_plain)(where, packs.sums, solved_one, tile_low, bands)
    base = rhs[0].T - pieces[0]
    got = [lax.ppermute(pieces[mask], "ct", [(i, i ^ mask) for i in range(bands)]) for mask in range(bands - 1, 0, -1)]
    tile_zero = invert_late(after(where, pieces), tile_zero, (0,))
    for piece in got:
        base = base - after(piece, tile_zero)

    nothing = jnp.zeros((columns, width), F32)
    solved_zero = sweep(where, base, tile_zero, nothing, bands)
    return jnp.stack([solved_zero.T, solved_one.T])


def solution(mesh):
    members, bands = mesh.shape["rt"], mesh.shape["ct"]
    in_specs = (P("rt", None, "ct", None), P(), P("rt", "ct", None), P(None, "ct", "rt"))
    out_specs = P(None, "ct", "rt")
    body = functools.partial(shards, members=members, bands=bands)
    return jax.shard_map(body, mesh=mesh, in_specs=in_specs, out_specs=out_specs, check_vma=False)
```

```python
import functools

import jax
import jax.numpy as jnp
from jax import lax
from jax.experimental import pallas as pl
from jax.experimental.pallas import tpu as pltpu
from jax.sharding import PartitionSpec as P

F32 = jnp.float32
BF16 = jnp.bfloat16
VMEM = pl.BlockSpec(memory_space=pltpu.MemorySpace.VMEM)
SMEM = pl.BlockSpec(memory_space=pltpu.MemorySpace.SMEM)
HBM = pl.BlockSpec(memory_space=pl.ANY)


def shape(*dims):
    return jax.ShapeDtypeStruct(dims, F32)


def call(body, out, specs, args, name, scratch=(), aliases=None):
    multiple = isinstance(out, tuple)
    return pl.pallas_call(
        body,
        out_shape=out,
        in_specs=list(specs),
        out_specs=tuple(VMEM for _ in out) if multiple else VMEM,
        scratch_shapes=list(scratch),
        input_output_aliases=aliases or {},
        compiler_params=pltpu.CompilerParams(vmem_limit_bytes=40 << 20),
        name=name,
    )(*args)


def split(value):
    high = value.astype(BF16)
    return high, (value - high.astype(F32)).astype(BF16)


def dot_split(a, b, dims):
    (ah, al), (bh, bl) = a, b

    def one(u, v):
        return lax.dot_general(u, v, (dims, ((), ())), preferred_element_type=F32)

    return one(al, bh) + one(ah, bl) + one(ah, bh)


def dot3(a, b):
    return dot_split(split(a), split(b), ((1,), (0,)))


def stage_orders(members):
    bits = members.bit_length() - 1
    first = list(range(1, bits))
    return first, first[::-1]


def swap_core(value, members):
    return lax.ppermute(value, "rt", [(i, i ^ 1) for i in range(members)])


def swap_chip(value, members, stage):
    orders = stage_orders(members)
    return lax.ppermute(value, "rt", [(i, i ^ (1 << orders[i & 1][stage])) for i in range(members)])


def send_tables(members):
    orders = stage_orders(members)
    count = len(orders[0])
    tables = []
    for core in range(2):
        table = []
        for place in range(members):
            other = place >> count
            rest = place & ((1 << count) - 1)
            relative = other
            for stage in range(count):
                if (rest >> (count - 1 - stage)) & 1:
                    relative |= 1 << orders[core ^ other][stage]
            table.append(relative)
        tables.append(table)
    return tables


def front_kernel(
    where_ref, rows_ref, factor_ref, known_ref, keep_one, send_one, keep_ref, send_ref, factor_buf, known_buf, acc_ref, sems, low,
    *, tables
):
    slots, _, band, _ = factor_buf.shape
    me = where_ref[0]

    def live(slot):
        return rows_ref[me * slots + slot] >= 2

    def copies(slot, column):
        copy = pltpu.make_async_copy(factor_ref.at[slot, column], factor_buf.at[slot, column], sems.at[column, slot])
        if column == 0:
            return [copy]
        return [pltpu.make_async_copy(known_ref.at[slot], known_buf.at[slot], sems.at[2, slot]), copy]

    for column in (1, 0):
        for slot in range(slots):

            @pl.when(live(slot))
            def _():
                for copy in copies(slot, column):
                    copy.start()

    finish = put_band(where_ref, rows_ref, factor_ref, 1, 0, keep_ref, send_ref, 0, band // 2, low)
    for column, keep, send, first in ((1, keep_one, send_one, 0), (0, keep_ref, send_ref, band // 2)):
        acc_ref[...] = jnp.zeros_like(acc_ref)
        for slot in range(slots):

            @pl.when(live(slot))
            def _():
                for copy in copies(slot, column):
                    copy.wait()
                acc_ref[...] += dot_split(split(known_buf[slot]), split(factor_buf[slot, column]), ((0,), (0,)))

        in_send_order(where_ref, acc_ref, keep, send, first, tables)
    finish()


def in_send_order(where_ref, acc_ref, keep_ref, send_ref, first, tables):
    count = len(tables[0])
    columns = acc_ref.shape[0] // count
    me = where_ref[0]
    for spot, (even, odd) in enumerate(zip(*tables)):
        group = me ^ jnp.where((me & 1) == 0, even, odd)
        rows = acc_ref[pl.ds(pl.multiple_of(group * columns, columns), columns), :]
        target, start = (keep_ref, spot) if spot < count // 2 else (send_ref, spot - count // 2)
        target[first + start * columns : first + (start + 1) * columns, :] = rows


def owned_slot(where_ref, rows_ref, row, slots):
    slot = jnp.int32(-1)
    for s in range(slots):
        slot = jnp.where(rows_ref[where_ref[0] * slots + s] == row, s, slot)
    return slot


def band_copies(where_ref, factor_ref, slot, column, keep_ref, send_ref, first, half, sems):
    core = where_ref[0] & 1
    copies = []
    for index, (target, which) in enumerate(((send_ref, 1 - core), (keep_ref, core))):
        start = pl.multiple_of(which * half, half)
        source = factor_ref.at[slot, column, pl.ds(start, half), :]
        copies.append(pltpu.make_async_copy(source, target.at[pl.ds(first, half), :], sems.at[index]))
    return copies


def put_band(where_ref, rows_ref, factor_ref, row, column, keep_ref, send_ref, first, half, sems):
    slot = owned_slot(where_ref, rows_ref, row, factor_ref.shape[0])

    @pl.when(slot >= 0)
    def _():
        for copy in band_copies(where_ref, factor_ref, slot, column, keep_ref, send_ref, first, half, sems):
            copy.start()

    @pl.when(slot < 0)
    def _():
        keep_ref[first : first + half, :] = jnp.zeros((half, keep_ref.shape[1]), F32)
        send_ref[first : first + half, :] = jnp.zeros((half, keep_ref.shape[1]), F32)

    def finish():
        @pl.when(slot >= 0)
        def _():
            for copy in band_copies(where_ref, factor_ref, slot, column, keep_ref, send_ref, first, half, sems):
                copy.wait()

    return finish


def first_band(where, slot_row, factor_rows):
    _, _, band, width = factor_rows.shape
    half = band // 2

    def body(where_ref, rows_ref, factor_ref, keep_ref, send_ref, sems):
        put_band(where_ref, rows_ref, factor_ref, 1, 1, keep_ref, send_ref, 0, half, sems)()

    out = (shape(half, width), shape(half, width))
    scratch = [pltpu.SemaphoreType.DMA((2,))]
    return call(body, out, (SMEM, SMEM, HBM), (where, slot_row, factor_rows), "first_band", scratch)


def front(where, slot_row, factor_rows, known, members):
    slots, _, band, width = factor_rows.shape
    total = known.shape[2]
    one, rest = shape(total // 2, width), shape(band // 2 + total // 2, width)
    scratch = [
        pltpu.VMEM(factor_rows.shape, F32),
        pltpu.VMEM(known.shape, F32),
        pltpu.VMEM((total, width), F32),
        pltpu.SemaphoreType.DMA((3, slots)),
        pltpu.SemaphoreType.DMA((2,)),
    ]
    body = functools.partial(front_kernel, tables=send_tables(members))
    args = (where, slot_row, factor_rows, known)
    return call(body, (one, one, rest, rest), (SMEM, SMEM, HBM, HBM), args, "front", scratch)


def top_band(where, slot_row, factor_rows):
    slots, _, band, width = factor_rows.shape
    half = band // 2

    def body(where_ref, rows_ref, factor_ref, keep_ref, send_ref, tile_ref, sem):
        slot = owned_slot(where_ref, rows_ref, 0, slots)
        core = where_ref[0] & 1

        @pl.when(slot >= 0)
        def _():
            copy = pltpu.make_async_copy(factor_ref.at[slot, 0], tile_ref, sem)
            copy.start()
            copy.wait()
            invert_diagonal(tile_ref, where_ref[1], range(width // band), band)
            keep_ref[...] = tile_ref[pl.ds(pl.multiple_of(core * half, half), half), :]
            send_ref[...] = tile_ref[pl.ds(pl.multiple_of((1 - core) * half, half), half), :]

        @pl.when(slot < 0)
        def _():
            keep_ref[...] = jnp.zeros_like(keep_ref)
            send_ref[...] = jnp.zeros_like(send_ref)

    out = (shape(half, width), shape(half, width))
    scratch = [pltpu.VMEM((band, width), F32), pltpu.SemaphoreType.DMA(())]
    return call(body, out, (SMEM, SMEM, HBM), (where, slot_row, factor_rows), "top_band", scratch)


def after(value, *others):
    return lax.optimization_barrier((value,) + others)[0]


def pack_parts(sums, skip, got, tile_rows, final):
    width = got.shape[1]
    count = got.shape[0] - tile_rows
    go = count if final else count // 2

    def add(tiles_ref, sums_ref, got_ref, out_ref, keep_ref):
        out_ref[:tile_rows, :] = tiles_ref[:tile_rows, :] + got_ref[:tile_rows, :]
        keep_ref[...] = sums_ref[skip : skip + go, :] + got_ref[tile_rows : tile_rows + go, :]
        if not final:
            out_ref[tile_rows:, :] = sums_ref[skip + go : skip + count, :] + got_ref[tile_rows + go :, :]

    def add_tile(tiles_ref, got_ref, out_ref):
        out_ref[...] = tiles_ref[...] + got_ref[...]

    if sums is None:
        return add_tile, (shape(tile_rows, width),)
    return add, (shape(tile_rows + count - go, width), shape(go, width))


def pack_inputs(tiles, sums, skip, got, tile_rows, final):
    return (tiles, got) if sums is None else (tiles, sums, got)


def pack_step(*pack):
    add, out = pack_parts(*pack[1:])
    args = pack_inputs(*pack)
    return call(add, out, (VMEM,) * len(args), args, "pack_step")


def inverse_of(block):
    size = block.shape[0]
    base = min(size, 64)
    row = lax.broadcasted_iota(jnp.int32, (base, base), 0)
    col = lax.broadcasted_iota(jnp.int32, (base, base), 1)
    pair = (row - col == 1) & (row & 1 == 1)
    starts = range(0, size, base)
    blocks = [block[at : at + base, at : at + base] for at in starts]
    inverses = []
    for part in blocks:
        diag = jnp.where(row == col, part, 0.0)
        recip_row = 1.0 / jnp.sum(diag, axis=0, keepdims=True)
        recip_col = 1.0 / jnp.sum(diag, axis=1, keepdims=True)
        off = -(part * recip_row) * recip_col
        inverses.append(jnp.where(row == col, recip_row, jnp.where(pair, off, 0.0)))
    step = 2
    while step < base:
        half = lax.div(row, step)
        below = (half - lax.div(col, step) == 1) & (half & 1 == 1)
        parts = [split(inverse) for inverse in inverses]
        middle = [dot_split(split(jnp.where(below, b, 0.0)), p, ((1,), (0,))) for b, p in zip(blocks, parts)]
        inverses = [i - dot_split(p, split(m), ((1,), (0,))) for i, p, m in zip(inverses, parts, middle)]
        step *= 2
    width = base
    while len(inverses) > 1:
        merged = []
        for index in range(0, len(inverses), 2):
            first, second = inverses[index : index + 2]
            lower = block[(index + 1) * width : (index + 2) * width, index * width : (index + 1) * width]
            corner = -dot3(second, dot3(lower, first))
            top = jnp.concatenate([first, jnp.zeros_like(first)], 1)
            merged.append(jnp.concatenate([top, jnp.concatenate([corner, second], 1)], 0))
        inverses = merged
        width *= 2
    return inverses[0]


def invert_diagonal(tile_ref, place, chosen, band):
    for spot in chosen:

        @pl.when(place == spot)
        def _():
            here = slice(spot * band, (spot + 1) * band)
            tile_ref[:, here] = inverse_of(tile_ref[:, here])


def join_halves(where, mine, other, first, half, chosen):
    width = mine.shape[1]

    def body(where_ref, mine_ref, other_ref, tile_ref):
        core = where_ref[0] & 1
        tile_ref[pl.ds(pl.multiple_of(core * half, half), half), :] = mine_ref[first : first + half, :]
        tile_ref[pl.ds(pl.multiple_of((1 - core) * half, half), half), :] = other_ref[first : first + half, :]
        invert_diagonal(tile_ref, where_ref[1], chosen, 2 * half)

    return call(body, shape(2 * half, width), (SMEM, VMEM, VMEM), (where, mine, other), "join")


def run_stage(where, base, tile, add, near, far, held, stage, packs=()):
    columns, band = base.shape
    left = stage * band
    last = max(left - band, 0)
    inputs = [pack_inputs(*pack) for pack in packs]
    more = [pack_parts(*pack[1:]) for pack in packs]
    count = sum(len(args) for args in inputs)

    def body(where_ref, base_ref, tile_ref, add_ref, near_ref, far_ref, held_ref, *refs):
        ins, (solved_ref, update_ref), outs = refs[:count], refs[count : count + 2], refs[count + 2 :]

        @pl.when(where_ref[1] == stage)
        def _():
            right = base_ref[...] - near_ref[...] - far_ref[:, left : left + band]
            solved = dot3(right, tile_ref[:, left : left + band])
            solved_ref[...] = solved
            if stage > 0:
                here = slice(last, left)
                update_ref[...] = far_ref[:, here] + add_ref[:, here] + dot3(solved, tile_ref[:, here])

        @pl.when(where_ref[1] != stage)
        def _():
            solved_ref[...] = held_ref[...]

        for args, (add_pack, out) in zip(inputs, more):
            add_pack(*ins[: len(args)], *outs[: len(out)])
            ins, outs = ins[len(args) :], outs[len(out) :]

    out = (shape(columns, band), shape(columns, band)) + sum((out for _, out in more), ())
    args = (where, base, tile, add, near, far, held) + sum(inputs, ())
    return call(body, out, (SMEM,) + (VMEM,) * (len(args) - 1), args, "stage")


def run_rest(where, tile, add, far, solved, stage):
    columns, band = solved.shape
    last = (stage - 1) * band

    def body(where_ref, tile_ref, add_ref, far_ref, solved_ref, rest_ref):
        @pl.when(where_ref[1] == stage)
        def _():
            rest_ref[...] = far_ref[:, :last] + add_ref[:, :last] + dot3(solved_ref[...], tile_ref[:, :last])

    return call(body, shape(columns, last), (SMEM,) + (VMEM,) * 4, (where, tile, add, far, solved), "rest")


def run_stage_plain(where, base, tile, add, near, far, held, stage, packs=()):
    high = lax.Precision.HIGHEST
    band = base.shape[1]
    left = stage * band
    here = slice(max(left - band, 0), max(left, band))
    solved = jnp.dot(base - near - far[:, left : left + band], tile[:, left : left + band], precision=high)
    update = jnp.dot(solved, tile[:, here], precision=high) + add[:, here] + far[:, here]
    more = sum((tuple(pack_step(*pack)) for pack in packs), ())
    return (jnp.where(where[1] == stage, solved, held), update) + more


def run_rest_plain(where, tile, add, far, solved, stage):
    last = (stage - 1) * solved.shape[1]
    return far[:, :last] + add[:, :last] + jnp.dot(solved, tile[:, :last], precision=lax.Precision.HIGHEST)


def sweep(where, base, tile, add, bands, packs=None):
    columns, band = base.shape
    aligned = band % 128 == 0
    stage_of, rest_of = (run_stage, run_rest) if aligned else (run_stage_plain, run_rest_plain)
    near = jnp.zeros((columns, band), F32)
    held = jnp.zeros((columns, band), F32)
    fars = [jnp.zeros((columns, bands * band), F32)] * 2
    for stage in range(bands - 1, -1, -1):
        far = fars.pop(0)
        taken = packs.take(bands - 1 - stage) if packs else ()
        held, update, *more = stage_of(where, base, tile, add, near, far, held, stage, taken)
        if stage > 0:
            near = lax.ppermute(update, "ct", [(stage, stage - 1)])
        if stage > 1:
            rest = rest_of(where, tile, add, far, held, stage)
            fars.append(lax.ppermute(rest, "ct", [(stage, stage - 2)]))
        if more:
            packs.put(*more)
    return held


class Packs:
    def __init__(self, pack, got, top, steps, bands, members):
        self.pack, self.got, self.top, self.got_top = pack, got, top, None
        self.steps, self.members = steps, members
        self.low_at = [bands - 2 - 2 * (steps - 1 - step) for step in range(steps)]
        self.top_at = [bands - steps + step for step in range(steps)]

    def take(self, index):
        taken = ()
        if index in self.low_at:
            tiles, sums, rows = self.pack
            taken += ((tiles, sums, 0, self.got, rows, index == self.low_at[-1]),)
        if index in self.top_at:
            taken += ((self.top, None, 0, self.got_top, self.top.shape[0], True),)
        self.index = index
        return taken

    def put(self, *outs):
        if self.index in self.low_at:
            tiles, sums, *outs = outs
            self.pack = (tiles, sums, self.pack[2])
            step = self.low_at.index(self.index) + 1
            if step < self.steps:
                self.got = swap_chip(tiles, self.members, step)
            else:
                self.got = swap_core(tiles, self.members)
            if step == 1:
                self.got_top = swap_chip(after(self.top, tiles), self.members, 0)
        if self.index in self.top_at:
            (self.top,) = outs
            step = self.top_at.index(self.index) + 1
            if step < self.steps:
                self.got_top = swap_chip(self.top, self.members, step)
            else:
                self.got_top = swap_core(self.top, self.members)


def couple(where, sums, solved, mine, other, bands):
    columns, band = solved.shape
    half, width = mine.shape

    def body(where_ref, sums_ref, solved_ref, mine_ref, other_ref, out_ref, tile_ref, whole_ref):
        core = where_ref[0] & 1
        tile_ref[pl.ds(pl.multiple_of(core * half, half), half), :] = mine_ref[...]
        tile_ref[pl.ds(pl.multiple_of((1 - core) * half, half), half), :] = other_ref[...]
        whole_ref[...] = sums_ref[...] + dot3(solved_ref[...], tile_ref[...])
        for mask in range(bands):
            start = pl.multiple_of((where_ref[1] ^ mask) * band, band)
            out_ref[mask] = whole_ref[:, pl.ds(start, band)]

    scratch = [pltpu.VMEM((band, width), F32), pltpu.VMEM((columns, width), F32)]
    args = (where, sums, solved, mine, other)
    return call(body, shape(bands, columns, band), (SMEM,) + (VMEM,) * 4, args, "couple", scratch)


def couple_plain(where, sums, solved, mine, other, bands):
    band = solved.shape[1]
    tile = join_halves(where, mine, other, 0, band // 2, ())
    whole = sums + jnp.dot(solved, tile, precision=lax.Precision.HIGHEST)
    return jnp.stack([own_band(whole, where[1] ^ mask, band) for mask in range(bands)])


def own_band(value, spot, band):
    return lax.dynamic_slice(value, (0, spot * band), (value.shape[0], band))


def shards(factor_rows, slot_row, known, rhs, *, members, bands):
    slots, _, band, width = factor_rows.shape
    half = band // 2
    columns = rhs.shape[2]
    stages = len(stage_orders(members)[0])
    aligned = band % 128 == 0
    place = lax.axis_index("ct")
    where = jnp.stack([lax.axis_index("rt"), place]).astype(jnp.int32)
    factor_rows = pltpu.with_memory_space_constraint(factor_rows, pltpu.HBM)
    known = pltpu.with_memory_space_constraint(known, pltpu.HBM)

    keep, send = first_band(where, slot_row, factor_rows)
    tile_one = keep + swap_core(send, members)
    got_tile = swap_chip(tile_one, members, 0)
    keep_one, send_one, keep, send = front(after(where, tile_one), slot_row, factor_rows, known, members)
    got_sum = swap_core(send_one, members)
    tile_one = tile_one + after(got_tile, keep_one)
    got_tile = swap_chip(tile_one, members, 1)
    sum_one = keep_one + after(got_sum, tile_one)
    got_pack = got_top = top = None
    for stage in range(stages):
        rows = sum_one.shape[0] // 2
        got_sum = swap_chip(sum_one[rows:], members, stage)
        if stage == 0:
            got_pack = swap_core(after(send, sum_one), members)
            top, send_top = top_band(after(where, sum_one), slot_row, factor_rows)
            got_sum = after(got_sum, top)
        sum_one = sum_one[:rows] + got_sum
        if stage == 0:
            got_top = swap_core(after(send_top, sum_one), members)
        if stage < stages - 1:
            tile_one = tile_one + after(got_tile, sum_one)
            got_tile = swap_chip(tile_one, members, stage + 2) if stage < stages - 2 else None

    got_up = []
    for shift in range(1, bands):
        piece = own_band(sum_one, jnp.minimum(place + shift, bands - 1), band)
        got_up.append(lax.ppermute(piece, "ct", [(i, i + shift) for i in range(bands - shift)]))

    other = swap_core(tile_one, members)

    tiles, sums = pack_step(keep, keep, half, after(got_pack, sum_one), half, False)
    got_pack = swap_chip(tiles, members, 0)
    top = top + after(got_top, sum_one)

    tile_one = join_halves(after(where, sum_one, top), tile_one, other, 0, half, range(bands))
    base = rhs[1].T - own_band(sum_one, place, band)
    for piece in got_up:
        base = base - after(piece, tile_one)

    packs = Packs((tiles, sums, half), got_pack, top, stages, bands, members)
    solved_one = sweep(where, base, tile_one, sum_one, bands, packs)

    low, sums, _ = packs.pack
    pieces = (couple if aligned else couple_plain)(where, sums, solved_one, low, packs.got, bands)
    base = rhs[0].T - pieces[0]
    tile_zero = join_halves(where, packs.top, packs.got_top, 0, half, ())
    for mask in range(bands - 1, 0, -1):
        got = lax.ppermute(pieces[mask], "ct", [(i, i ^ mask) for i in range(bands)])
        base = base - after(got, tile_zero)

    nothing = jnp.zeros((columns, width), F32)
    solved_zero = sweep(where, base, tile_zero, nothing, bands)
    return jnp.stack([solved_zero.T, solved_one.T])


def solution(mesh):
    members, bands = mesh.shape["rt"], mesh.shape["ct"]
    in_specs = (P("rt", None, "ct", None), P(), P("rt", "ct", None), P(None, "ct", "rt"))
    out_specs = P(None, "ct", "rt")
    body = functools.partial(shards, members=members, bands=bands)
    return jax.shard_map(body, mesh=mesh, in_specs=in_specs, out_specs=out_specs, check_vma=False)
```

```python
import functools

import jax
import jax.numpy as jnp
from jax import lax
from jax.experimental import pallas as pl
from jax.experimental.pallas import tpu as pltpu
from jax.sharding import PartitionSpec as P

F32 = jnp.float32
BF16 = jnp.bfloat16
VMEM = pl.BlockSpec(memory_space=pltpu.MemorySpace.VMEM)
SMEM = pl.BlockSpec(memory_space=pltpu.MemorySpace.SMEM)
HBM = pl.BlockSpec(memory_space=pl.ANY)


def shape(*dims):
    return jax.ShapeDtypeStruct(dims, F32)


def call(body, out, specs, args, name, scratch=(), aliases=None):
    multiple = isinstance(out, tuple)
    return pl.pallas_call(
        body,
        out_shape=out,
        in_specs=list(specs),
        out_specs=tuple(VMEM for _ in out) if multiple else VMEM,
        scratch_shapes=list(scratch),
        input_output_aliases=aliases or {},
        compiler_params=pltpu.CompilerParams(vmem_limit_bytes=40 << 20),
        name=name,
    )(*args)


def split(value):
    high = value.astype(BF16)
    return high, (value - high.astype(F32)).astype(BF16)


def dot_split(a, b, dims):
    (ah, al), (bh, bl) = a, b

    def one(u, v):
        return lax.dot_general(u, v, (dims, ((), ())), preferred_element_type=F32)

    return one(al, bh) + one(ah, bl) + one(ah, bh)


def dot3(a, b):
    return dot_split(split(a), split(b), ((1,), (0,)))


def stage_orders(members):
    bits = members.bit_length() - 1
    first = list(range(1, bits))
    return first, first[::-1]


def swap_core(value, members):
    return lax.ppermute(value, "rt", [(i, i ^ 1) for i in range(members)])


def swap_chip(value, members, stage):
    orders = stage_orders(members)
    return lax.ppermute(value, "rt", [(i, i ^ (1 << orders[i & 1][stage])) for i in range(members)])


def send_tables(members):
    orders = stage_orders(members)
    count = len(orders[0])
    tables = []
    for core in range(2):
        table = []
        for place in range(members):
            other = place >> count
            rest = place & ((1 << count) - 1)
            relative = other
            for stage in range(count):
                if (rest >> (count - 1 - stage)) & 1:
                    relative |= 1 << orders[core ^ other][stage]
            table.append(relative)
        tables.append(table)
    return tables


def accumulate(where_ref, rows_ref, factor_ref, known_ref, factor_buf, known_buf, acc_ref, sems, column):
    slots = factor_buf.shape[0]
    me = where_ref[0]

    def live(slot):
        return rows_ref[me * slots + slot] >= 2

    def copies(slot):
        return (
            pltpu.make_async_copy(known_ref.at[slot], known_buf.at[slot], sems.at[0, slot]),
            pltpu.make_async_copy(factor_ref.at[slot, column], factor_buf.at[slot], sems.at[1, slot]),
        )

    for slot in range(slots):

        @pl.when(live(slot))
        def _():
            for copy in copies(slot):
                copy.start()

    acc_ref[...] = jnp.zeros_like(acc_ref)
    for slot in range(slots):

        @pl.when(live(slot))
        def _():
            for copy in copies(slot):
                copy.wait()
            acc_ref[...] += dot_split(split(known_buf[slot]), split(factor_buf[slot]), ((0,), (0,)))


def in_send_order(where_ref, acc_ref, keep_ref, send_ref, first, tables):
    count = len(tables[0])
    columns = acc_ref.shape[0] // count
    me = where_ref[0]
    for spot, (even, odd) in enumerate(zip(*tables)):
        group = me ^ jnp.where((me & 1) == 0, even, odd)
        rows = acc_ref[pl.ds(pl.multiple_of(group * columns, columns), columns), :]
        target, start = (keep_ref, spot) if spot < count // 2 else (send_ref, spot - count // 2)
        target[first + start * columns : first + (start + 1) * columns, :] = rows


def owned_slot(where_ref, rows_ref, row, slots):
    slot = jnp.int32(-1)
    for s in range(slots):
        slot = jnp.where(rows_ref[where_ref[0] * slots + s] == row, s, slot)
    return slot


def band_copies(where_ref, factor_ref, slot, column, keep_ref, send_ref, first, half, sems):
    core = where_ref[0] & 1
    copies = []
    for index, (target, which) in enumerate(((send_ref, 1 - core), (keep_ref, core))):
        start = pl.multiple_of(which * half, half)
        source = factor_ref.at[slot, column, pl.ds(start, half), :]
        copies.append(pltpu.make_async_copy(source, target.at[pl.ds(first, half), :], sems.at[index]))
    return copies


def put_band(where_ref, rows_ref, factor_ref, row, column, keep_ref, send_ref, first, half, sems):
    slot = owned_slot(where_ref, rows_ref, row, factor_ref.shape[0])

    @pl.when(slot >= 0)
    def _():
        for copy in band_copies(where_ref, factor_ref, slot, column, keep_ref, send_ref, first, half, sems):
            copy.start()

    @pl.when(slot < 0)
    def _():
        keep_ref[first : first + half, :] = jnp.zeros((half, keep_ref.shape[1]), F32)
        send_ref[first : first + half, :] = jnp.zeros((half, keep_ref.shape[1]), F32)

    def finish():
        @pl.when(slot >= 0)
        def _():
            for copy in band_copies(where_ref, factor_ref, slot, column, keep_ref, send_ref, first, half, sems):
                copy.wait()

    return finish


def first_band(where, slot_row, factor_rows):
    _, _, band, width = factor_rows.shape
    half = band // 2

    def body(where_ref, rows_ref, factor_ref, keep_ref, send_ref, sems):
        put_band(where_ref, rows_ref, factor_ref, 1, 1, keep_ref, send_ref, 0, half, sems)()

    out = (shape(half, width), shape(half, width))
    scratch = [pltpu.SemaphoreType.DMA((2,))]
    return call(body, out, (SMEM, SMEM, HBM), (where, slot_row, factor_rows), "first_band", scratch)


def partial_scratch(slots, band, width, total):
    return [
        pltpu.VMEM((slots, band, width), F32),
        pltpu.VMEM((slots, band, total), F32),
        pltpu.VMEM((total, width), F32),
        pltpu.SemaphoreType.DMA((2, slots)),
    ]


def partial_one(where, slot_row, factor_rows, known, members):
    slots, _, band, width = factor_rows.shape
    total = known.shape[2]
    tables = send_tables(members)

    def body(where_ref, rows_ref, factor_ref, known_ref, keep_ref, send_ref, factor_buf, known_buf, acc_ref, sems):
        accumulate(where_ref, rows_ref, factor_ref, known_ref, factor_buf, known_buf, acc_ref, sems, 1)
        in_send_order(where_ref, acc_ref, keep_ref, send_ref, 0, tables)

    out = (shape(total // 2, width), shape(total // 2, width))
    args = (where, slot_row, factor_rows, known)
    return call(body, out, (SMEM, SMEM, HBM, HBM), args, "partial_one", partial_scratch(slots, band, width, total))


def pack_rest(where, slot_row, factor_rows, known, members):
    slots, _, band, width = factor_rows.shape
    half, total = band // 2, known.shape[2]
    tables = send_tables(members)

    def body(where_ref, rows_ref, factor_ref, known_ref, keep_ref, send_ref, factor_buf, known_buf, acc_ref, sems, low):
        finish = put_band(where_ref, rows_ref, factor_ref, 1, 0, keep_ref, send_ref, 0, half, low)
        accumulate(where_ref, rows_ref, factor_ref, known_ref, factor_buf, known_buf, acc_ref, sems, 0)
        in_send_order(where_ref, acc_ref, keep_ref, send_ref, half, tables)
        finish()

    rows = half + total // 2
    scratch = partial_scratch(slots, band, width, total) + [pltpu.SemaphoreType.DMA((2,))]
    args = (where, slot_row, factor_rows, known)
    return call(body, (shape(rows, width),) * 2, (SMEM, SMEM, HBM, HBM), args, "pack_rest", scratch)


def top_band(where, slot_row, factor_rows):
    slots, _, band, width = factor_rows.shape
    half = band // 2

    def body(where_ref, rows_ref, factor_ref, keep_ref, send_ref, tile_ref, sem):
        slot = owned_slot(where_ref, rows_ref, 0, slots)
        core = where_ref[0] & 1

        @pl.when(slot >= 0)
        def _():
            copy = pltpu.make_async_copy(factor_ref.at[slot, 0], tile_ref, sem)
            copy.start()
            copy.wait()
            invert_diagonal(tile_ref, where_ref[1], range(width // band), band)
            keep_ref[...] = tile_ref[pl.ds(pl.multiple_of(core * half, half), half), :]
            send_ref[...] = tile_ref[pl.ds(pl.multiple_of((1 - core) * half, half), half), :]

        @pl.when(slot < 0)
        def _():
            keep_ref[...] = jnp.zeros_like(keep_ref)
            send_ref[...] = jnp.zeros_like(send_ref)

    out = (shape(half, width), shape(half, width))
    scratch = [pltpu.VMEM((band, width), F32), pltpu.SemaphoreType.DMA(())]
    return call(body, out, (SMEM, SMEM, HBM), (where, slot_row, factor_rows), "top_band", scratch)


def after(value, *others):
    return lax.optimization_barrier((value,) + others)[0]


def pack_parts(sums, skip, got, tile_rows, final):
    width = got.shape[1]
    count = got.shape[0] - tile_rows
    go = count if final else count // 2

    def add(tiles_ref, sums_ref, got_ref, out_ref, keep_ref):
        out_ref[:tile_rows, :] = tiles_ref[:tile_rows, :] + got_ref[:tile_rows, :]
        keep_ref[...] = sums_ref[skip : skip + go, :] + got_ref[tile_rows : tile_rows + go, :]
        if not final:
            out_ref[tile_rows:, :] = sums_ref[skip + go : skip + count, :] + got_ref[tile_rows + go :, :]

    def add_tile(tiles_ref, got_ref, out_ref):
        out_ref[...] = tiles_ref[...] + got_ref[...]

    if sums is None:
        return add_tile, (shape(tile_rows, width),)
    return add, (shape(tile_rows + count - go, width), shape(go, width))


def pack_inputs(tiles, sums, skip, got, tile_rows, final):
    return (tiles, got) if sums is None else (tiles, sums, got)


def pack_step(*pack):
    add, out = pack_parts(*pack[1:])
    args = pack_inputs(*pack)
    return call(add, out, (VMEM,) * len(args), args, "pack_step")


def inverse_of(block):
    size = block.shape[0]
    base = min(size, 64)
    row = lax.broadcasted_iota(jnp.int32, (base, base), 0)
    col = lax.broadcasted_iota(jnp.int32, (base, base), 1)
    pair = (row - col == 1) & (row & 1 == 1)
    starts = range(0, size, base)
    blocks = [block[at : at + base, at : at + base] for at in starts]
    inverses = []
    for part in blocks:
        diag = jnp.where(row == col, part, 0.0)
        recip_row = 1.0 / jnp.sum(diag, axis=0, keepdims=True)
        recip_col = 1.0 / jnp.sum(diag, axis=1, keepdims=True)
        off = -(part * recip_row) * recip_col
        inverses.append(jnp.where(row == col, recip_row, jnp.where(pair, off, 0.0)))
    step = 2
    while step < base:
        half = lax.div(row, step)
        below = (half - lax.div(col, step) == 1) & (half & 1 == 1)
        parts = [split(inverse) for inverse in inverses]
        middle = [dot_split(split(jnp.where(below, b, 0.0)), p, ((1,), (0,))) for b, p in zip(blocks, parts)]
        inverses = [i - dot_split(p, split(m), ((1,), (0,))) for i, p, m in zip(inverses, parts, middle)]
        step *= 2
    width = base
    while len(inverses) > 1:
        merged = []
        for index in range(0, len(inverses), 2):
            first, second = inverses[index : index + 2]
            lower = block[(index + 1) * width : (index + 2) * width, index * width : (index + 1) * width]
            corner = -dot3(second, dot3(lower, first))
            top = jnp.concatenate([first, jnp.zeros_like(first)], 1)
            merged.append(jnp.concatenate([top, jnp.concatenate([corner, second], 1)], 0))
        inverses = merged
        width *= 2
    return inverses[0]


def invert_diagonal(tile_ref, place, chosen, band):
    for spot in chosen:

        @pl.when(place == spot)
        def _():
            here = slice(spot * band, (spot + 1) * band)
            tile_ref[:, here] = inverse_of(tile_ref[:, here])


def join_halves(where, mine, other, first, half, chosen):
    width = mine.shape[1]

    def body(where_ref, mine_ref, other_ref, tile_ref):
        core = where_ref[0] & 1
        tile_ref[pl.ds(pl.multiple_of(core * half, half), half), :] = mine_ref[first : first + half, :]
        tile_ref[pl.ds(pl.multiple_of((1 - core) * half, half), half), :] = other_ref[first : first + half, :]
        invert_diagonal(tile_ref, where_ref[1], chosen, 2 * half)

    return call(body, shape(2 * half, width), (SMEM, VMEM, VMEM), (where, mine, other), "join")


def run_stage(where, base, tile, add, near, far, held, stage, packs=()):
    columns, band = base.shape
    left = stage * band
    last = max(left - band, 0)
    inputs = [pack_inputs(*pack) for pack in packs]
    more = [pack_parts(*pack[1:]) for pack in packs]
    count = sum(len(args) for args in inputs)

    def body(where_ref, base_ref, tile_ref, add_ref, near_ref, far_ref, held_ref, *refs):
        ins, (solved_ref, update_ref), outs = refs[:count], refs[count : count + 2], refs[count + 2 :]

        @pl.when(where_ref[1] == stage)
        def _():
            right = base_ref[...] - near_ref[...] - far_ref[:, left : left + band]
            solved = dot3(right, tile_ref[:, left : left + band])
            solved_ref[...] = solved
            if stage > 0:
                here = slice(last, left)
                update_ref[...] = far_ref[:, here] + add_ref[:, here] + dot3(solved, tile_ref[:, here])

        @pl.when(where_ref[1] != stage)
        def _():
            solved_ref[...] = held_ref[...]

        for args, (add_pack, out) in zip(inputs, more):
            add_pack(*ins[: len(args)], *outs[: len(out)])
            ins, outs = ins[len(args) :], outs[len(out) :]

    out = (shape(columns, band), shape(columns, band)) + sum((out for _, out in more), ())
    args = (where, base, tile, add, near, far, held) + sum(inputs, ())
    return call(body, out, (SMEM,) + (VMEM,) * (len(args) - 1), args, "stage")


def run_rest(where, tile, add, far, solved, stage):
    columns, band = solved.shape
    last = (stage - 1) * band

    def body(where_ref, tile_ref, add_ref, far_ref, solved_ref, rest_ref):
        @pl.when(where_ref[1] == stage)
        def _():
            rest_ref[...] = far_ref[:, :last] + add_ref[:, :last] + dot3(solved_ref[...], tile_ref[:, :last])

    return call(body, shape(columns, last), (SMEM,) + (VMEM,) * 4, (where, tile, add, far, solved), "rest")


def run_stage_plain(where, base, tile, add, near, far, held, stage, packs=()):
    high = lax.Precision.HIGHEST
    band = base.shape[1]
    left = stage * band
    here = slice(max(left - band, 0), max(left, band))
    solved = jnp.dot(base - near - far[:, left : left + band], tile[:, left : left + band], precision=high)
    update = jnp.dot(solved, tile[:, here], precision=high) + add[:, here] + far[:, here]
    more = sum((tuple(pack_step(*pack)) for pack in packs), ())
    return (jnp.where(where[1] == stage, solved, held), update) + more


def run_rest_plain(where, tile, add, far, solved, stage):
    last = (stage - 1) * solved.shape[1]
    return far[:, :last] + add[:, :last] + jnp.dot(solved, tile[:, :last], precision=lax.Precision.HIGHEST)


def sweep(where, base, tile, add, bands, packs=None):
    columns, band = base.shape
    aligned = band % 128 == 0
    stage_of, rest_of = (run_stage, run_rest) if aligned else (run_stage_plain, run_rest_plain)
    near = jnp.zeros((columns, band), F32)
    held = jnp.zeros((columns, band), F32)
    fars = [jnp.zeros((columns, bands * band), F32)] * 2
    for stage in range(bands - 1, -1, -1):
        far = fars.pop(0)
        taken = packs.take(bands - 1 - stage) if packs else ()
        held, update, *more = stage_of(where, base, tile, add, near, far, held, stage, taken)
        if stage > 0:
            near = lax.ppermute(update, "ct", [(stage, stage - 1)])
        if stage > 1:
            rest = rest_of(where, tile, add, far, held, stage)
            fars.append(lax.ppermute(rest, "ct", [(stage, stage - 2)]))
        if more:
            packs.put(*more)
    return held


class Packs:
    def __init__(self, pack, got, top, got_top, steps, bands, members):
        self.pack, self.got, self.top, self.got_top = pack, got, top, got_top
        self.steps, self.members = steps, members
        self.low_at = [bands - 2 - 2 * (steps - 1 - step) for step in range(steps)]
        self.top_at = [0] + [bands - steps + step for step in range(steps)]

    def take(self, index):
        taken = ()
        if index in self.low_at:
            tiles, sums, rows = self.pack
            taken += ((tiles, sums, 0, self.got, rows, index == self.low_at[-1]),)
        if index in self.top_at:
            taken += ((self.top, None, 0, self.got_top, self.top.shape[0], True),)
        self.index = index
        return taken

    def put(self, *outs):
        if self.index in self.low_at:
            tiles, sums, *outs = outs
            self.pack = (tiles, sums, self.pack[2])
            step = self.low_at.index(self.index) + 1
            self.got = swap_chip(tiles, self.members, step) if step < self.steps else swap_core(tiles, self.members)
        if outs:
            (self.top,) = outs
            step = self.top_at.index(self.index)
            self.got_top = swap_chip(self.top, self.members, step) if step < self.steps else swap_core(self.top, self.members)


def couple(where, sums, solved, mine, other, bands):
    columns, band = solved.shape
    half, width = mine.shape

    def body(where_ref, sums_ref, solved_ref, mine_ref, other_ref, out_ref, tile_ref, whole_ref):
        core = where_ref[0] & 1
        tile_ref[pl.ds(pl.multiple_of(core * half, half), half), :] = mine_ref[...]
        tile_ref[pl.ds(pl.multiple_of((1 - core) * half, half), half), :] = other_ref[...]
        whole_ref[...] = sums_ref[...] + dot3(solved_ref[...], tile_ref[...])
        for mask in range(bands):
            start = pl.multiple_of((where_ref[1] ^ mask) * band, band)
            out_ref[mask] = whole_ref[:, pl.ds(start, band)]

    scratch = [pltpu.VMEM((band, width), F32), pltpu.VMEM((columns, width), F32)]
    args = (where, sums, solved, mine, other)
    return call(body, shape(bands, columns, band), (SMEM,) + (VMEM,) * 4, args, "couple", scratch)


def couple_plain(where, sums, solved, mine, other, bands):
    band = solved.shape[1]
    tile = join_halves(where, mine, other, 0, band // 2, ())
    whole = sums + jnp.dot(solved, tile, precision=lax.Precision.HIGHEST)
    return jnp.stack([own_band(whole, where[1] ^ mask, band) for mask in range(bands)])


def own_band(value, spot, band):
    return lax.dynamic_slice(value, (0, spot * band), (value.shape[0], band))


def shards(factor_rows, slot_row, known, rhs, *, members, bands):
    slots, _, band, width = factor_rows.shape
    half = band // 2
    columns = rhs.shape[2]
    stages = len(stage_orders(members)[0])
    aligned = band % 128 == 0
    place = lax.axis_index("ct")
    where = jnp.stack([lax.axis_index("rt"), place]).astype(jnp.int32)
    factor_rows = pltpu.with_memory_space_constraint(factor_rows, pltpu.HBM)
    known = pltpu.with_memory_space_constraint(known, pltpu.HBM)

    keep, send = first_band(where, slot_row, factor_rows)
    tile_one = keep + swap_core(send, members)
    got_tile = swap_chip(tile_one, members, 0)
    keep_one, send_one = partial_one(after(where, tile_one), slot_row, factor_rows, known, members)
    got_sum = swap_core(send_one, members)
    tile_one = tile_one + after(got_tile, keep_one)
    got_tile = swap_chip(tile_one, members, 1)
    sum_one = keep_one + after(got_sum, tile_one)
    keep = send = top = send_top = got_pack = got_top = None
    for stage in range(stages):
        rows = sum_one.shape[0] // 2
        got_sum = swap_chip(sum_one[rows:], members, stage)
        if stage == 0:
            keep, send = pack_rest(after(where, sum_one), slot_row, factor_rows, known, members)
            got_sum = after(got_sum, keep)
        if stage == 1:
            top, send_top = top_band(after(where, sum_one), slot_row, factor_rows)
            got_sum = after(got_sum, top)
        sum_one = sum_one[:rows] + got_sum
        if stage == 0:
            got_pack = swap_core(after(send, sum_one), members)
        if stage < stages - 1:
            tile_one = tile_one + (after(got_tile, sum_one) if stage < stages - 2 else got_tile)
            got_tile = swap_chip(tile_one, members, stage + 2) if stage < stages - 2 else None
    got_top = swap_core(send_top, members)

    got_up = []
    for shift in range(bands - 1, 0, -1):
        piece = own_band(sum_one, jnp.minimum(place + shift, bands - 1), band)
        got_up.append(lax.ppermute(piece, "ct", [(i, i + shift) for i in range(bands - shift)]))

    other = swap_core(tile_one, members)

    tiles, sums = pack_step(keep, keep, half, after(got_pack, sum_one), half, False)
    got_pack = swap_chip(tiles, members, 0)
    tile_one = join_halves(after(where, sum_one), tile_one, other, 0, half, range(bands))
    packs = Packs((tiles, sums, half), got_pack, top, got_top, stages, bands, members)
    base = rhs[1].T - own_band(sum_one, place, band)
    for piece in got_up:
        base = base - after(piece, tile_one)
    solved_one = sweep(where, base, tile_one, sum_one, bands, packs)

    low, sums, _ = packs.pack
    pieces = (couple if aligned else couple_plain)(where, sums, solved_one, low, packs.got, bands)
    base = rhs[0].T - pieces[0]
    tile_zero = join_halves(where, packs.top, packs.got_top, 0, half, ())
    for mask in range(bands - 1, 0, -1):
        got = lax.ppermute(pieces[mask], "ct", [(i, i ^ mask) for i in range(bands)])
        base = base - after(got, tile_zero)

    nothing = jnp.zeros((columns, width), F32)
    solved_zero = sweep(where, base, tile_zero, nothing, bands)
    return jnp.stack([solved_zero.T, solved_one.T])


def solution(mesh):
    members, bands = mesh.shape["rt"], mesh.shape["ct"]
    in_specs = (P("rt", None, "ct", None), P(), P("rt", "ct", None), P(None, "ct", "rt"))
    out_specs = P(None, "ct", "rt")
    body = functools.partial(shards, members=members, bands=bands)
    return jax.shard_map(body, mesh=mesh, in_specs=in_specs, out_specs=out_specs, check_vma=False)
```

```python
import functools

import jax
import jax.numpy as jnp
from jax import lax
from jax.experimental import pallas as pl
from jax.experimental.pallas import tpu as pltpu
from jax.sharding import PartitionSpec as P

F32 = jnp.float32
BF16 = jnp.bfloat16
VMEM = pl.BlockSpec(memory_space=pltpu.MemorySpace.VMEM)
SMEM = pl.BlockSpec(memory_space=pltpu.MemorySpace.SMEM)
HBM = pl.BlockSpec(memory_space=pl.ANY)


def shape(*dims):
    return jax.ShapeDtypeStruct(dims, F32)


def call(body, out, specs, args, name, scratch=(), aliases=None):
    multiple = isinstance(out, tuple)
    return pl.pallas_call(
        body,
        out_shape=out,
        in_specs=list(specs),
        out_specs=tuple(VMEM for _ in out) if multiple else VMEM,
        scratch_shapes=list(scratch),
        input_output_aliases=aliases or {},
        compiler_params=pltpu.CompilerParams(vmem_limit_bytes=40 << 20),
        name=name,
    )(*args)


def split(value):
    high = value.astype(BF16)
    return high, (value - high.astype(F32)).astype(BF16)


def dot_split(a, b, dims):
    (ah, al), (bh, bl) = a, b

    def one(u, v):
        return lax.dot_general(u, v, (dims, ((), ())), preferred_element_type=F32)

    return one(al, bh) + one(ah, bl) + one(ah, bh)


def dot3(a, b):
    return dot_split(split(a), split(b), ((1,), (0,)))


def stage_orders(members):
    bits = members.bit_length() - 1
    first = list(range(1, bits))
    return first, first[::-1]


def swap_core(value, members):
    return lax.ppermute(value, "rt", [(i, i ^ 1) for i in range(members)])


def swap_chip(value, members, stage):
    orders = stage_orders(members)
    return lax.ppermute(value, "rt", [(i, i ^ (1 << orders[i & 1][stage])) for i in range(members)])


def send_tables(members):
    orders = stage_orders(members)
    count = len(orders[0])
    tables = []
    for core in range(2):
        table = []
        for place in range(members):
            other = place >> count
            rest = place & ((1 << count) - 1)
            relative = other
            for stage in range(count):
                if (rest >> (count - 1 - stage)) & 1:
                    relative |= 1 << orders[core ^ other][stage]
            table.append(relative)
        tables.append(table)
    return tables


def accumulate(where_ref, rows_ref, factor_ref, known_ref, factor_buf, known_buf, acc_ref, sems, column):
    slots = factor_buf.shape[0]
    me = where_ref[0]

    def live(slot):
        return rows_ref[me * slots + slot] >= 2

    def copies(slot):
        return (
            pltpu.make_async_copy(known_ref.at[slot], known_buf.at[slot], sems.at[0, slot]),
            pltpu.make_async_copy(factor_ref.at[slot, column], factor_buf.at[slot], sems.at[1, slot]),
        )

    for slot in range(slots):

        @pl.when(live(slot))
        def _():
            for copy in copies(slot):
                copy.start()

    acc_ref[...] = jnp.zeros_like(acc_ref)
    for slot in range(slots):

        @pl.when(live(slot))
        def _():
            for copy in copies(slot):
                copy.wait()
            acc_ref[...] += dot_split(split(known_buf[slot]), split(factor_buf[slot]), ((0,), (0,)))


def in_send_order(where_ref, acc_ref, keep_ref, send_ref, first, tables):
    count = len(tables[0])
    columns = acc_ref.shape[0] // count
    me = where_ref[0]
    for spot, (even, odd) in enumerate(zip(*tables)):
        group = me ^ jnp.where((me & 1) == 0, even, odd)
        rows = acc_ref[pl.ds(pl.multiple_of(group * columns, columns), columns), :]
        target, start = (keep_ref, spot) if spot < count // 2 else (send_ref, spot - count // 2)
        target[first + start * columns : first + (start + 1) * columns, :] = rows


def owned_slot(where_ref, rows_ref, row, slots):
    slot = jnp.int32(-1)
    for s in range(slots):
        slot = jnp.where(rows_ref[where_ref[0] * slots + s] == row, s, slot)
    return slot


def band_copies(where_ref, factor_ref, slot, column, keep_ref, send_ref, first, half, sems):
    core = where_ref[0] & 1
    copies = []
    for index, (target, which) in enumerate(((send_ref, 1 - core), (keep_ref, core))):
        start = pl.multiple_of(which * half, half)
        source = factor_ref.at[slot, column, pl.ds(start, half), :]
        copies.append(pltpu.make_async_copy(source, target.at[pl.ds(first, half), :], sems.at[index]))
    return copies


def put_band(where_ref, rows_ref, factor_ref, row, column, keep_ref, send_ref, first, half, sems):
    slot = owned_slot(where_ref, rows_ref, row, factor_ref.shape[0])

    @pl.when(slot >= 0)
    def _():
        for copy in band_copies(where_ref, factor_ref, slot, column, keep_ref, send_ref, first, half, sems):
            copy.start()

    @pl.when(slot < 0)
    def _():
        keep_ref[first : first + half, :] = jnp.zeros((half, keep_ref.shape[1]), F32)
        send_ref[first : first + half, :] = jnp.zeros((half, keep_ref.shape[1]), F32)

    def finish():
        @pl.when(slot >= 0)
        def _():
            for copy in band_copies(where_ref, factor_ref, slot, column, keep_ref, send_ref, first, half, sems):
                copy.wait()

    return finish


def first_band(where, slot_row, factor_rows):
    _, _, band, width = factor_rows.shape
    half = band // 2

    def body(where_ref, rows_ref, factor_ref, keep_ref, send_ref, sems):
        put_band(where_ref, rows_ref, factor_ref, 1, 1, keep_ref, send_ref, 0, half, sems)()

    out = (shape(half, width), shape(half, width))
    scratch = [pltpu.SemaphoreType.DMA((2,))]
    return call(body, out, (SMEM, SMEM, HBM), (where, slot_row, factor_rows), "first_band", scratch)


def partial_scratch(slots, band, width, total):
    return [
        pltpu.VMEM((slots, band, width), F32),
        pltpu.VMEM((slots, band, total), F32),
        pltpu.VMEM((total, width), F32),
        pltpu.SemaphoreType.DMA((2, slots)),
    ]


def partial_one(where, slot_row, factor_rows, known, members):
    slots, _, band, width = factor_rows.shape
    total = known.shape[2]
    tables = send_tables(members)

    def body(where_ref, rows_ref, factor_ref, known_ref, keep_ref, send_ref, factor_buf, known_buf, acc_ref, sems):
        accumulate(where_ref, rows_ref, factor_ref, known_ref, factor_buf, known_buf, acc_ref, sems, 1)
        in_send_order(where_ref, acc_ref, keep_ref, send_ref, 0, tables)

    out = (shape(total // 2, width), shape(total // 2, width))
    args = (where, slot_row, factor_rows, known)
    return call(body, out, (SMEM, SMEM, HBM, HBM), args, "partial_one", partial_scratch(slots, band, width, total))


def pack_rest(where, slot_row, factor_rows, known, members):
    slots, _, band, width = factor_rows.shape
    half, total = band // 2, known.shape[2]
    tables = send_tables(members)

    def body(where_ref, rows_ref, factor_ref, known_ref, keep_ref, send_ref, factor_buf, known_buf, acc_ref, sems, low, top):
        accumulate(where_ref, rows_ref, factor_ref, known_ref, factor_buf, known_buf, acc_ref, sems, 0)
        finish_low = put_band(where_ref, rows_ref, factor_ref, 1, 0, keep_ref, send_ref, 0, half, low)
        finish_top = put_band(where_ref, rows_ref, factor_ref, 0, 0, keep_ref, send_ref, half, half, top)
        in_send_order(where_ref, acc_ref, keep_ref, send_ref, band, tables)
        finish_low()
        finish_top()

    rows = band + total // 2
    scratch = partial_scratch(slots, band, width, total) + [pltpu.SemaphoreType.DMA((2,))] * 2
    args = (where, slot_row, factor_rows, known)
    return call(body, (shape(rows, width),) * 2, (SMEM, SMEM, HBM, HBM), args, "pack_rest", scratch)


def after(value, *others):
    return lax.optimization_barrier((value,) + others)[0]


def pack_parts(sums, skip, got, tile_rows, final):
    width = got.shape[1]
    count = got.shape[0] - tile_rows
    go = count if final else count // 2

    def add(tiles_ref, sums_ref, got_ref, out_ref, keep_ref):
        out_ref[:tile_rows, :] = tiles_ref[:tile_rows, :] + got_ref[:tile_rows, :]
        keep_ref[...] = sums_ref[skip : skip + go, :] + got_ref[tile_rows : tile_rows + go, :]
        if not final:
            out_ref[tile_rows:, :] = sums_ref[skip + go : skip + count, :] + got_ref[tile_rows + go :, :]

    def add_tile(tiles_ref, got_ref, out_ref):
        out_ref[...] = tiles_ref[...] + got_ref[...]

    if sums is None:
        return add_tile, (shape(tile_rows, width),)
    return add, (shape(tile_rows + count - go, width), shape(go, width))


def pack_inputs(tiles, sums, skip, got, tile_rows, final):
    return (tiles, got) if sums is None else (tiles, sums, got)


def pack_step(*pack):
    add, out = pack_parts(*pack[1:])
    args = pack_inputs(*pack)
    return call(add, out, (VMEM,) * len(args), args, "pack_step")


def unpack_first(keep, got, half):
    rows, width = keep.shape
    band = 2 * half
    go = (rows - band) // 2

    def body(keep_ref, got_ref, low_ref, sum_ref, top_ref):
        low_ref[:half, :] = keep_ref[:half, :] + got_ref[:half, :]
        top_ref[...] = keep_ref[half:band, :] + got_ref[half:band, :]
        sum_ref[...] = keep_ref[band : band + go, :] + got_ref[band : band + go, :]
        low_ref[half:, :] = keep_ref[band + go :, :] + got_ref[band + go :, :]

    out = (shape(half + go, width), shape(go, width), shape(half, width))
    return call(body, out, (VMEM, VMEM), (keep, got), "unpack_first")


def inverse_of(block):
    size = block.shape[0]
    base = min(size, 64)
    row = lax.broadcasted_iota(jnp.int32, (base, base), 0)
    col = lax.broadcasted_iota(jnp.int32, (base, base), 1)
    pair = (row - col == 1) & (row & 1 == 1)
    starts = range(0, size, base)
    blocks = [block[at : at + base, at : at + base] for at in starts]
    inverses = []
    for part in blocks:
        diag = jnp.where(row == col, part, 0.0)
        recip_row = 1.0 / jnp.sum(diag, axis=0, keepdims=True)
        recip_col = 1.0 / jnp.sum(diag, axis=1, keepdims=True)
        off = -(part * recip_row) * recip_col
        inverses.append(jnp.where(row == col, recip_row, jnp.where(pair, off, 0.0)))
    step = 2
    while step < base:
        half = lax.div(row, step)
        below = (half - lax.div(col, step) == 1) & (half & 1 == 1)
        parts = [split(inverse) for inverse in inverses]
        middle = [dot_split(split(jnp.where(below, b, 0.0)), p, ((1,), (0,))) for b, p in zip(blocks, parts)]
        inverses = [i - dot_split(p, split(m), ((1,), (0,))) for i, p, m in zip(inverses, parts, middle)]
        step *= 2
    width = base
    while len(inverses) > 1:
        merged = []
        for index in range(0, len(inverses), 2):
            first, second = inverses[index : index + 2]
            lower = block[(index + 1) * width : (index + 2) * width, index * width : (index + 1) * width]
            corner = -dot3(second, dot3(lower, first))
            top = jnp.concatenate([first, jnp.zeros_like(first)], 1)
            merged.append(jnp.concatenate([top, jnp.concatenate([corner, second], 1)], 0))
        inverses = merged
        width *= 2
    return inverses[0]


def invert_diagonal(tile_ref, place, chosen, band):
    for spot in chosen:

        @pl.when(place == spot)
        def _():
            here = slice(spot * band, (spot + 1) * band)
            tile_ref[:, here] = inverse_of(tile_ref[:, here])


def join_halves(where, mine, other, first, half, chosen):
    width = mine.shape[1]

    def body(where_ref, mine_ref, other_ref, tile_ref):
        core = where_ref[0] & 1
        tile_ref[pl.ds(pl.multiple_of(core * half, half), half), :] = mine_ref[first : first + half, :]
        tile_ref[pl.ds(pl.multiple_of((1 - core) * half, half), half), :] = other_ref[first : first + half, :]
        invert_diagonal(tile_ref, where_ref[1], chosen, 2 * half)

    return call(body, shape(2 * half, width), (SMEM, VMEM, VMEM), (where, mine, other), "join")


def run_stage(where, base, tile, add, near, far, held, stage, packs=()):
    columns, band = base.shape
    left = stage * band
    last = max(left - band, 0)
    inputs = [pack_inputs(*pack) for pack in packs]
    more = [pack_parts(*pack[1:]) for pack in packs]
    count = sum(len(args) for args in inputs)

    def body(where_ref, base_ref, tile_ref, add_ref, near_ref, far_ref, held_ref, *refs):
        ins, (solved_ref, update_ref), outs = refs[:count], refs[count : count + 2], refs[count + 2 :]

        @pl.when(where_ref[1] == stage)
        def _():
            right = base_ref[...] - near_ref[...] - far_ref[:, left : left + band]
            solved = dot3(right, tile_ref[:, left : left + band])
            solved_ref[...] = solved
            if stage > 0:
                here = slice(last, left)
                update_ref[...] = far_ref[:, here] + add_ref[:, here] + dot3(solved, tile_ref[:, here])

        @pl.when(where_ref[1] != stage)
        def _():
            solved_ref[...] = held_ref[...]

        for args, (add_pack, out) in zip(inputs, more):
            add_pack(*ins[: len(args)], *outs[: len(out)])
            ins, outs = ins[len(args) :], outs[len(out) :]

    out = (shape(columns, band), shape(columns, band)) + sum((out for _, out in more), ())
    args = (where, base, tile, add, near, far, held) + sum(inputs, ())
    return call(body, out, (SMEM,) + (VMEM,) * (len(args) - 1), args, "stage")


def run_rest(where, tile, add, far, solved, stage):
    columns, band = solved.shape
    last = (stage - 1) * band

    def body(where_ref, tile_ref, add_ref, far_ref, solved_ref, rest_ref):
        @pl.when(where_ref[1] == stage)
        def _():
            rest_ref[...] = far_ref[:, :last] + add_ref[:, :last] + dot3(solved_ref[...], tile_ref[:, :last])

    return call(body, shape(columns, last), (SMEM,) + (VMEM,) * 4, (where, tile, add, far, solved), "rest")


def run_stage_plain(where, base, tile, add, near, far, held, stage, packs=()):
    high = lax.Precision.HIGHEST
    band = base.shape[1]
    left = stage * band
    here = slice(max(left - band, 0), max(left, band))
    solved = jnp.dot(base - near - far[:, left : left + band], tile[:, left : left + band], precision=high)
    update = jnp.dot(solved, tile[:, here], precision=high) + add[:, here] + far[:, here]
    more = sum((tuple(pack_step(*pack)) for pack in packs), ())
    return (jnp.where(where[1] == stage, solved, held), update) + more


def run_rest_plain(where, tile, add, far, solved, stage):
    last = (stage - 1) * solved.shape[1]
    return far[:, :last] + add[:, :last] + jnp.dot(solved, tile[:, :last], precision=lax.Precision.HIGHEST)


def sweep(where, base, tile, add, bands, packs=None):
    columns, band = base.shape
    aligned = band % 128 == 0
    stage_of, rest_of = (run_stage, run_rest) if aligned else (run_stage_plain, run_rest_plain)
    near = jnp.zeros((columns, band), F32)
    held = jnp.zeros((columns, band), F32)
    fars = [jnp.zeros((columns, bands * band), F32)] * 2
    for stage in range(bands - 1, -1, -1):
        far = fars.pop(0)
        taken = packs.take(bands - 1 - stage) if packs else ()
        held, update, *more = stage_of(where, base, tile, add, near, far, held, stage, taken)
        if stage > 0:
            near = lax.ppermute(update, "ct", [(stage, stage - 1)])
        if stage > 1:
            rest = rest_of(where, tile, add, far, held, stage)
            fars.append(lax.ppermute(rest, "ct", [(stage, stage - 2)]))
        if more:
            packs.put(*more)
    return held


class Packs:
    def __init__(self, pack, got, top, got_top, steps, bands, members):
        self.pack, self.got, self.top, self.got_top = pack, got, top, got_top
        self.steps, self.members = steps, members
        self.low_at = [bands - 1 - 2 * (steps - 1 - step) for step in range(steps)]
        self.top_at = [bands - steps + step for step in range(steps - 1)]

    def take(self, index):
        taken = ()
        if index in self.low_at:
            tiles, sums, rows = self.pack
            taken += ((tiles, sums, 0, self.got, rows, index == self.low_at[-1]),)
        if index in self.top_at:
            taken += ((self.top, None, 0, self.got_top, self.top.shape[0], True),)
        self.index = index
        return taken

    def put(self, *outs):
        if self.index in self.low_at:
            tiles, sums, *outs = outs
            self.pack = (tiles, sums, self.pack[2])
            step = self.low_at.index(self.index) + 1
            self.got = swap_chip(tiles, self.members, step) if step < self.steps else swap_core(tiles, self.members)
        if outs:
            (self.top,) = outs
            self.got_top = swap_chip(self.top, self.members, self.top_at.index(self.index) + 1)

    def last_tile(self, where, ready, bands):
        (tile,) = pack_step(self.top, None, 0, after(self.got_top, ready), self.top.shape[0], True)
        return join_halves(where, tile, swap_core(tile, self.members), 0, tile.shape[0], range(bands))


def couple(where, sums, solved, mine, other, bands):
    columns, band = solved.shape
    half, width = mine.shape

    def body(where_ref, sums_ref, solved_ref, mine_ref, other_ref, out_ref, tile_ref, whole_ref):
        core = where_ref[0] & 1
        tile_ref[pl.ds(pl.multiple_of(core * half, half), half), :] = mine_ref[...]
        tile_ref[pl.ds(pl.multiple_of((1 - core) * half, half), half), :] = other_ref[...]
        whole_ref[...] = sums_ref[...] + dot3(solved_ref[...], tile_ref[...])
        for mask in range(bands):
            start = pl.multiple_of((where_ref[1] ^ mask) * band, band)
            out_ref[mask] = whole_ref[:, pl.ds(start, band)]

    scratch = [pltpu.VMEM((band, width), F32), pltpu.VMEM((columns, width), F32)]
    args = (where, sums, solved, mine, other)
    return call(body, shape(bands, columns, band), (SMEM,) + (VMEM,) * 4, args, "couple", scratch)


def couple_plain(where, sums, solved, mine, other, bands):
    band = solved.shape[1]
    tile = join_halves(where, mine, other, 0, band // 2, ())
    whole = sums + jnp.dot(solved, tile, precision=lax.Precision.HIGHEST)
    return jnp.stack([own_band(whole, where[1] ^ mask, band) for mask in range(bands)])


def own_band(value, spot, band):
    return lax.dynamic_slice(value, (0, spot * band), (value.shape[0], band))


def shards(factor_rows, slot_row, known, rhs, *, members, bands):
    slots, _, band, width = factor_rows.shape
    half = band // 2
    columns = rhs.shape[2]
    stages = len(stage_orders(members)[0])
    aligned = band % 128 == 0
    place = lax.axis_index("ct")
    where = jnp.stack([lax.axis_index("rt"), place]).astype(jnp.int32)
    factor_rows = pltpu.with_memory_space_constraint(factor_rows, pltpu.HBM)
    known = pltpu.with_memory_space_constraint(known, pltpu.HBM)

    keep, send = first_band(where, slot_row, factor_rows)
    tile_one = keep + swap_core(send, members)
    got_tile = swap_chip(tile_one, members, 0)
    keep_one, send_one = partial_one(after(where, tile_one), slot_row, factor_rows, known, members)
    got_sum = swap_core(send_one, members)
    tile_one = tile_one + after(got_tile, keep_one)
    sum_one = keep_one + after(got_sum, tile_one)
    keep = send = got_pack = got_tile = None
    for stage in range(stages):
        rows = sum_one.shape[0] // 2
        got_sum = swap_chip(sum_one[rows:], members, stage)
        if stage == 0:
            keep, send = pack_rest(after(where, sum_one), slot_row, factor_rows, known, members)
            got_sum = after(got_sum, keep)
        sum_one = sum_one[:rows] + got_sum
        if stage == 0:
            got_pack = swap_core(after(send, sum_one), members)

    got_up = []
    for shift in range(bands - 1, 0, -1):
        piece = own_band(sum_one, jnp.minimum(place + shift, bands - 1), band)
        got_up.append(lax.ppermute(piece, "ct", [(i, i + shift) for i in range(bands - shift)]))

    for stage in range(1, stages):
        got_tile = swap_chip(after(tile_one, sum_one), members, stage)
        tile_one = tile_one + after(got_tile, *got_up)
    other = swap_core(tile_one, members)

    tiles, sums, top = unpack_first(keep, after(got_pack, sum_one), half)
    tiles = after(tiles, tile_one)
    got_pack = swap_chip(tiles, members, 0)
    got_top = swap_chip(after(top, tiles), members, 0)

    tile_one = join_halves(after(where, sum_one), tile_one, other, 0, half, range(bands))
    packs = Packs((tiles, sums, half), got_pack, top, got_top, stages, bands, members)
    base = rhs[1].T - own_band(sum_one, place, band)
    for piece in got_up:
        base = base - piece
    solved_one = sweep(where, base, tile_one, sum_one, bands, packs)

    low, sums, _ = packs.pack
    pieces = (couple if aligned else couple_plain)(where, sums, solved_one, low, packs.got, bands)
    base = rhs[0].T - pieces[0]
    tile_zero = packs.last_tile(where, pieces, bands)
    for mask in range(bands - 1, 0, -1):
        got = lax.ppermute(pieces[mask], "ct", [(i, i ^ mask) for i in range(bands)])
        base = base - after(got, tile_zero)

    nothing = jnp.zeros((columns, width), F32)
    solved_zero = sweep(where, base, tile_zero, nothing, bands)
    return jnp.stack([solved_zero.T, solved_one.T])


def solution(mesh):
    members, bands = mesh.shape["rt"], mesh.shape["ct"]
    in_specs = (P("rt", None, "ct", None), P(), P("rt", "ct", None), P(None, "ct", "rt"))
    out_specs = P(None, "ct", "rt")
    body = functools.partial(shards, members=members, bands=bands)
    return jax.shard_map(body, mesh=mesh, in_specs=in_specs, out_specs=out_specs, check_vma=False)
```

```python
import functools

import jax
import jax.numpy as jnp
from jax import lax
from jax.experimental import pallas as pl
from jax.experimental.pallas import tpu as pltpu
from jax.sharding import PartitionSpec as P

F32 = jnp.float32
BF16 = jnp.bfloat16
VMEM = pl.BlockSpec(memory_space=pltpu.MemorySpace.VMEM)
SMEM = pl.BlockSpec(memory_space=pltpu.MemorySpace.SMEM)
HBM = pl.BlockSpec(memory_space=pl.ANY)


def shape(*dims):
    return jax.ShapeDtypeStruct(dims, F32)


def call(body, out, specs, args, name, scratch=(), aliases=None):
    multiple = isinstance(out, tuple)
    return pl.pallas_call(
        body,
        out_shape=out,
        in_specs=list(specs),
        out_specs=tuple(VMEM for _ in out) if multiple else VMEM,
        scratch_shapes=list(scratch),
        input_output_aliases=aliases or {},
        compiler_params=pltpu.CompilerParams(vmem_limit_bytes=40 << 20),
        name=name,
    )(*args)


def split(value):
    high = value.astype(BF16)
    return high, (value - high.astype(F32)).astype(BF16)


def dot_split(a, b, dims):
    (ah, al), (bh, bl) = a, b

    def one(u, v):
        return lax.dot_general(u, v, (dims, ((), ())), preferred_element_type=F32)

    return one(al, bh) + one(ah, bl) + one(ah, bh)


def dot3(a, b):
    return dot_split(split(a), split(b), ((1,), (0,)))


def stage_orders(members):
    bits = members.bit_length() - 1
    first = list(range(1, bits))
    return first, first[::-1]


def swap_core(value, members):
    return lax.ppermute(value, "rt", [(i, i ^ 1) for i in range(members)])


def swap_chip(value, members, stage):
    orders = stage_orders(members)
    return lax.ppermute(value, "rt", [(i, i ^ (1 << orders[i & 1][stage])) for i in range(members)])


def send_tables(members):
    orders = stage_orders(members)
    count = len(orders[0])
    tables = []
    for core in range(2):
        table = []
        for place in range(members):
            other = place >> count
            rest = place & ((1 << count) - 1)
            relative = other
            for stage in range(count):
                if (rest >> (count - 1 - stage)) & 1:
                    relative |= 1 << orders[core ^ other][stage]
            table.append(relative)
        tables.append(table)
    return tables


def front_kernel(
    where_ref, rows_ref, factor_ref, known_ref, keep_one, send_one, keep_ref, send_ref, factor_buf, known_buf, acc_ref, sems, low,
    *, tables
):
    slots, _, band, _ = factor_buf.shape
    me = where_ref[0]

    def live(slot):
        return rows_ref[me * slots + slot] >= 2

    def copies(slot, column):
        copy = pltpu.make_async_copy(factor_ref.at[slot, column], factor_buf.at[slot, column], sems.at[column, slot])
        if column == 0:
            return [copy]
        return [pltpu.make_async_copy(known_ref.at[slot], known_buf.at[slot], sems.at[2, slot]), copy]

    for column in (1, 0):
        for slot in range(slots):

            @pl.when(live(slot))
            def _():
                for copy in copies(slot, column):
                    copy.start()

    finish = put_band(where_ref, rows_ref, factor_ref, 1, 0, keep_ref, send_ref, 0, band // 2, low)
    for column, keep, send, first in ((1, keep_one, send_one, 0), (0, keep_ref, send_ref, band // 2)):
        acc_ref[...] = jnp.zeros_like(acc_ref)
        for slot in range(slots):

            @pl.when(live(slot))
            def _():
                for copy in copies(slot, column):
                    copy.wait()
                acc_ref[...] += dot_split(split(known_buf[slot]), split(factor_buf[slot, column]), ((0,), (0,)))

        in_send_order(where_ref, acc_ref, keep, send, first, tables)
    finish()


def in_send_order(where_ref, acc_ref, keep_ref, send_ref, first, tables):
    count = len(tables[0])
    columns = acc_ref.shape[0] // count
    me = where_ref[0]
    for spot, (even, odd) in enumerate(zip(*tables)):
        group = me ^ jnp.where((me & 1) == 0, even, odd)
        rows = acc_ref[pl.ds(pl.multiple_of(group * columns, columns), columns), :]
        target, start = (keep_ref, spot) if spot < count // 2 else (send_ref, spot - count // 2)
        target[first + start * columns : first + (start + 1) * columns, :] = rows


def owned_slot(where_ref, rows_ref, row, slots):
    slot = jnp.int32(-1)
    for s in range(slots):
        slot = jnp.where(rows_ref[where_ref[0] * slots + s] == row, s, slot)
    return slot


def band_copies(where_ref, factor_ref, slot, column, keep_ref, send_ref, first, half, sems):
    core = where_ref[0] & 1
    copies = []
    for index, (target, which) in enumerate(((send_ref, 1 - core), (keep_ref, core))):
        start = pl.multiple_of(which * half, half)
        source = factor_ref.at[slot, column, pl.ds(start, half), :]
        copies.append(pltpu.make_async_copy(source, target.at[pl.ds(first, half), :], sems.at[index]))
    return copies


def put_band(where_ref, rows_ref, factor_ref, row, column, keep_ref, send_ref, first, half, sems):
    slot = owned_slot(where_ref, rows_ref, row, factor_ref.shape[0])

    @pl.when(slot >= 0)
    def _():
        for copy in band_copies(where_ref, factor_ref, slot, column, keep_ref, send_ref, first, half, sems):
            copy.start()

    @pl.when(slot < 0)
    def _():
        keep_ref[first : first + half, :] = jnp.zeros((half, keep_ref.shape[1]), F32)
        send_ref[first : first + half, :] = jnp.zeros((half, keep_ref.shape[1]), F32)

    def finish():
        @pl.when(slot >= 0)
        def _():
            for copy in band_copies(where_ref, factor_ref, slot, column, keep_ref, send_ref, first, half, sems):
                copy.wait()

    return finish


def first_band(where, slot_row, factor_rows):
    _, _, band, width = factor_rows.shape
    half = band // 2

    def body(where_ref, rows_ref, factor_ref, keep_ref, send_ref, sems):
        put_band(where_ref, rows_ref, factor_ref, 1, 1, keep_ref, send_ref, 0, half, sems)()

    out = (shape(half, width), shape(half, width))
    scratch = [pltpu.SemaphoreType.DMA((2,))]
    return call(body, out, (SMEM, SMEM, HBM), (where, slot_row, factor_rows), "first_band", scratch)


def front(where, slot_row, factor_rows, known, members):
    slots, _, band, width = factor_rows.shape
    total = known.shape[2]
    one, rest = shape(total // 2, width), shape(band // 2 + total // 2, width)
    scratch = [
        pltpu.VMEM(factor_rows.shape, F32),
        pltpu.VMEM(known.shape, F32),
        pltpu.VMEM((total, width), F32),
        pltpu.SemaphoreType.DMA((3, slots)),
        pltpu.SemaphoreType.DMA((2,)),
    ]
    body = functools.partial(front_kernel, tables=send_tables(members))
    args = (where, slot_row, factor_rows, known)
    return call(body, (one, one, rest, rest), (SMEM, SMEM, HBM, HBM), args, "front", scratch)


def top_band(where, slot_row, factor_rows):
    slots, _, band, width = factor_rows.shape
    half = band // 2

    def body(where_ref, rows_ref, factor_ref, keep_ref, send_ref, tile_ref, sem):
        slot = owned_slot(where_ref, rows_ref, 0, slots)
        core = where_ref[0] & 1

        @pl.when(slot >= 0)
        def _():
            copy = pltpu.make_async_copy(factor_ref.at[slot, 0], tile_ref, sem)
            copy.start()
            copy.wait()
            invert_diagonal(tile_ref, where_ref[1], range(width // band), band)
            keep_ref[...] = tile_ref[pl.ds(pl.multiple_of(core * half, half), half), :]
            send_ref[...] = tile_ref[pl.ds(pl.multiple_of((1 - core) * half, half), half), :]

        @pl.when(slot < 0)
        def _():
            keep_ref[...] = jnp.zeros_like(keep_ref)
            send_ref[...] = jnp.zeros_like(send_ref)

    out = (shape(half, width), shape(half, width))
    scratch = [pltpu.VMEM((band, width), F32), pltpu.SemaphoreType.DMA(())]
    return call(body, out, (SMEM, SMEM, HBM), (where, slot_row, factor_rows), "top_band", scratch)


def after(value, *others):
    return lax.optimization_barrier((value,) + others)[0]


def pack_parts(sums, skip, got, tile_rows, final):
    width = got.shape[1]
    count = got.shape[0] - tile_rows
    go = count if final else count // 2

    def add(tiles_ref, sums_ref, got_ref, out_ref, keep_ref):
        out_ref[:tile_rows, :] = tiles_ref[:tile_rows, :] + got_ref[:tile_rows, :]
        keep_ref[...] = sums_ref[skip : skip + go, :] + got_ref[tile_rows : tile_rows + go, :]
        if not final:
            out_ref[tile_rows:, :] = sums_ref[skip + go : skip + count, :] + got_ref[tile_rows + go :, :]

    def add_tile(tiles_ref, got_ref, out_ref):
        out_ref[...] = tiles_ref[...] + got_ref[...]

    if sums is None:
        return add_tile, (shape(tile_rows, width),)
    return add, (shape(tile_rows + count - go, width), shape(go, width))


def pack_inputs(tiles, sums, skip, got, tile_rows, final):
    return (tiles, got) if sums is None else (tiles, sums, got)


def pack_step(*pack):
    add, out = pack_parts(*pack[1:])
    args = pack_inputs(*pack)
    return call(add, out, (VMEM,) * len(args), args, "pack_step")


def inverse_of(block):
    size = block.shape[0]
    base = min(size, 64)
    row = lax.broadcasted_iota(jnp.int32, (base, base), 0)
    col = lax.broadcasted_iota(jnp.int32, (base, base), 1)
    pair = (row - col == 1) & (row & 1 == 1)
    starts = range(0, size, base)
    blocks = [block[at : at + base, at : at + base] for at in starts]
    inverses = []
    for part in blocks:
        diag = jnp.where(row == col, part, 0.0)
        recip_row = 1.0 / jnp.sum(diag, axis=0, keepdims=True)
        recip_col = 1.0 / jnp.sum(diag, axis=1, keepdims=True)
        off = -(part * recip_row) * recip_col
        inverses.append(jnp.where(row == col, recip_row, jnp.where(pair, off, 0.0)))
    step = 2
    while step < base:
        half = lax.div(row, step)
        below = (half - lax.div(col, step) == 1) & (half & 1 == 1)
        parts = [split(inverse) for inverse in inverses]
        middle = [dot_split(split(jnp.where(below, b, 0.0)), p, ((1,), (0,))) for b, p in zip(blocks, parts)]
        inverses = [i - dot_split(p, split(m), ((1,), (0,))) for i, p, m in zip(inverses, parts, middle)]
        step *= 2
    width = base
    while len(inverses) > 1:
        merged = []
        for index in range(0, len(inverses), 2):
            first, second = inverses[index : index + 2]
            lower = block[(index + 1) * width : (index + 2) * width, index * width : (index + 1) * width]
            corner = -dot3(second, dot3(lower, first))
            top = jnp.concatenate([first, jnp.zeros_like(first)], 1)
            merged.append(jnp.concatenate([top, jnp.concatenate([corner, second], 1)], 0))
        inverses = merged
        width *= 2
    return inverses[0]


def invert_diagonal(tile_ref, place, chosen, band):
    for spot in chosen:

        @pl.when(place == spot)
        def _():
            here = slice(spot * band, (spot + 1) * band)
            tile_ref[:, here] = inverse_of(tile_ref[:, here])


def join_halves(where, mine, other, first, half, chosen):
    width = mine.shape[1]

    def body(where_ref, mine_ref, other_ref, tile_ref):
        core = where_ref[0] & 1
        tile_ref[pl.ds(pl.multiple_of(core * half, half), half), :] = mine_ref[first : first + half, :]
        tile_ref[pl.ds(pl.multiple_of((1 - core) * half, half), half), :] = other_ref[first : first + half, :]
        invert_diagonal(tile_ref, where_ref[1], chosen, 2 * half)

    return call(body, shape(2 * half, width), (SMEM, VMEM, VMEM), (where, mine, other), "join")


def run_stage(where, base, tile, add, near, far, held, stage, packs=()):
    columns, band = base.shape
    left = stage * band
    last = max(left - band, 0)
    inputs = [pack_inputs(*pack) for pack in packs]
    more = [pack_parts(*pack[1:]) for pack in packs]
    count = sum(len(args) for args in inputs)

    def body(where_ref, base_ref, tile_ref, add_ref, near_ref, far_ref, held_ref, *refs):
        ins, (solved_ref, update_ref), outs = refs[:count], refs[count : count + 2], refs[count + 2 :]

        @pl.when(where_ref[1] == stage)
        def _():
            right = base_ref[...] - near_ref[...] - far_ref[:, left : left + band]
            solved = dot3(right, tile_ref[:, left : left + band])
            solved_ref[...] = solved
            if stage > 0:
                here = slice(last, left)
                update_ref[...] = far_ref[:, here] + add_ref[:, here] + dot3(solved, tile_ref[:, here])

        @pl.when(where_ref[1] != stage)
        def _():
            solved_ref[...] = held_ref[...]

        for args, (add_pack, out) in zip(inputs, more):
            add_pack(*ins[: len(args)], *outs[: len(out)])
            ins, outs = ins[len(args) :], outs[len(out) :]

    out = (shape(columns, band), shape(columns, band)) + sum((out for _, out in more), ())
    args = (where, base, tile, add, near, far, held) + sum(inputs, ())
    return call(body, out, (SMEM,) + (VMEM,) * (len(args) - 1), args, "stage")


def run_rest(where, tile, add, far, solved, stage):
    columns, band = solved.shape
    last = (stage - 1) * band

    def body(where_ref, tile_ref, add_ref, far_ref, solved_ref, rest_ref):
        @pl.when(where_ref[1] == stage)
        def _():
            rest_ref[...] = far_ref[:, :last] + add_ref[:, :last] + dot3(solved_ref[...], tile_ref[:, :last])

    return call(body, shape(columns, last), (SMEM,) + (VMEM,) * 4, (where, tile, add, far, solved), "rest")


def run_stage_plain(where, base, tile, add, near, far, held, stage, packs=()):
    high = lax.Precision.HIGHEST
    band = base.shape[1]
    left = stage * band
    here = slice(max(left - band, 0), max(left, band))
    solved = jnp.dot(base - near - far[:, left : left + band], tile[:, left : left + band], precision=high)
    update = jnp.dot(solved, tile[:, here], precision=high) + add[:, here] + far[:, here]
    more = sum((tuple(pack_step(*pack)) for pack in packs), ())
    return (jnp.where(where[1] == stage, solved, held), update) + more


def run_rest_plain(where, tile, add, far, solved, stage):
    last = (stage - 1) * solved.shape[1]
    return far[:, :last] + add[:, :last] + jnp.dot(solved, tile[:, :last], precision=lax.Precision.HIGHEST)


def sweep(where, base, tile, add, bands, packs=None):
    columns, band = base.shape
    aligned = band % 128 == 0
    stage_of, rest_of = (run_stage, run_rest) if aligned else (run_stage_plain, run_rest_plain)
    near = jnp.zeros((columns, band), F32)
    held = jnp.zeros((columns, band), F32)
    fars = [jnp.zeros((columns, bands * band), F32)] * 2
    for stage in range(bands - 1, -1, -1):
        far = fars.pop(0)
        taken = packs.take(bands - 1 - stage) if packs else ()
        held, update, *more = stage_of(where, base, tile, add, near, far, held, stage, taken)
        if stage > 0:
            near = lax.ppermute(update, "ct", [(stage, stage - 1)])
        if stage > 1:
            rest = rest_of(where, tile, add, far, held, stage)
            fars.append(lax.ppermute(rest, "ct", [(stage, stage - 2)]))
        if more:
            packs.put(*more)
    return held


class Packs:
    def __init__(self, pack, got, top, got_top, steps, bands, members):
        self.pack, self.got, self.top, self.got_top = pack, got, top, got_top
        self.steps, self.members = steps, members
        self.low_at = [bands - 2 - 2 * (steps - 1 - step) for step in range(steps)]
        self.top_at = [bands - 1 - 2 * (steps - 1 - step) for step in range(steps)]

    def take(self, index):
        taken = ()
        if index in self.low_at:
            tiles, sums, rows = self.pack
            taken += ((tiles, sums, 0, self.got, rows, index == self.low_at[-1]),)
        if index in self.top_at:
            taken += ((self.top, None, 0, self.got_top, self.top.shape[0], True),)
        self.index = index
        return taken

    def put(self, *outs):
        if self.index in self.low_at:
            tiles, sums, *outs = outs
            self.pack = (tiles, sums, self.pack[2])
            step = self.low_at.index(self.index) + 1
            if step < self.steps:
                self.got = swap_chip(tiles, self.members, step)
            else:
                self.got = swap_core(tiles, self.members)
        if self.index in self.top_at:
            (self.top,) = outs
            step = self.top_at.index(self.index) + 1
            if step < self.steps:
                self.got_top = swap_chip(self.top, self.members, step)
            else:
                self.got_top = swap_core(self.top, self.members)


def couple(where, sums, solved, mine, other, bands):
    columns, band = solved.shape
    half, width = mine.shape

    def body(where_ref, sums_ref, solved_ref, mine_ref, other_ref, out_ref, tile_ref, whole_ref):
        core = where_ref[0] & 1
        tile_ref[pl.ds(pl.multiple_of(core * half, half), half), :] = mine_ref[...]
        tile_ref[pl.ds(pl.multiple_of((1 - core) * half, half), half), :] = other_ref[...]
        whole_ref[...] = sums_ref[...] + dot3(solved_ref[...], tile_ref[...])
        for mask in range(bands):
            start = pl.multiple_of((where_ref[1] ^ mask) * band, band)
            out_ref[mask] = whole_ref[:, pl.ds(start, band)]

    scratch = [pltpu.VMEM((band, width), F32), pltpu.VMEM((columns, width), F32)]
    args = (where, sums, solved, mine, other)
    return call(body, shape(bands, columns, band), (SMEM,) + (VMEM,) * 4, args, "couple", scratch)


def couple_plain(where, sums, solved, mine, other, bands):
    band = solved.shape[1]
    tile = join_halves(where, mine, other, 0, band // 2, ())
    whole = sums + jnp.dot(solved, tile, precision=lax.Precision.HIGHEST)
    return jnp.stack([own_band(whole, where[1] ^ mask, band) for mask in range(bands)])


def own_band(value, spot, band):
    return lax.dynamic_slice(value, (0, spot * band), (value.shape[0], band))


def shards(factor_rows, slot_row, known, rhs, *, members, bands):
    slots, _, band, width = factor_rows.shape
    half = band // 2
    columns = rhs.shape[2]
    stages = len(stage_orders(members)[0])
    aligned = band % 128 == 0
    place = lax.axis_index("ct")
    where = jnp.stack([lax.axis_index("rt"), place]).astype(jnp.int32)
    factor_rows = pltpu.with_memory_space_constraint(factor_rows, pltpu.HBM)
    known = pltpu.with_memory_space_constraint(known, pltpu.HBM)

    keep, send = first_band(where, slot_row, factor_rows)
    tile_one = keep + swap_core(send, members)
    got_tile = swap_chip(tile_one, members, 0)
    keep_one, send_one, keep, send = front(after(where, tile_one), slot_row, factor_rows, known, members)
    got_sum = swap_core(send_one, members)
    tile_one = tile_one + after(got_tile, keep_one)
    got_tile = swap_chip(tile_one, members, 1)
    sum_one = keep_one + after(got_sum, tile_one)
    got_pack = got_top = top = None
    for stage in range(stages):
        rows = sum_one.shape[0] // 2
        got_sum = swap_chip(sum_one[rows:], members, stage)
        if stage == 0:
            got_pack = swap_core(after(send, sum_one), members)
            top, send_top = top_band(after(where, sum_one), slot_row, factor_rows)
            got_sum = after(got_sum, top)
        sum_one = sum_one[:rows] + got_sum
        if stage == 0:
            got_top = swap_core(after(send_top, sum_one), members)
        if stage < stages - 1:
            tile_one = tile_one + after(got_tile, sum_one)
            got_tile = swap_chip(tile_one, members, stage + 2) if stage < stages - 2 else None

    got_up = []
    for shift in range(1, bands):
        piece = own_band(sum_one, jnp.minimum(place + shift, bands - 1), band)
        got_up.append(lax.ppermute(piece, "ct", [(i, i + shift) for i in range(bands - shift)]))

    other = swap_core(tile_one, members)

    tiles, sums = pack_step(keep, keep, half, after(got_pack, sum_one), half, False)
    got_pack = swap_chip(tiles, members, 0)
    (top,) = pack_step(top, None, 0, after(got_top, sum_one), half, True)
    got_top = swap_chip(top, members, 0)

    tile_one = join_halves(after(where, sum_one, top), tile_one, other, 0, half, range(bands))
    base = rhs[1].T - own_band(sum_one, place, band)
    for piece in got_up:
        base = base - after(piece, tile_one)

    packs = Packs((tiles, sums, half), got_pack, top, got_top, stages, bands, members)
    solved_one = sweep(where, base, tile_one, sum_one, bands, packs)

    low, sums, _ = packs.pack
    pieces = (couple if aligned else couple_plain)(where, sums, solved_one, low, packs.got, bands)
    base = rhs[0].T - pieces[0]
    tile_zero = join_halves(where, packs.top, packs.got_top, 0, half, ())
    for mask in range(bands - 1, 0, -1):
        got = lax.ppermute(pieces[mask], "ct", [(i, i ^ mask) for i in range(bands)])
        base = base - after(got, tile_zero)

    nothing = jnp.zeros((columns, width), F32)
    solved_zero = sweep(where, base, tile_zero, nothing, bands)
    return jnp.stack([solved_zero.T, solved_one.T])


def solution(mesh):
    members, bands = mesh.shape["rt"], mesh.shape["ct"]
    in_specs = (P("rt", None, "ct", None), P(), P("rt", "ct", None), P(None, "ct", "rt"))
    out_specs = P(None, "ct", "rt")
    body = functools.partial(shards, members=members, bands=bands)
    return jax.shard_map(body, mesh=mesh, in_specs=in_specs, out_specs=out_specs, check_vma=False)
```

```python
import functools

import jax
import jax.numpy as jnp
from jax import lax
from jax.experimental import pallas as pl
from jax.experimental.pallas import tpu as pltpu
from jax.sharding import PartitionSpec as P

F32 = jnp.float32
BF16 = jnp.bfloat16
VMEM = pl.BlockSpec(memory_space=pltpu.MemorySpace.VMEM)
SMEM = pl.BlockSpec(memory_space=pltpu.MemorySpace.SMEM)
HBM = pl.BlockSpec(memory_space=pl.ANY)


def shape(*dims):
    return jax.ShapeDtypeStruct(dims, F32)


def call(body, out, specs, args, name, scratch=(), aliases=None):
    multiple = isinstance(out, tuple)
    return pl.pallas_call(
        body,
        out_shape=out,
        in_specs=list(specs),
        out_specs=tuple(VMEM for _ in out) if multiple else VMEM,
        scratch_shapes=list(scratch),
        input_output_aliases=aliases or {},
        compiler_params=pltpu.CompilerParams(vmem_limit_bytes=40 << 20),
        name=name,
    )(*args)


def split(value):
    high = value.astype(BF16)
    return high, (value - high.astype(F32)).astype(BF16)


def dot_split(a, b, dims):
    (ah, al), (bh, bl) = a, b

    def one(u, v):
        return lax.dot_general(u, v, (dims, ((), ())), preferred_element_type=F32)

    return one(al, bh) + one(ah, bl) + one(ah, bh)


def dot3(a, b):
    return dot_split(split(a), split(b), ((1,), (0,)))


def stage_orders(members):
    bits = members.bit_length() - 1
    first = list(range(1, bits))
    return first, first[::-1]


def swap_core(value, members):
    return lax.ppermute(value, "rt", [(i, i ^ 1) for i in range(members)])


def swap_chip(value, members, stage):
    orders = stage_orders(members)
    return lax.ppermute(value, "rt", [(i, i ^ (1 << orders[i & 1][stage])) for i in range(members)])


def send_tables(members):
    orders = stage_orders(members)
    count = len(orders[0])
    tables = []
    for core in range(2):
        table = []
        for place in range(members):
            other = place >> count
            rest = place & ((1 << count) - 1)
            relative = other
            for stage in range(count):
                if (rest >> (count - 1 - stage)) & 1:
                    relative |= 1 << orders[core ^ other][stage]
            table.append(relative)
        tables.append(table)
    return tables


def front_kernel(
    where_ref, rows_ref, factor_ref, known_ref, keep_one, send_one, keep_ref, send_ref, factor_buf, known_buf, acc_ref, sems, low,
    *, tables
):
    slots, _, band, _ = factor_buf.shape
    me = where_ref[0]

    def live(slot):
        return rows_ref[me * slots + slot] >= 2

    def copies(slot, column):
        copy = pltpu.make_async_copy(factor_ref.at[slot, column], factor_buf.at[slot, column], sems.at[column, slot])
        if column == 0:
            return [copy]
        return [pltpu.make_async_copy(known_ref.at[slot], known_buf.at[slot], sems.at[2, slot]), copy]

    for column in (1, 0):
        for slot in range(slots):

            @pl.when(live(slot))
            def _():
                for copy in copies(slot, column):
                    copy.start()

    finish = put_band(where_ref, rows_ref, factor_ref, 1, 0, keep_ref, send_ref, 0, band // 2, low)
    for column, keep, send, first in ((1, keep_one, send_one, 0), (0, keep_ref, send_ref, band // 2)):
        acc_ref[...] = jnp.zeros_like(acc_ref)
        for slot in range(slots):

            @pl.when(live(slot))
            def _():
                for copy in copies(slot, column):
                    copy.wait()
                acc_ref[...] += dot_split(split(known_buf[slot]), split(factor_buf[slot, column]), ((0,), (0,)))

        in_send_order(where_ref, acc_ref, keep, send, first, tables)
    finish()


def in_send_order(where_ref, acc_ref, keep_ref, send_ref, first, tables):
    count = len(tables[0])
    columns = acc_ref.shape[0] // count
    me = where_ref[0]
    for spot, (even, odd) in enumerate(zip(*tables)):
        group = me ^ jnp.where((me & 1) == 0, even, odd)
        rows = acc_ref[pl.ds(pl.multiple_of(group * columns, columns), columns), :]
        target, start = (keep_ref, spot) if spot < count // 2 else (send_ref, spot - count // 2)
        target[first + start * columns : first + (start + 1) * columns, :] = rows


def owned_slot(where_ref, rows_ref, row, slots):
    slot = jnp.int32(-1)
    for s in range(slots):
        slot = jnp.where(rows_ref[where_ref[0] * slots + s] == row, s, slot)
    return slot


def band_copies(where_ref, factor_ref, slot, column, keep_ref, send_ref, first, half, sems):
    core = where_ref[0] & 1
    copies = []
    for index, (target, which) in enumerate(((send_ref, 1 - core), (keep_ref, core))):
        start = pl.multiple_of(which * half, half)
        source = factor_ref.at[slot, column, pl.ds(start, half), :]
        copies.append(pltpu.make_async_copy(source, target.at[pl.ds(first, half), :], sems.at[index]))
    return copies


def put_band(where_ref, rows_ref, factor_ref, row, column, keep_ref, send_ref, first, half, sems):
    slot = owned_slot(where_ref, rows_ref, row, factor_ref.shape[0])

    @pl.when(slot >= 0)
    def _():
        for copy in band_copies(where_ref, factor_ref, slot, column, keep_ref, send_ref, first, half, sems):
            copy.start()

    @pl.when(slot < 0)
    def _():
        keep_ref[first : first + half, :] = jnp.zeros((half, keep_ref.shape[1]), F32)
        send_ref[first : first + half, :] = jnp.zeros((half, keep_ref.shape[1]), F32)

    def finish():
        @pl.when(slot >= 0)
        def _():
            for copy in band_copies(where_ref, factor_ref, slot, column, keep_ref, send_ref, first, half, sems):
                copy.wait()

    return finish


def first_band(where, slot_row, factor_rows):
    _, _, band, width = factor_rows.shape
    half = band // 2

    def body(where_ref, rows_ref, factor_ref, keep_ref, send_ref, sems):
        put_band(where_ref, rows_ref, factor_ref, 1, 1, keep_ref, send_ref, 0, half, sems)()

    out = (shape(half, width), shape(half, width))
    scratch = [pltpu.SemaphoreType.DMA((2,))]
    return call(body, out, (SMEM, SMEM, HBM), (where, slot_row, factor_rows), "first_band", scratch)


def front(where, slot_row, factor_rows, known, members):
    slots, _, band, width = factor_rows.shape
    total = known.shape[2]
    one, rest = shape(total // 2, width), shape(band // 2 + total // 2, width)
    scratch = [
        pltpu.VMEM(factor_rows.shape, F32),
        pltpu.VMEM(known.shape, F32),
        pltpu.VMEM((total, width), F32),
        pltpu.SemaphoreType.DMA((3, slots)),
        pltpu.SemaphoreType.DMA((2,)),
    ]
    body = functools.partial(front_kernel, tables=send_tables(members))
    args = (where, slot_row, factor_rows, known)
    return call(body, (one, one, rest, rest), (SMEM, SMEM, HBM, HBM), args, "front", scratch)


def top_band(where, slot_row, factor_rows):
    slots, _, band, width = factor_rows.shape
    half = band // 2

    def body(where_ref, rows_ref, factor_ref, keep_ref, send_ref, tile_ref, sem):
        slot = owned_slot(where_ref, rows_ref, 0, slots)
        core = where_ref[0] & 1

        @pl.when(slot >= 0)
        def _():
            copy = pltpu.make_async_copy(factor_ref.at[slot, 0], tile_ref, sem)
            copy.start()
            copy.wait()
            invert_diagonal(tile_ref, where_ref[1], range(width // band), band)
            keep_ref[...] = tile_ref[pl.ds(pl.multiple_of(core * half, half), half), :]
            send_ref[...] = tile_ref[pl.ds(pl.multiple_of((1 - core) * half, half), half), :]

        @pl.when(slot < 0)
        def _():
            keep_ref[...] = jnp.zeros_like(keep_ref)
            send_ref[...] = jnp.zeros_like(send_ref)

    out = (shape(half, width), shape(half, width))
    scratch = [pltpu.VMEM((band, width), F32), pltpu.SemaphoreType.DMA(())]
    return call(body, out, (SMEM, SMEM, HBM), (where, slot_row, factor_rows), "top_band", scratch)


def after(value, *others):
    return lax.optimization_barrier((value,) + others)[0]


def pack_parts(sums, skip, got, tile_rows, final):
    width = got.shape[1]
    count = got.shape[0] - tile_rows
    go = count if final else count // 2

    def add(tiles_ref, sums_ref, got_ref, out_ref, keep_ref):
        out_ref[:tile_rows, :] = tiles_ref[:tile_rows, :] + got_ref[:tile_rows, :]
        keep_ref[...] = sums_ref[skip : skip + go, :] + got_ref[tile_rows : tile_rows + go, :]
        if not final:
            out_ref[tile_rows:, :] = sums_ref[skip + go : skip + count, :] + got_ref[tile_rows + go :, :]

    def add_tile(tiles_ref, got_ref, out_ref):
        out_ref[...] = tiles_ref[...] + got_ref[...]

    if sums is None:
        return add_tile, (shape(tile_rows, width),)
    return add, (shape(tile_rows + count - go, width), shape(go, width))


def pack_inputs(tiles, sums, skip, got, tile_rows, final):
    return (tiles, got) if sums is None else (tiles, sums, got)


def pack_step(*pack):
    add, out = pack_parts(*pack[1:])
    args = pack_inputs(*pack)
    return call(add, out, (VMEM,) * len(args), args, "pack_step")


def inverse_of(block):
    size = block.shape[0]
    base = min(size, 64)
    row = lax.broadcasted_iota(jnp.int32, (base, base), 0)
    col = lax.broadcasted_iota(jnp.int32, (base, base), 1)
    pair = (row - col == 1) & (row & 1 == 1)
    starts = range(0, size, base)
    blocks = [block[at : at + base, at : at + base] for at in starts]
    inverses = []
    for part in blocks:
        diag = jnp.where(row == col, part, 0.0)
        recip_row = 1.0 / jnp.sum(diag, axis=0, keepdims=True)
        recip_col = 1.0 / jnp.sum(diag, axis=1, keepdims=True)
        off = -(part * recip_row) * recip_col
        inverses.append(jnp.where(row == col, recip_row, jnp.where(pair, off, 0.0)))
    step = 2
    while step < base:
        half = lax.div(row, step)
        below = (half - lax.div(col, step) == 1) & (half & 1 == 1)
        parts = [split(inverse) for inverse in inverses]
        middle = [dot_split(split(jnp.where(below, b, 0.0)), p, ((1,), (0,))) for b, p in zip(blocks, parts)]
        inverses = [i - dot_split(p, split(m), ((1,), (0,))) for i, p, m in zip(inverses, parts, middle)]
        step *= 2
    width = base
    while len(inverses) > 1:
        merged = []
        for index in range(0, len(inverses), 2):
            first, second = inverses[index : index + 2]
            lower = block[(index + 1) * width : (index + 2) * width, index * width : (index + 1) * width]
            corner = -dot3(second, dot3(lower, first))
            top = jnp.concatenate([first, jnp.zeros_like(first)], 1)
            merged.append(jnp.concatenate([top, jnp.concatenate([corner, second], 1)], 0))
        inverses = merged
        width *= 2
    return inverses[0]


def invert_diagonal(tile_ref, place, chosen, band):
    for spot in chosen:

        @pl.when(place == spot)
        def _():
            here = slice(spot * band, (spot + 1) * band)
            tile_ref[:, here] = inverse_of(tile_ref[:, here])


def join_halves(where, mine, other, first, half, chosen):
    width = mine.shape[1]

    def body(where_ref, mine_ref, other_ref, tile_ref):
        core = where_ref[0] & 1
        tile_ref[pl.ds(pl.multiple_of(core * half, half), half), :] = mine_ref[first : first + half, :]
        tile_ref[pl.ds(pl.multiple_of((1 - core) * half, half), half), :] = other_ref[first : first + half, :]
        invert_diagonal(tile_ref, where_ref[1], chosen, 2 * half)

    return call(body, shape(2 * half, width), (SMEM, VMEM, VMEM), (where, mine, other), "join")


def run_stage(where, base, tile, add, near, far, held, stage, packs=()):
    columns, band = base.shape
    left = stage * band
    wide = far is None
    first = 0 if wide else max(left - band, 0)
    width = max(left, band) - first
    inputs = [pack_inputs(*pack) for pack in packs]
    more = [pack_parts(*pack[1:]) for pack in packs]
    count = sum(len(args) for args in inputs)
    come = (near,) if wide else (near, far)

    def body(where_ref, base_ref, tile_ref, add_ref, held_ref, *refs):
        come_refs, refs = refs[: len(come)], refs[len(come) :]
        ins, (solved_ref, update_ref), outs = refs[:count], refs[count : count + 2], refs[count + 2 :]

        @pl.when(where_ref[1] == stage)
        def _():
            if wide:
                right = base_ref[...] - come_refs[0][:, left:]
            else:
                right = base_ref[...] - come_refs[0][...] - come_refs[1][:, left : left + band]
            solved = dot3(right, tile_ref[:, left : left + band])
            solved_ref[...] = solved
            if stage > 0:
                here = slice(first, left)
                passed = come_refs[-1][:, here] + add_ref[:, here]
                update_ref[...] = passed + dot3(solved, tile_ref[:, here])

        @pl.when(where_ref[1] != stage)
        def _():
            solved_ref[...] = held_ref[...]

        for args, (add_pack, out) in zip(inputs, more):
            add_pack(*ins[: len(args)], *outs[: len(out)])
            ins, outs = ins[len(args) :], outs[len(out) :]

    out = (shape(columns, band), shape(columns, width)) + sum((out for _, out in more), ())
    args = (where, base, tile, add, held) + come + sum(inputs, ())
    return call(body, out, (SMEM,) + (VMEM,) * (len(args) - 1), args, "stage")


def run_rest(where, tile, add, far, solved, stage):
    columns, band = solved.shape
    last = (stage - 1) * band

    def body(where_ref, tile_ref, add_ref, far_ref, solved_ref, rest_ref):
        @pl.when(where_ref[1] == stage)
        def _():
            rest_ref[...] = far_ref[:, :last] + add_ref[:, :last] + dot3(solved_ref[...], tile_ref[:, :last])

    return call(body, shape(columns, last), (SMEM,) + (VMEM,) * 4, (where, tile, add, far, solved), "rest")


def run_stage_plain(where, base, tile, add, near, far, held, stage, packs=()):
    high = lax.Precision.HIGHEST
    band = base.shape[1]
    left = stage * band
    here = slice(max(left - band, 0), max(left, band))
    solved = jnp.dot(base - near - far[:, left : left + band], tile[:, left : left + band], precision=high)
    update = jnp.dot(solved, tile[:, here], precision=high) + add[:, here] + far[:, here]
    more = sum((tuple(pack_step(*pack)) for pack in packs), ())
    return (jnp.where(where[1] == stage, solved, held), update) + more


def run_rest_plain(where, tile, add, far, solved, stage):
    last = (stage - 1) * solved.shape[1]
    return far[:, :last] + add[:, :last] + jnp.dot(solved, tile[:, :last], precision=lax.Precision.HIGHEST)


def sweep(where, base, tile, add, bands, packs=None):
    columns, band = base.shape
    aligned = band % 128 == 0
    wide = packs is not None and aligned
    stage_of, rest_of = (run_stage, run_rest) if aligned else (run_stage_plain, run_rest_plain)
    near = jnp.zeros((columns, bands * band if wide else band), F32)
    held = jnp.zeros((columns, band), F32)
    fars = [None] * bands if wide else [jnp.zeros((columns, bands * band), F32)] * 2
    for stage in range(bands - 1, -1, -1):
        far = fars.pop(0)
        taken = packs.take(bands - 1 - stage) if packs else ()
        held, update, *more = stage_of(where, base, tile, add, near, far, held, stage, taken)
        if stage > 0:
            near = lax.ppermute(update, "ct", [(stage, stage - 1)])
        if stage > 1 and not wide:
            rest = rest_of(where, tile, add, far, held, stage)
            fars.append(lax.ppermute(rest, "ct", [(stage, stage - 2)]))
        if more:
            packs.put(*more)
    return held


class Packs:
    def __init__(self, pack, got, top, got_top, steps, bands, members):
        self.pack, self.got, self.top, self.got_top = pack, got, top, got_top
        self.steps, self.members = steps, members
        self.low_at = [bands - 2 - 2 * (steps - 1 - step) for step in range(steps)]
        self.top_at = [bands - 1 - 2 * (steps - 1 - step) for step in range(steps)]

    def take(self, index):
        taken = ()
        if index in self.low_at:
            tiles, sums, rows = self.pack
            taken += ((tiles, sums, 0, self.got, rows, index == self.low_at[-1]),)
        if index in self.top_at:
            taken += ((self.top, None, 0, self.got_top, self.top.shape[0], True),)
        self.index = index
        return taken

    def put(self, *outs):
        if self.index in self.low_at:
            tiles, sums, *outs = outs
            self.pack = (tiles, sums, self.pack[2])
            step = self.low_at.index(self.index) + 1
            if step < self.steps:
                self.got = swap_chip(tiles, self.members, step)
            else:
                self.got = swap_core(tiles, self.members)
        if self.index in self.top_at:
            (self.top,) = outs
            step = self.top_at.index(self.index) + 1
            if step < self.steps:
                self.got_top = swap_chip(self.top, self.members, step)
            else:
                self.got_top = swap_core(self.top, self.members)


def couple(where, sums, solved, mine, other, bands):
    columns, band = solved.shape
    half, width = mine.shape

    def body(where_ref, sums_ref, solved_ref, mine_ref, other_ref, out_ref, tile_ref, whole_ref):
        core = where_ref[0] & 1
        tile_ref[pl.ds(pl.multiple_of(core * half, half), half), :] = mine_ref[...]
        tile_ref[pl.ds(pl.multiple_of((1 - core) * half, half), half), :] = other_ref[...]
        whole_ref[...] = sums_ref[...] + dot3(solved_ref[...], tile_ref[...])
        for mask in range(bands):
            start = pl.multiple_of((where_ref[1] ^ mask) * band, band)
            out_ref[mask] = whole_ref[:, pl.ds(start, band)]

    scratch = [pltpu.VMEM((band, width), F32), pltpu.VMEM((columns, width), F32)]
    args = (where, sums, solved, mine, other)
    return call(body, shape(bands, columns, band), (SMEM,) + (VMEM,) * 4, args, "couple", scratch)


def couple_plain(where, sums, solved, mine, other, bands):
    band = solved.shape[1]
    tile = join_halves(where, mine, other, 0, band // 2, ())
    whole = sums + jnp.dot(solved, tile, precision=lax.Precision.HIGHEST)
    return jnp.stack([own_band(whole, where[1] ^ mask, band) for mask in range(bands)])


def own_band(value, spot, band):
    return lax.dynamic_slice(value, (0, spot * band), (value.shape[0], band))


def shards(factor_rows, slot_row, known, rhs, *, members, bands):
    slots, _, band, width = factor_rows.shape
    half = band // 2
    columns = rhs.shape[2]
    stages = len(stage_orders(members)[0])
    aligned = band % 128 == 0
    place = lax.axis_index("ct")
    where = jnp.stack([lax.axis_index("rt"), place]).astype(jnp.int32)
    factor_rows = pltpu.with_memory_space_constraint(factor_rows, pltpu.HBM)
    known = pltpu.with_memory_space_constraint(known, pltpu.HBM)

    keep, send = first_band(where, slot_row, factor_rows)
    tile_one = keep + swap_core(send, members)
    got_tile = swap_chip(tile_one, members, 0)
    keep_one, send_one, keep, send = front(after(where, tile_one), slot_row, factor_rows, known, members)
    got_sum = swap_core(send_one, members)
    tile_one = tile_one + after(got_tile, keep_one)
    got_tile = swap_chip(tile_one, members, 1)
    sum_one = keep_one + after(got_sum, tile_one)
    got_pack = got_top = top = None
    for stage in range(stages):
        rows = sum_one.shape[0] // 2
        got_sum = swap_chip(sum_one[rows:], members, stage)
        if stage == 0:
            got_pack = swap_core(after(send, sum_one), members)
            top, send_top = top_band(after(where, sum_one), slot_row, factor_rows)
            got_sum = after(got_sum, top)
        sum_one = sum_one[:rows] + got_sum
        if stage == 0:
            got_top = swap_core(after(send_top, sum_one), members)
        if stage < stages - 1:
            tile_one = tile_one + after(got_tile, sum_one)
            got_tile = swap_chip(tile_one, members, stage + 2) if stage < stages - 2 else None

    got_up = []
    for shift in range(bands - 1, 0, -1):
        piece = own_band(sum_one, jnp.minimum(place + shift, bands - 1), band)
        got_up.append(lax.ppermute(piece, "ct", [(i, i + shift) for i in range(bands - shift)]))

    other = swap_core(tile_one, members)

    tiles, sums = pack_step(keep, keep, half, after(got_pack, sum_one), half, False)
    got_pack = swap_chip(tiles, members, 0)
    (top,) = pack_step(top, None, 0, after(got_top, sum_one), half, True)
    got_top = swap_chip(top, members, 0)

    tile_one = join_halves(after(where, sum_one, top), tile_one, other, 0, half, range(bands))
    base = rhs[1].T - own_band(sum_one, place, band)
    for piece in got_up:
        base = base - after(piece, tile_one)

    packs = Packs((tiles, sums, half), got_pack, top, got_top, stages, bands, members)
    solved_one = sweep(where, base, tile_one, sum_one, bands, packs)

    low, sums, _ = packs.pack
    pieces = (couple if aligned else couple_plain)(where, sums, solved_one, low, packs.got, bands)
    base = rhs[0].T - pieces[0]
    tile_zero = join_halves(where, packs.top, packs.got_top, 0, half, ())
    for mask in range(bands - 1, 0, -1):
        got = lax.ppermute(pieces[mask], "ct", [(i, i ^ mask) for i in range(bands)])
        base = base - after(got, tile_zero)

    nothing = jnp.zeros((columns, width), F32)
    solved_zero = sweep(where, base, tile_zero, nothing, bands)
    return jnp.stack([solved_zero.T, solved_one.T])


def solution(mesh):
    members, bands = mesh.shape["rt"], mesh.shape["ct"]
    in_specs = (P("rt", None, "ct", None), P(), P("rt", "ct", None), P(None, "ct", "rt"))
    out_specs = P(None, "ct", "rt")
    body = functools.partial(shards, members=members, bands=bands)
    return jax.shard_map(body, mesh=mesh, in_specs=in_specs, out_specs=out_specs, check_vma=False)
```

```python
import functools

import jax
import jax.numpy as jnp
from jax import lax
from jax.experimental import pallas as pl
from jax.experimental.pallas import tpu as pltpu
from jax.sharding import PartitionSpec as P

F32 = jnp.float32
BF16 = jnp.bfloat16
VMEM = pl.BlockSpec(memory_space=pltpu.MemorySpace.VMEM)
SMEM = pl.BlockSpec(memory_space=pltpu.MemorySpace.SMEM)
HBM = pl.BlockSpec(memory_space=pl.ANY)


def shape(*dims):
    return jax.ShapeDtypeStruct(dims, F32)


def call(body, out, specs, args, name, scratch=(), aliases=None):
    multiple = isinstance(out, tuple)
    return pl.pallas_call(
        body,
        out_shape=out,
        in_specs=list(specs),
        out_specs=tuple(VMEM for _ in out) if multiple else VMEM,
        scratch_shapes=list(scratch),
        input_output_aliases=aliases or {},
        compiler_params=pltpu.CompilerParams(vmem_limit_bytes=40 << 20),
        name=name,
    )(*args)


def split(value):
    high = value.astype(BF16)
    return high, (value - high.astype(F32)).astype(BF16)


def dot_split(a, b, dims):
    (ah, al), (bh, bl) = a, b

    def one(u, v):
        return lax.dot_general(u, v, (dims, ((), ())), preferred_element_type=F32)

    return one(al, bh) + one(ah, bl) + one(ah, bh)


def dot3(a, b):
    return dot_split(split(a), split(b), ((1,), (0,)))


def stage_orders(members):
    bits = members.bit_length() - 1
    first = list(range(1, bits))
    return first, first[::-1]


def swap_core(value, members):
    return lax.ppermute(value, "rt", [(i, i ^ 1) for i in range(members)])


def swap_chip(value, members, stage):
    orders = stage_orders(members)
    return lax.ppermute(value, "rt", [(i, i ^ (1 << orders[i & 1][stage])) for i in range(members)])


def send_tables(members):
    orders = stage_orders(members)
    count = len(orders[0])
    tables = []
    for core in range(2):
        table = []
        for place in range(members):
            other = place >> count
            rest = place & ((1 << count) - 1)
            relative = other
            for stage in range(count):
                if (rest >> (count - 1 - stage)) & 1:
                    relative |= 1 << orders[core ^ other][stage]
            table.append(relative)
        tables.append(table)
    return tables


def front_kernel(
    where_ref, rows_ref, factor_ref, known_ref, keep_one, send_one, keep_ref, send_ref, factor_buf, known_buf, acc_ref, sems, low,
    *, tables
):
    slots, _, band, _ = factor_buf.shape
    me = where_ref[0]

    def live(slot):
        return rows_ref[me * slots + slot] >= 2

    def copies(slot, column):
        copy = pltpu.make_async_copy(factor_ref.at[slot, column], factor_buf.at[slot, column], sems.at[column, slot])
        if column == 0:
            return [copy]
        return [pltpu.make_async_copy(known_ref.at[slot], known_buf.at[slot], sems.at[2, slot]), copy]

    for column in (1, 0):
        for slot in range(slots):

            @pl.when(live(slot))
            def _():
                for copy in copies(slot, column):
                    copy.start()

    finish = put_band(where_ref, rows_ref, factor_ref, 1, 0, keep_ref, send_ref, 0, band // 2, low)
    for column, keep, send, first in ((1, keep_one, send_one, 0), (0, keep_ref, send_ref, band // 2)):
        acc_ref[...] = jnp.zeros_like(acc_ref)
        for slot in range(slots):

            @pl.when(live(slot))
            def _():
                for copy in copies(slot, column):
                    copy.wait()
                acc_ref[...] += dot_split(split(known_buf[slot]), split(factor_buf[slot, column]), ((0,), (0,)))

        in_send_order(where_ref, acc_ref, keep, send, first, tables)
    finish()


def in_send_order(where_ref, acc_ref, keep_ref, send_ref, first, tables):
    count = len(tables[0])
    columns = acc_ref.shape[0] // count
    me = where_ref[0]
    for spot, (even, odd) in enumerate(zip(*tables)):
        group = me ^ jnp.where((me & 1) == 0, even, odd)
        rows = acc_ref[pl.ds(pl.multiple_of(group * columns, columns), columns), :]
        target, start = (keep_ref, spot) if spot < count // 2 else (send_ref, spot - count // 2)
        target[first + start * columns : first + (start + 1) * columns, :] = rows


def owned_slot(where_ref, rows_ref, row, slots):
    slot = jnp.int32(-1)
    for s in range(slots):
        slot = jnp.where(rows_ref[where_ref[0] * slots + s] == row, s, slot)
    return slot


def band_copies(where_ref, factor_ref, slot, column, keep_ref, send_ref, first, half, sems):
    core = where_ref[0] & 1
    copies = []
    for index, (target, which) in enumerate(((send_ref, 1 - core), (keep_ref, core))):
        start = pl.multiple_of(which * half, half)
        source = factor_ref.at[slot, column, pl.ds(start, half), :]
        copies.append(pltpu.make_async_copy(source, target.at[pl.ds(first, half), :], sems.at[index]))
    return copies


def put_band(where_ref, rows_ref, factor_ref, row, column, keep_ref, send_ref, first, half, sems):
    slot = owned_slot(where_ref, rows_ref, row, factor_ref.shape[0])

    @pl.when(slot >= 0)
    def _():
        for copy in band_copies(where_ref, factor_ref, slot, column, keep_ref, send_ref, first, half, sems):
            copy.start()

    @pl.when(slot < 0)
    def _():
        keep_ref[first : first + half, :] = jnp.zeros((half, keep_ref.shape[1]), F32)
        send_ref[first : first + half, :] = jnp.zeros((half, keep_ref.shape[1]), F32)

    def finish():
        @pl.when(slot >= 0)
        def _():
            for copy in band_copies(where_ref, factor_ref, slot, column, keep_ref, send_ref, first, half, sems):
                copy.wait()

    return finish


def first_band(where, slot_row, factor_rows):
    _, _, band, width = factor_rows.shape
    half = band // 2

    def body(where_ref, rows_ref, factor_ref, keep_ref, send_ref, sems):
        put_band(where_ref, rows_ref, factor_ref, 1, 1, keep_ref, send_ref, 0, half, sems)()

    out = (shape(half, width), shape(half, width))
    scratch = [pltpu.SemaphoreType.DMA((2,))]
    return call(body, out, (SMEM, SMEM, HBM), (where, slot_row, factor_rows), "first_band", scratch)


def front(where, slot_row, factor_rows, known, members):
    slots, _, band, width = factor_rows.shape
    total = known.shape[2]
    one, rest = shape(total // 2, width), shape(band // 2 + total // 2, width)
    scratch = [
        pltpu.VMEM(factor_rows.shape, F32),
        pltpu.VMEM(known.shape, F32),
        pltpu.VMEM((total, width), F32),
        pltpu.SemaphoreType.DMA((3, slots)),
        pltpu.SemaphoreType.DMA((2,)),
    ]
    body = functools.partial(front_kernel, tables=send_tables(members))
    args = (where, slot_row, factor_rows, known)
    return call(body, (one, one, rest, rest), (SMEM, SMEM, HBM, HBM), args, "front", scratch)


def top_band(where, slot_row, factor_rows):
    slots, _, band, width = factor_rows.shape
    half = band // 2

    def body(where_ref, rows_ref, factor_ref, keep_ref, send_ref, tile_ref, sem):
        slot = owned_slot(where_ref, rows_ref, 0, slots)
        core = where_ref[0] & 1

        @pl.when(slot >= 0)
        def _():
            copy = pltpu.make_async_copy(factor_ref.at[slot, 0], tile_ref, sem)
            copy.start()
            copy.wait()
            invert_diagonal(tile_ref, where_ref[1], range(width // band), band)
            keep_ref[...] = tile_ref[pl.ds(pl.multiple_of(core * half, half), half), :]
            send_ref[...] = tile_ref[pl.ds(pl.multiple_of((1 - core) * half, half), half), :]

        @pl.when(slot < 0)
        def _():
            keep_ref[...] = jnp.zeros_like(keep_ref)
            send_ref[...] = jnp.zeros_like(send_ref)

    out = (shape(half, width), shape(half, width))
    scratch = [pltpu.VMEM((band, width), F32), pltpu.SemaphoreType.DMA(())]
    return call(body, out, (SMEM, SMEM, HBM), (where, slot_row, factor_rows), "top_band", scratch)


def finish_sum(where, value, got, rhs, bands):
    columns, width = got.shape
    band = width // bands

    def body(where_ref, value_ref, got_ref, rhs_ref, total_ref, base_ref, *piece_refs):
        total_ref[...] = value_ref[:columns, :] + got_ref[...]
        place = where_ref[1]

        def own(spot):
            return total_ref[:, pl.ds(pl.multiple_of(spot * band, band), band)]

        base_ref[...] = rhs_ref[1] - own(place)
        for shift, piece_ref in enumerate(piece_refs, 1):
            piece_ref[...] = own(jnp.minimum(place + shift, bands - 1))

    out = (shape(columns, width),) + (shape(columns, band),) * bands
    total, base, *pieces = call(body, out, (SMEM,) + (VMEM,) * 3, (where, value, got, rhs), "finish_sum")
    return total, base, pieces


def finish_plain(where, value, got, rhs, bands):
    total = value[: got.shape[0]] + got
    band = total.shape[1] // bands
    spots = [jnp.minimum(where[1] + shift, bands - 1) for shift in range(bands)]
    base, *pieces = [own_band(total, spot, band) for spot in spots]
    return total, rhs[1] - base, pieces


def after(value, *others):
    return lax.optimization_barrier((value,) + others)[0]


def pack_parts(sums, skip, got, tile_rows, final):
    width = got.shape[1]
    count = got.shape[0] - tile_rows
    go = count if final else count // 2

    def add(tiles_ref, sums_ref, got_ref, out_ref, keep_ref):
        out_ref[:tile_rows, :] = tiles_ref[:tile_rows, :] + got_ref[:tile_rows, :]
        keep_ref[...] = sums_ref[skip : skip + go, :] + got_ref[tile_rows : tile_rows + go, :]
        if not final:
            out_ref[tile_rows:, :] = sums_ref[skip + go : skip + count, :] + got_ref[tile_rows + go :, :]

    def add_tile(tiles_ref, got_ref, out_ref):
        out_ref[...] = tiles_ref[...] + got_ref[...]

    if sums is None:
        return add_tile, (shape(tile_rows, width),)
    return add, (shape(tile_rows + count - go, width), shape(go, width))


def pack_inputs(tiles, sums, skip, got, tile_rows, final):
    return (tiles, got) if sums is None else (tiles, sums, got)


def pack_step(*pack):
    add, out = pack_parts(*pack[1:])
    args = pack_inputs(*pack)
    return call(add, out, (VMEM,) * len(args), args, "pack_step")


def inverse_of(block):
    size = block.shape[0]
    base = min(size, 64)
    row = lax.broadcasted_iota(jnp.int32, (base, base), 0)
    col = lax.broadcasted_iota(jnp.int32, (base, base), 1)
    pair = (row - col == 1) & (row & 1 == 1)
    starts = range(0, size, base)
    blocks = [block[at : at + base, at : at + base] for at in starts]
    inverses = []
    for part in blocks:
        diag = jnp.where(row == col, part, 0.0)
        recip_row = 1.0 / jnp.sum(diag, axis=0, keepdims=True)
        recip_col = 1.0 / jnp.sum(diag, axis=1, keepdims=True)
        off = -(part * recip_row) * recip_col
        inverses.append(jnp.where(row == col, recip_row, jnp.where(pair, off, 0.0)))
    step = 2
    while step < base:
        half = lax.div(row, step)
        below = (half - lax.div(col, step) == 1) & (half & 1 == 1)
        parts = [split(inverse) for inverse in inverses]
        middle = [dot_split(split(jnp.where(below, b, 0.0)), p, ((1,), (0,))) for b, p in zip(blocks, parts)]
        inverses = [i - dot_split(p, split(m), ((1,), (0,))) for i, p, m in zip(inverses, parts, middle)]
        step *= 2
    width = base
    while len(inverses) > 1:
        merged = []
        for index in range(0, len(inverses), 2):
            first, second = inverses[index : index + 2]
            lower = block[(index + 1) * width : (index + 2) * width, index * width : (index + 1) * width]
            corner = -dot3(second, dot3(lower, first))
            top = jnp.concatenate([first, jnp.zeros_like(first)], 1)
            merged.append(jnp.concatenate([top, jnp.concatenate([corner, second], 1)], 0))
        inverses = merged
        width *= 2
    return inverses[0]


def invert_diagonal(tile_ref, place, chosen, band):
    for spot in chosen:

        @pl.when(place == spot)
        def _():
            here = slice(spot * band, (spot + 1) * band)
            tile_ref[:, here] = inverse_of(tile_ref[:, here])


def join_halves(where, mine, other, first, half, chosen):
    width = mine.shape[1]

    def body(where_ref, mine_ref, other_ref, tile_ref):
        core = where_ref[0] & 1
        tile_ref[pl.ds(pl.multiple_of(core * half, half), half), :] = mine_ref[first : first + half, :]
        tile_ref[pl.ds(pl.multiple_of((1 - core) * half, half), half), :] = other_ref[first : first + half, :]
        invert_diagonal(tile_ref, where_ref[1], chosen, 2 * half)

    return call(body, shape(2 * half, width), (SMEM, VMEM, VMEM), (where, mine, other), "join")


def run_stage(where, base, tile, add, near, far, held, stage, packs=(), ups=(), other=None):
    columns, band = base.shape
    left = stage * band
    wide = far is None
    first = 0 if wide else max(left - band, 0)
    width = max(left, band) - first
    inputs = [pack_inputs(*pack) for pack in packs]
    more = [pack_parts(*pack[1:]) for pack in packs]
    count = sum(len(args) for args in inputs)
    come = (near,) if wide else (near, far)
    stacked = other is not None
    extra = ups + ((other,) if stacked else ())

    def body(where_ref, base_ref, tile_ref, add_ref, held_ref, *refs):
        come_refs, refs = refs[: len(come)], refs[len(come) :]
        extra_refs, refs = refs[: len(extra)], refs[len(extra) :]
        ins, (solved_ref, update_ref), outs = refs[:count], refs[count : count + 2], refs[count + 2 :]
        if stacked:
            solved_ref[1] = extra_refs[-1][...]
            solved_ref = solved_ref.at[0]

        @pl.when(where_ref[1] == stage)
        def _():
            if wide:
                right = base_ref[...] - come_refs[0][:, left:]
            else:
                right = base_ref[...] - come_refs[0][...] - come_refs[1][:, left : left + band]
            for up_ref in extra_refs[: len(ups)]:
                right = right - up_ref[...]
            solved = dot3(right, tile_ref[:, left : left + band])
            solved_ref[...] = solved
            if stage > 0:
                here = slice(first, left)
                passed = come_refs[-1][:, here] + add_ref[:, here]
                update_ref[...] = passed + dot3(solved, tile_ref[:, here])

        @pl.when(where_ref[1] != stage)
        def _():
            solved_ref[...] = held_ref[...]

        for args, (add_pack, out) in zip(inputs, more):
            add_pack(*ins[: len(args)], *outs[: len(out)])
            ins, outs = ins[len(args) :], outs[len(out) :]

    answer = shape(2, columns, band) if stacked else shape(columns, band)
    out = (answer, shape(columns, width)) + sum((out for _, out in more), ())
    args = (where, base, tile, add, held) + come + extra + sum(inputs, ())
    return call(body, out, (SMEM,) + (VMEM,) * (len(args) - 1), args, "stage")


def run_rest(where, tile, add, far, solved, stage):
    columns, band = solved.shape
    last = (stage - 1) * band

    def body(where_ref, tile_ref, add_ref, far_ref, solved_ref, rest_ref):
        @pl.when(where_ref[1] == stage)
        def _():
            rest_ref[...] = far_ref[:, :last] + add_ref[:, :last] + dot3(solved_ref[...], tile_ref[:, :last])

    return call(body, shape(columns, last), (SMEM,) + (VMEM,) * 4, (where, tile, add, far, solved), "rest")


def run_stage_plain(where, base, tile, add, near, far, held, stage, packs=(), ups=(), other=None):
    high = lax.Precision.HIGHEST
    band = base.shape[1]
    left = stage * band
    here = slice(max(left - band, 0), max(left, band))
    solved = jnp.dot(base - near - far[:, left : left + band] - sum(ups), tile[:, left : left + band], precision=high)
    update = jnp.dot(solved, tile[:, here], precision=high) + add[:, here] + far[:, here]
    more = sum((tuple(pack_step(*pack)) for pack in packs), ())
    solved = jnp.where(where[1] == stage, solved, held)
    return (solved if other is None else jnp.stack([solved, other]), update) + more


def run_rest_plain(where, tile, add, far, solved, stage):
    last = (stage - 1) * solved.shape[1]
    return far[:, :last] + add[:, :last] + jnp.dot(solved, tile[:, :last], precision=lax.Precision.HIGHEST)


def sweep(where, base, tile, add, bands, packs=None, ups=(), other=None):
    columns, band = base.shape
    aligned = band % 128 == 0
    wide = packs is not None and aligned
    stage_of, rest_of = (run_stage, run_rest) if aligned else (run_stage_plain, run_rest_plain)
    near = jnp.zeros((columns, bands * band if wide else band), F32)
    held = jnp.zeros((columns, band), F32)
    fars = [None] * bands if wide else [jnp.zeros((columns, bands * band), F32)] * 2
    for stage in range(bands - 1, -1, -1):
        far = fars.pop(0)
        taken = packs.take(bands - 1 - stage) if packs else ()
        last = other if stage == 0 else None
        held, update, *more = stage_of(where, base, tile, add, near, far, held, stage, taken, ups, last)
        if stage > 0:
            near = lax.ppermute(update, "ct", [(stage, stage - 1)])
        if stage > 1 and not wide:
            rest = rest_of(where, tile, add, far, held, stage)
            fars.append(lax.ppermute(rest, "ct", [(stage, stage - 2)]))
        if more:
            packs.put(*more)
    return held


class Packs:
    def __init__(self, pack, got, top, got_top, steps, bands, members):
        self.pack, self.got, self.top, self.got_top = pack, got, top, got_top
        self.steps, self.members = steps, members
        self.low_at = [bands - 2 - 2 * (steps - 1 - step) for step in range(steps)]
        self.top_at = [bands - 1 - 2 * (steps - 1 - step) for step in range(steps)]

    def take(self, index):
        taken = ()
        if index in self.low_at:
            tiles, sums, rows = self.pack
            taken += ((tiles, sums, 0, self.got, rows, index == self.low_at[-1]),)
        if index in self.top_at:
            taken += ((self.top, None, 0, self.got_top, self.top.shape[0], True),)
        self.index = index
        return taken

    def put(self, *outs):
        if self.index in self.low_at:
            tiles, sums, *outs = outs
            self.pack = (tiles, sums, self.pack[2])
            step = self.low_at.index(self.index) + 1
            if step < self.steps:
                self.got = swap_chip(tiles, self.members, step)
            else:
                self.got = swap_core(tiles, self.members)
        if self.index in self.top_at:
            (self.top,) = outs
            step = self.top_at.index(self.index) + 1
            if step < self.steps:
                self.got_top = swap_chip(self.top, self.members, step)
            else:
                self.got_top = swap_core(self.top, self.members)


def couple(where, sums, solved, mine, other, rhs, bands):
    columns, band = solved.shape
    half, width = mine.shape

    def body(where_ref, sums_ref, solved_ref, mine_ref, other_ref, rhs_ref, *refs):
        outs, (tile_ref, whole_ref) = refs[:bands], refs[bands:]
        core = where_ref[0] & 1
        tile_ref[pl.ds(pl.multiple_of(core * half, half), half), :] = mine_ref[...]
        tile_ref[pl.ds(pl.multiple_of((1 - core) * half, half), half), :] = other_ref[...]
        whole_ref[...] = sums_ref[...] + dot3(solved_ref[...], tile_ref[...])
        for mask, out_ref in enumerate(outs):
            start = pl.multiple_of((where_ref[1] ^ mask) * band, band)
            piece = whole_ref[:, pl.ds(start, band)]
            out_ref[...] = piece if mask else rhs_ref[0] - piece

    scratch = [pltpu.VMEM((band, width), F32), pltpu.VMEM((columns, width), F32)]
    args = (where, sums, solved, mine, other, rhs)
    return call(body, (shape(columns, band),) * bands, (SMEM,) + (VMEM,) * 5, args, "couple", scratch)


def couple_plain(where, sums, solved, mine, other, rhs, bands):
    band = solved.shape[1]
    tile = join_halves(where, mine, other, 0, band // 2, ())
    whole = sums + jnp.dot(solved, tile, precision=lax.Precision.HIGHEST)
    pieces = [own_band(whole, where[1] ^ mask, band) for mask in range(bands)]
    return [rhs[0] - pieces[0]] + pieces[1:]


def own_band(value, spot, band):
    return lax.dynamic_slice(value, (0, spot * band), (value.shape[0], band))


def shards(factor_rows, slot_row, known, rhs, *, members, bands):
    slots, _, band, width = factor_rows.shape
    half = band // 2
    columns = rhs.shape[2]
    stages = len(stage_orders(members)[0])
    aligned = band % 128 == 0
    place = lax.axis_index("ct")
    where = jnp.stack([lax.axis_index("rt"), place]).astype(jnp.int32)
    factor_rows = pltpu.with_memory_space_constraint(factor_rows, pltpu.HBM)
    known = pltpu.with_memory_space_constraint(known, pltpu.HBM)
    rhs = jnp.swapaxes(rhs, 1, 2)

    keep, send = first_band(where, slot_row, factor_rows)
    tile_one = keep + swap_core(send, members)
    got_tile = swap_chip(tile_one, members, 0)
    keep_one, send_one, keep, send = front(after(where, tile_one), slot_row, factor_rows, known, members)
    got_sum = swap_core(send_one, members)
    tile_one = tile_one + after(got_tile, keep_one)
    got_tile = swap_chip(tile_one, members, 1)
    sum_one = keep_one + after(got_sum, tile_one)
    got_pack = got_top = top = None
    for stage in range(stages):
        rows = sum_one.shape[0] // 2
        got_sum = swap_chip(sum_one[rows:], members, stage)
        if stage == 0:
            got_pack = swap_core(after(send, sum_one), members)
            top, send_top = top_band(after(where, sum_one), slot_row, factor_rows)
            got_sum = after(got_sum, top)
        if stage < stages - 1:
            sum_one = sum_one[:rows] + got_sum
        else:
            finish = finish_sum if aligned else finish_plain
            sum_one, base, pieces = finish(where, sum_one, got_sum, rhs, bands)
        if stage == 0:
            got_top = swap_core(after(send_top, sum_one), members)
        if stage < stages - 1:
            tile_one = tile_one + after(got_tile, sum_one)
            got_tile = swap_chip(tile_one, members, stage + 2) if stage < stages - 2 else None

    got_up = []
    for shift in range(bands - 1, 0, -1):
        got_up.append(lax.ppermute(pieces[shift - 1], "ct", [(i, i + shift) for i in range(bands - shift)]))

    other = swap_core(tile_one, members)

    tiles, sums = pack_step(keep, keep, half, after(got_pack, sum_one), half, False)
    got_pack = swap_chip(tiles, members, 0)
    (top,) = pack_step(top, None, 0, after(got_top, sum_one), half, True)
    got_top = swap_chip(top, members, 0)

    tile_one = join_halves(after(where, sum_one, top), tile_one, other, 0, half, range(bands))
    packs = Packs((tiles, sums, half), got_pack, top, got_top, stages, bands, members)
    ups = tuple(after(piece, tile_one) for piece in got_up)
    solved_one = sweep(where, base, tile_one, sum_one, bands, packs, ups)

    low, sums, _ = packs.pack
    base, *pieces = (couple if aligned else couple_plain)(where, sums, solved_one, low, packs.got, rhs, bands)
    tile_zero = join_halves(where, packs.top, packs.got_top, 0, half, ())
    ups = ()
    for mask in range(bands - 1, 0, -1):
        got = lax.ppermute(pieces[mask - 1], "ct", [(i, i ^ mask) for i in range(bands)])
        ups += (after(got, tile_zero),)

    nothing = jnp.zeros((columns, width), F32)
    answer = sweep(where, base, tile_zero, nothing, bands, None, ups, solved_one)
    return jnp.swapaxes(answer, 1, 2)


def solution(mesh):
    members, bands = mesh.shape["rt"], mesh.shape["ct"]
    in_specs = (P("rt", None, "ct", None), P(), P("rt", "ct", None), P(None, "ct", "rt"))
    out_specs = P(None, "ct", "rt")
    body = functools.partial(shards, members=members, bands=bands)
    return jax.shard_map(body, mesh=mesh, in_specs=in_specs, out_specs=out_specs, check_vma=False)
```

```python
import functools

import jax
import jax.numpy as jnp
from jax import lax
from jax.experimental import pallas as pl
from jax.experimental.pallas import tpu as pltpu
from jax.sharding import PartitionSpec as P

F32 = jnp.float32
BF16 = jnp.bfloat16
VMEM = pl.BlockSpec(memory_space=pltpu.MemorySpace.VMEM)
SMEM = pl.BlockSpec(memory_space=pltpu.MemorySpace.SMEM)
HBM = pl.BlockSpec(memory_space=pl.ANY)


def shape(*dims):
    return jax.ShapeDtypeStruct(dims, F32)


def call(body, out, specs, args, name, scratch=(), aliases=None):
    multiple = isinstance(out, tuple)
    return pl.pallas_call(
        body,
        out_shape=out,
        in_specs=list(specs),
        out_specs=tuple(VMEM for _ in out) if multiple else VMEM,
        scratch_shapes=list(scratch),
        input_output_aliases=aliases or {},
        compiler_params=pltpu.CompilerParams(vmem_limit_bytes=40 << 20),
        name=name,
    )(*args)


def split(value):
    high = value.astype(BF16)
    return high, (value - high.astype(F32)).astype(BF16)


def dot_split(a, b, dims):
    (ah, al), (bh, bl) = a, b

    def one(u, v):
        return lax.dot_general(u, v, (dims, ((), ())), preferred_element_type=F32)

    return one(al, bh) + one(ah, bl) + one(ah, bh)


def dot3(a, b):
    return dot_split(split(a), split(b), ((1,), (0,)))


def stage_orders(members):
    bits = members.bit_length() - 1
    first = list(range(1, bits))
    return first, first[::-1]


def swap_core(value, members):
    return lax.ppermute(value, "rt", [(i, i ^ 1) for i in range(members)])


def swap_chip(value, members, stage):
    orders = stage_orders(members)
    return lax.ppermute(value, "rt", [(i, i ^ (1 << orders[i & 1][stage])) for i in range(members)])


def send_tables(members):
    orders = stage_orders(members)
    count = len(orders[0])
    tables = []
    for core in range(2):
        table = []
        for place in range(members):
            other = place >> count
            rest = place & ((1 << count) - 1)
            relative = other
            for stage in range(count):
                if (rest >> (count - 1 - stage)) & 1:
                    relative |= 1 << orders[core ^ other][stage]
            table.append(relative)
        tables.append(table)
    return tables


def front_kernel(
    where_ref, rows_ref, factor_ref, known_ref, keep_one, send_one, keep_ref, send_ref, factor_buf, known_buf, acc_ref, sems, low,
    *, tables
):
    slots, _, band, _ = factor_buf.shape
    me = where_ref[0]

    def live(slot):
        return rows_ref[me * slots + slot] >= 2

    def copies(slot, column):
        copy = pltpu.make_async_copy(factor_ref.at[slot, column], factor_buf.at[slot, column], sems.at[column, slot])
        if column == 0:
            return [copy]
        return [pltpu.make_async_copy(known_ref.at[slot], known_buf.at[slot], sems.at[2, slot]), copy]

    for column in (1, 0):
        for slot in range(slots):

            @pl.when(live(slot))
            def _():
                for copy in copies(slot, column):
                    copy.start()

    finish = put_band(where_ref, rows_ref, factor_ref, 1, 0, keep_ref, send_ref, 0, band // 2, low)
    for column, keep, send, first in ((1, keep_one, send_one, 0), (0, keep_ref, send_ref, band // 2)):
        acc_ref[...] = jnp.zeros_like(acc_ref)
        for slot in range(slots):

            @pl.when(live(slot))
            def _():
                for copy in copies(slot, column):
                    copy.wait()
                acc_ref[...] += dot_split(split(known_buf[slot]), split(factor_buf[slot, column]), ((0,), (0,)))

        in_send_order(where_ref, acc_ref, keep, send, first, tables)
    finish()


def in_send_order(where_ref, acc_ref, keep_ref, send_ref, first, tables):
    count = len(tables[0])
    columns = acc_ref.shape[0] // count
    me = where_ref[0]
    for spot, (even, odd) in enumerate(zip(*tables)):
        group = me ^ jnp.where((me & 1) == 0, even, odd)
        rows = acc_ref[pl.ds(pl.multiple_of(group * columns, columns), columns), :]
        target, start = (keep_ref, spot) if spot < count // 2 else (send_ref, spot - count // 2)
        target[first + start * columns : first + (start + 1) * columns, :] = rows


def owned_slot(where_ref, rows_ref, row, slots):
    slot = jnp.int32(-1)
    for s in range(slots):
        slot = jnp.where(rows_ref[where_ref[0] * slots + s] == row, s, slot)
    return slot


def band_copies(where_ref, factor_ref, slot, column, keep_ref, send_ref, first, half, sems):
    core = where_ref[0] & 1
    copies = []
    for index, (target, which) in enumerate(((send_ref, 1 - core), (keep_ref, core))):
        start = pl.multiple_of(which * half, half)
        source = factor_ref.at[slot, column, pl.ds(start, half), :]
        copies.append(pltpu.make_async_copy(source, target.at[pl.ds(first, half), :], sems.at[index]))
    return copies


def put_band(where_ref, rows_ref, factor_ref, row, column, keep_ref, send_ref, first, half, sems):
    slot = owned_slot(where_ref, rows_ref, row, factor_ref.shape[0])

    @pl.when(slot >= 0)
    def _():
        for copy in band_copies(where_ref, factor_ref, slot, column, keep_ref, send_ref, first, half, sems):
            copy.start()

    @pl.when(slot < 0)
    def _():
        keep_ref[first : first + half, :] = jnp.zeros((half, keep_ref.shape[1]), F32)
        send_ref[first : first + half, :] = jnp.zeros((half, keep_ref.shape[1]), F32)

    def finish():
        @pl.when(slot >= 0)
        def _():
            for copy in band_copies(where_ref, factor_ref, slot, column, keep_ref, send_ref, first, half, sems):
                copy.wait()

    return finish


def first_band(where, slot_row, factor_rows):
    _, _, band, width = factor_rows.shape
    half = band // 2

    def body(where_ref, rows_ref, factor_ref, keep_ref, send_ref, sems):
        put_band(where_ref, rows_ref, factor_ref, 1, 1, keep_ref, send_ref, 0, half, sems)()

    out = (shape(half, width), shape(half, width))
    scratch = [pltpu.SemaphoreType.DMA((2,))]
    return call(body, out, (SMEM, SMEM, HBM), (where, slot_row, factor_rows), "first_band", scratch)


def front(where, slot_row, factor_rows, known, members):
    slots, _, band, width = factor_rows.shape
    total = known.shape[2]
    one, rest = shape(total // 2, width), shape(band // 2 + total // 2, width)
    scratch = [
        pltpu.VMEM(factor_rows.shape, F32),
        pltpu.VMEM(known.shape, F32),
        pltpu.VMEM((total, width), F32),
        pltpu.SemaphoreType.DMA((3, slots)),
        pltpu.SemaphoreType.DMA((2,)),
    ]
    body = functools.partial(front_kernel, tables=send_tables(members))
    args = (where, slot_row, factor_rows, known)
    return call(body, (one, one, rest, rest), (SMEM, SMEM, HBM, HBM), args, "front", scratch)


def top_band(where, slot_row, factor_rows):
    slots, _, band, width = factor_rows.shape
    half = band // 2

    def body(where_ref, rows_ref, factor_ref, keep_ref, send_ref, tile_ref, sem):
        slot = owned_slot(where_ref, rows_ref, 0, slots)
        core = where_ref[0] & 1

        @pl.when(slot >= 0)
        def _():
            copy = pltpu.make_async_copy(factor_ref.at[slot, 0], tile_ref, sem)
            copy.start()
            copy.wait()
            invert_diagonal(tile_ref, where_ref[1], range(width // band), band)
            keep_ref[...] = tile_ref[pl.ds(pl.multiple_of(core * half, half), half), :]
            send_ref[...] = tile_ref[pl.ds(pl.multiple_of((1 - core) * half, half), half), :]

        @pl.when(slot < 0)
        def _():
            keep_ref[...] = jnp.zeros_like(keep_ref)
            send_ref[...] = jnp.zeros_like(send_ref)

    out = (shape(half, width), shape(half, width))
    scratch = [pltpu.VMEM((band, width), F32), pltpu.SemaphoreType.DMA(())]
    return call(body, out, (SMEM, SMEM, HBM), (where, slot_row, factor_rows), "top_band", scratch)


def finish_sum(where, value, got, rhs, bands):
    columns, width = got.shape
    band = width // bands

    def body(where_ref, value_ref, got_ref, rhs_ref, total_ref, base_ref, *piece_refs):
        total_ref[...] = value_ref[:columns, :] + got_ref[...]
        place = where_ref[1]

        def own(spot):
            return total_ref[:, pl.ds(pl.multiple_of(spot * band, band), band)]

        base_ref[...] = rhs_ref[1] - own(place)
        for shift, piece_ref in enumerate(piece_refs, 1):
            piece_ref[...] = own(jnp.minimum(place + shift, bands - 1))

    out = (shape(columns, width),) + (shape(columns, band),) * bands
    total, base, *pieces = call(body, out, (SMEM,) + (VMEM,) * 3, (where, value, got, rhs), "finish_sum")
    return total, base, pieces


def finish_plain(where, value, got, rhs, bands):
    total = value[: got.shape[0]] + got
    band = total.shape[1] // bands
    spots = [jnp.minimum(where[1] + shift, bands - 1) for shift in range(bands)]
    base, *pieces = [own_band(total, spot, band) for spot in spots]
    return total, rhs[1] - base, pieces


def after(value, *others):
    return lax.optimization_barrier((value,) + others)[0]


def pack_parts(sums, skip, got, tile_rows, final):
    width = got.shape[1]
    count = got.shape[0] - tile_rows
    go = count if final else count // 2

    def add(tiles_ref, sums_ref, got_ref, out_ref, keep_ref):
        out_ref[:tile_rows, :] = tiles_ref[:tile_rows, :] + got_ref[:tile_rows, :]
        keep_ref[...] = sums_ref[skip : skip + go, :] + got_ref[tile_rows : tile_rows + go, :]
        if not final:
            out_ref[tile_rows:, :] = sums_ref[skip + go : skip + count, :] + got_ref[tile_rows + go :, :]

    def add_tile(tiles_ref, got_ref, out_ref):
        out_ref[...] = tiles_ref[...] + got_ref[...]

    if sums is None:
        return add_tile, (shape(tile_rows, width),)
    return add, (shape(tile_rows + count - go, width), shape(go, width))


def pack_inputs(tiles, sums, skip, got, tile_rows, final):
    return (tiles, got) if sums is None else (tiles, sums, got)


def pack_step(*pack):
    add, out = pack_parts(*pack[1:])
    args = pack_inputs(*pack)
    return call(add, out, (VMEM,) * len(args), args, "pack_step")


def inverse_of(block):
    size = block.shape[0]
    base = min(size, 64)
    row = lax.broadcasted_iota(jnp.int32, (base, base), 0)
    col = lax.broadcasted_iota(jnp.int32, (base, base), 1)
    pair = (row - col == 1) & (row & 1 == 1)
    starts = range(0, size, base)
    blocks = [block[at : at + base, at : at + base] for at in starts]
    inverses = []
    for part in blocks:
        diag = jnp.where(row == col, part, 0.0)
        recip_row = 1.0 / jnp.sum(diag, axis=0, keepdims=True)
        recip_col = 1.0 / jnp.sum(diag, axis=1, keepdims=True)
        off = -(part * recip_row) * recip_col
        inverses.append(jnp.where(row == col, recip_row, jnp.where(pair, off, 0.0)))
    step = 2
    while step < base:
        half = lax.div(row, step)
        below = (half - lax.div(col, step) == 1) & (half & 1 == 1)
        parts = [split(inverse) for inverse in inverses]
        middle = [dot_split(split(jnp.where(below, b, 0.0)), p, ((1,), (0,))) for b, p in zip(blocks, parts)]
        inverses = [i - dot_split(p, split(m), ((1,), (0,))) for i, p, m in zip(inverses, parts, middle)]
        step *= 2
    width = base
    while len(inverses) > 1:
        merged = []
        for index in range(0, len(inverses), 2):
            first, second = inverses[index : index + 2]
            lower = block[(index + 1) * width : (index + 2) * width, index * width : (index + 1) * width]
            corner = -dot3(second, dot3(lower, first))
            top = jnp.concatenate([first, jnp.zeros_like(first)], 1)
            merged.append(jnp.concatenate([top, jnp.concatenate([corner, second], 1)], 0))
        inverses = merged
        width *= 2
    return inverses[0]


def invert_diagonal(tile_ref, place, chosen, band):
    for spot in chosen:

        @pl.when(place == spot)
        def _():
            here = slice(spot * band, (spot + 1) * band)
            tile_ref[:, here] = inverse_of(tile_ref[:, here])


def join_halves(where, mine, other, first, half, chosen):
    width = mine.shape[1]

    def body(where_ref, mine_ref, other_ref, tile_ref):
        core = where_ref[0] & 1
        tile_ref[pl.ds(pl.multiple_of(core * half, half), half), :] = mine_ref[first : first + half, :]
        tile_ref[pl.ds(pl.multiple_of((1 - core) * half, half), half), :] = other_ref[first : first + half, :]
        invert_diagonal(tile_ref, where_ref[1], chosen, 2 * half)

    return call(body, shape(2 * half, width), (SMEM, VMEM, VMEM), (where, mine, other), "join")


def run_stage(where, base, tile, add, near, far, held, stage, packs=(), ups=(), other=None):
    columns, band = base.shape
    left = stage * band
    wide = far is None
    first = 0 if wide else max(left - band, 0)
    width = max(left, band) - first
    inputs = [pack_inputs(*pack) for pack in packs]
    more = [pack_parts(*pack[1:]) for pack in packs]
    count = sum(len(args) for args in inputs)
    come = (near,) if wide else (near, far)
    stacked = other is not None
    extra = ups + ((other,) if stacked else ())

    def body(where_ref, base_ref, tile_ref, add_ref, held_ref, *refs):
        come_refs, refs = refs[: len(come)], refs[len(come) :]
        extra_refs, refs = refs[: len(extra)], refs[len(extra) :]
        ins, (solved_ref, update_ref), outs = refs[:count], refs[count : count + 2], refs[count + 2 :]
        if stacked:
            solved_ref[1] = extra_refs[-1][...]
            solved_ref = solved_ref.at[0]

        @pl.when(where_ref[1] == stage)
        def _():
            if wide:
                right = base_ref[...] - come_refs[0][:, left:]
            else:
                right = base_ref[...] - come_refs[0][...] - come_refs[1][:, left : left + band]
            for up_ref in extra_refs[: len(ups)]:
                right = right - up_ref[...]
            solved = dot3(right, tile_ref[:, left : left + band])
            solved_ref[...] = solved
            if stage > 0:
                here = slice(first, left)
                passed = come_refs[-1][:, here] + add_ref[:, here]
                update_ref[...] = passed + dot3(solved, tile_ref[:, here])

        @pl.when(where_ref[1] != stage)
        def _():
            solved_ref[...] = held_ref[...]

        for args, (add_pack, out) in zip(inputs, more):
            add_pack(*ins[: len(args)], *outs[: len(out)])
            ins, outs = ins[len(args) :], outs[len(out) :]

    answer = shape(2, columns, band) if stacked else shape(columns, band)
    out = (answer, shape(columns, width)) + sum((out for _, out in more), ())
    args = (where, base, tile, add, held) + come + extra + sum(inputs, ())
    return call(body, out, (SMEM,) + (VMEM,) * (len(args) - 1), args, "stage")


def run_rest(where, tile, add, far, solved, stage):
    columns, band = solved.shape
    last = (stage - 1) * band

    def body(where_ref, tile_ref, add_ref, far_ref, solved_ref, rest_ref):
        @pl.when(where_ref[1] == stage)
        def _():
            rest_ref[...] = far_ref[:, :last] + add_ref[:, :last] + dot3(solved_ref[...], tile_ref[:, :last])

    return call(body, shape(columns, last), (SMEM,) + (VMEM,) * 4, (where, tile, add, far, solved), "rest")


def run_stage_plain(where, base, tile, add, near, far, held, stage, packs=(), ups=(), other=None):
    high = lax.Precision.HIGHEST
    band = base.shape[1]
    left = stage * band
    here = slice(max(left - band, 0), max(left, band))
    solved = jnp.dot(base - near - far[:, left : left + band] - sum(ups), tile[:, left : left + band], precision=high)
    update = jnp.dot(solved, tile[:, here], precision=high) + add[:, here] + far[:, here]
    more = sum((tuple(pack_step(*pack)) for pack in packs), ())
    solved = jnp.where(where[1] == stage, solved, held)
    return (solved if other is None else jnp.stack([solved, other]), update) + more


def run_rest_plain(where, tile, add, far, solved, stage):
    last = (stage - 1) * solved.shape[1]
    return far[:, :last] + add[:, :last] + jnp.dot(solved, tile[:, :last], precision=lax.Precision.HIGHEST)


def sweep(where, base, tile, add, bands, packs=None, ups=(), other=None):
    columns, band = base.shape
    aligned = band % 128 == 0
    wide = packs is not None and aligned
    stage_of, rest_of = (run_stage, run_rest) if aligned else (run_stage_plain, run_rest_plain)
    near = jnp.zeros((columns, bands * band if wide else band), F32)
    held = jnp.zeros((columns, band), F32)
    fars = [None] * bands if wide else [jnp.zeros((columns, bands * band), F32)] * 2
    for stage in range(bands - 1, -1, -1):
        far = fars.pop(0)
        taken = packs.take(bands - 1 - stage) if packs else ()
        last = other if stage == 0 else None
        held, update, *more = stage_of(where, base, tile, add, near, far, held, stage, taken, ups, last)
        if stage > 0:
            near = lax.ppermute(update, "ct", [(stage, stage - 1)])
        if stage > 1 and not wide:
            rest = rest_of(where, tile, add, far, held, stage)
            fars.append(lax.ppermute(rest, "ct", [(stage, stage - 2)]))
        if more:
            packs.put(*more)
        if packs:
            near = packs.loose(held, near)
    return held


class Packs:
    def __init__(self, pack, got, top, got_top, steps, bands, members):
        self.pack, self.got, self.top, self.got_top = pack, got, top, got_top
        self.steps, self.members = steps, members
        self.low_at = [bands - 2 - 2 * (steps - 1 - step) for step in range(steps - 1)]
        self.loose_at = bands - 2
        self.top_at = [bands - 1 - 2 * (steps - 1 - step) for step in range(steps)]

    def take(self, index):
        taken = ()
        if index in self.low_at:
            tiles, sums, rows = self.pack
            taken += ((tiles, sums, 0, self.got, rows, False),)
        if index in self.top_at:
            taken += ((self.top, None, 0, self.got_top, self.top.shape[0], True),)
        self.index = index
        return taken

    def loose(self, held, near):
        if self.index != self.loose_at:
            return near
        tiles, sums, rows = self.pack
        tiles, sums = pack_step(tiles, sums, 0, after(self.got, held), rows, True)
        self.pack = (tiles, sums, rows)
        self.got = swap_core(tiles, self.members)
        return after(near, tiles)

    def put(self, *outs):
        if self.index in self.low_at:
            tiles, sums, *outs = outs
            self.pack = (tiles, sums, self.pack[2])
            step = self.low_at.index(self.index) + 1
            if step < self.steps:
                self.got = swap_chip(tiles, self.members, step)
            else:
                self.got = swap_core(tiles, self.members)
        if self.index in self.top_at:
            (self.top,) = outs
            step = self.top_at.index(self.index) + 1
            if step < self.steps:
                self.got_top = swap_chip(self.top, self.members, step)
            else:
                self.got_top = swap_core(self.top, self.members)


def couple(where, sums, solved, mine, other, rhs, bands):
    columns, band = solved.shape
    half, width = mine.shape

    def body(where_ref, sums_ref, solved_ref, mine_ref, other_ref, rhs_ref, *refs):
        outs, (tile_ref, whole_ref) = refs[:bands], refs[bands:]
        core = where_ref[0] & 1
        tile_ref[pl.ds(pl.multiple_of(core * half, half), half), :] = mine_ref[...]
        tile_ref[pl.ds(pl.multiple_of((1 - core) * half, half), half), :] = other_ref[...]
        whole_ref[...] = sums_ref[...] + dot3(solved_ref[...], tile_ref[...])
        for mask, out_ref in enumerate(outs):
            start = pl.multiple_of((where_ref[1] ^ mask) * band, band)
            piece = whole_ref[:, pl.ds(start, band)]
            out_ref[...] = piece if mask else rhs_ref[0] - piece

    scratch = [pltpu.VMEM((band, width), F32), pltpu.VMEM((columns, width), F32)]
    args = (where, sums, solved, mine, other, rhs)
    return call(body, (shape(columns, band),) * bands, (SMEM,) + (VMEM,) * 5, args, "couple", scratch)


def couple_plain(where, sums, solved, mine, other, rhs, bands):
    band = solved.shape[1]
    tile = join_halves(where, mine, other, 0, band // 2, ())
    whole = sums + jnp.dot(solved, tile, precision=lax.Precision.HIGHEST)
    pieces = [own_band(whole, where[1] ^ mask, band) for mask in range(bands)]
    return [rhs[0] - pieces[0]] + pieces[1:]


def own_band(value, spot, band):
    return lax.dynamic_slice(value, (0, spot * band), (value.shape[0], band))


def shards(factor_rows, slot_row, known, rhs, *, members, bands):
    slots, _, band, width = factor_rows.shape
    half = band // 2
    columns = rhs.shape[2]
    stages = len(stage_orders(members)[0])
    aligned = band % 128 == 0
    place = lax.axis_index("ct")
    where = jnp.stack([lax.axis_index("rt"), place]).astype(jnp.int32)
    factor_rows = pltpu.with_memory_space_constraint(factor_rows, pltpu.HBM)
    known = pltpu.with_memory_space_constraint(known, pltpu.HBM)
    rhs = jnp.swapaxes(rhs, 1, 2)

    keep, send = first_band(where, slot_row, factor_rows)
    tile_one = keep + swap_core(send, members)
    got_tile = swap_chip(tile_one, members, 0)
    keep_one, send_one, keep, send = front(after(where, tile_one), slot_row, factor_rows, known, members)
    got_sum = swap_core(send_one, members)
    tile_one = tile_one + after(got_tile, keep_one)
    got_tile = swap_chip(tile_one, members, 1)
    sum_one = keep_one + after(got_sum, tile_one)
    got_pack = got_top = top = None
    for stage in range(stages):
        rows = sum_one.shape[0] // 2
        got_sum = swap_chip(sum_one[rows:], members, stage)
        if stage == 0:
            got_pack = swap_core(after(send, sum_one), members)
            top, send_top = top_band(after(where, sum_one), slot_row, factor_rows)
            got_sum = after(got_sum, top)
        if stage < stages - 1:
            sum_one = sum_one[:rows] + got_sum
        else:
            finish = finish_sum if aligned else finish_plain
            sum_one, base, pieces = finish(where, sum_one, got_sum, rhs, bands)
        if stage == 0:
            got_top = swap_core(after(send_top, sum_one), members)
        if stage < stages - 1:
            tile_one = tile_one + after(got_tile, sum_one)
            got_tile = swap_chip(tile_one, members, stage + 2) if stage < stages - 2 else None

    got_up = []
    for shift in range(bands - 1, 0, -1):
        got_up.append(lax.ppermute(pieces[shift - 1], "ct", [(i, i + shift) for i in range(bands - shift)]))

    other = swap_core(tile_one, members)

    tiles, sums = pack_step(keep, keep, half, after(got_pack, sum_one), half, False)
    got_pack = swap_chip(tiles, members, 0)
    (top,) = pack_step(top, None, 0, after(got_top, other), half, True)
    got_top = swap_chip(top, members, 0)

    tile_one = join_halves(after(where, sum_one, top), tile_one, other, 0, half, range(bands))
    packs = Packs((tiles, sums, half), got_pack, top, got_top, stages, bands, members)
    ups = tuple(after(piece, tile_one) for piece in got_up)
    solved_one = sweep(where, base, tile_one, sum_one, bands, packs, ups)

    low, sums, _ = packs.pack
    base, *pieces = (couple if aligned else couple_plain)(where, sums, solved_one, low, packs.got, rhs, bands)
    tile_zero = join_halves(where, packs.top, packs.got_top, 0, half, ())
    ups = ()
    for mask in range(bands - 1, 0, -1):
        got = lax.ppermute(pieces[mask - 1], "ct", [(i, i ^ mask) for i in range(bands)])
        ups += (after(got, tile_zero),)

    nothing = jnp.zeros((columns, width), F32)
    answer = sweep(where, base, tile_zero, nothing, bands, None, ups, solved_one)
    return jnp.swapaxes(answer, 1, 2)


def solution(mesh):
    members, bands = mesh.shape["rt"], mesh.shape["ct"]
    in_specs = (P("rt", None, "ct", None), P(), P("rt", "ct", None), P(None, "ct", "rt"))
    out_specs = P(None, "ct", "rt")
    body = functools.partial(shards, members=members, bands=bands)
    return jax.shard_map(body, mesh=mesh, in_specs=in_specs, out_specs=out_specs, check_vma=False)
```

```python
import functools

import jax
import jax.numpy as jnp
from jax import lax
from jax.experimental import pallas as pl
from jax.experimental.pallas import tpu as pltpu
from jax.sharding import PartitionSpec as P

F32 = jnp.float32
BF16 = jnp.bfloat16
VMEM = pl.BlockSpec(memory_space=pltpu.MemorySpace.VMEM)
SMEM = pl.BlockSpec(memory_space=pltpu.MemorySpace.SMEM)
HBM = pl.BlockSpec(memory_space=pl.ANY)


def shape(*dims):
    return jax.ShapeDtypeStruct(dims, F32)


def call(body, out, specs, args, name, scratch=(), aliases=None):
    multiple = isinstance(out, tuple)
    return pl.pallas_call(
        body,
        out_shape=out,
        in_specs=list(specs),
        out_specs=tuple(VMEM for _ in out) if multiple else VMEM,
        scratch_shapes=list(scratch),
        input_output_aliases=aliases or {},
        compiler_params=pltpu.CompilerParams(vmem_limit_bytes=40 << 20),
        name=name,
    )(*args)


def split(value):
    high = value.astype(BF16)
    return high, (value - high.astype(F32)).astype(BF16)


def dot_split(a, b, dims):
    (ah, al), (bh, bl) = a, b

    def one(u, v):
        return lax.dot_general(u, v, (dims, ((), ())), preferred_element_type=F32)

    return one(al, bh) + one(ah, bl) + one(ah, bh)


def dot3(a, b):
    return dot_split(split(a), split(b), ((1,), (0,)))


def stage_orders(members):
    bits = members.bit_length() - 1
    first = list(range(1, bits))
    return first, first[::-1]


def swap_core(value, members):
    return lax.ppermute(value, "rt", [(i, i ^ 1) for i in range(members)])


def swap_chip(value, members, stage):
    orders = stage_orders(members)
    return lax.ppermute(value, "rt", [(i, i ^ (1 << orders[i & 1][stage])) for i in range(members)])


def send_tables(members):
    orders = stage_orders(members)
    count = len(orders[0])
    tables = []
    for core in range(2):
        table = []
        for place in range(members):
            other = place >> count
            rest = place & ((1 << count) - 1)
            relative = other
            for stage in range(count):
                if (rest >> (count - 1 - stage)) & 1:
                    relative |= 1 << orders[core ^ other][stage]
            table.append(relative)
        tables.append(table)
    return tables


def front_kernel(
    where_ref, rows_ref, factor_ref, known_ref, keep_one, send_one, keep_ref, send_ref, factor_buf, known_buf, acc_ref, sems, low,
    *, tables
):
    slots, _, band, _ = factor_buf.shape
    me = where_ref[0]

    def live(slot):
        return rows_ref[me * slots + slot] >= 2

    def copies(slot, column):
        copy = pltpu.make_async_copy(factor_ref.at[slot, column], factor_buf.at[slot, column], sems.at[column, slot])
        if column == 0:
            return [copy]
        return [pltpu.make_async_copy(known_ref.at[slot], known_buf.at[slot], sems.at[2, slot]), copy]

    for column in (1, 0):
        for slot in range(slots):

            @pl.when(live(slot))
            def _():
                for copy in copies(slot, column):
                    copy.start()

    finish = put_band(where_ref, rows_ref, factor_ref, 1, 0, keep_ref, send_ref, 0, band // 2, low)
    for column, keep, send, first in ((1, keep_one, send_one, 0), (0, keep_ref, send_ref, band // 2)):
        acc_ref[...] = jnp.zeros_like(acc_ref)
        for slot in range(slots):

            @pl.when(live(slot))
            def _():
                for copy in copies(slot, column):
                    copy.wait()
                acc_ref[...] += dot_split(split(known_buf[slot]), split(factor_buf[slot, column]), ((0,), (0,)))

        in_send_order(where_ref, acc_ref, keep, send, first, tables)
    finish()


def in_send_order(where_ref, acc_ref, keep_ref, send_ref, first, tables):
    count = len(tables[0])
    columns = acc_ref.shape[0] // count
    me = where_ref[0]
    for spot, (even, odd) in enumerate(zip(*tables)):
        group = me ^ jnp.where((me & 1) == 0, even, odd)
        rows = acc_ref[pl.ds(pl.multiple_of(group * columns, columns), columns), :]
        target, start = (keep_ref, spot) if spot < count // 2 else (send_ref, spot - count // 2)
        target[first + start * columns : first + (start + 1) * columns, :] = rows


def owned_slot(where_ref, rows_ref, row, slots):
    slot = jnp.int32(-1)
    for s in range(slots):
        slot = jnp.where(rows_ref[where_ref[0] * slots + s] == row, s, slot)
    return slot


def band_copies(where_ref, factor_ref, slot, column, keep_ref, send_ref, first, half, sems):
    core = where_ref[0] & 1
    copies = []
    for index, (target, which) in enumerate(((send_ref, 1 - core), (keep_ref, core))):
        start = pl.multiple_of(which * half, half)
        source = factor_ref.at[slot, column, pl.ds(start, half), :]
        copies.append(pltpu.make_async_copy(source, target.at[pl.ds(first, half), :], sems.at[index]))
    return copies


def put_band(where_ref, rows_ref, factor_ref, row, column, keep_ref, send_ref, first, half, sems):
    slot = owned_slot(where_ref, rows_ref, row, factor_ref.shape[0])

    @pl.when(slot >= 0)
    def _():
        for copy in band_copies(where_ref, factor_ref, slot, column, keep_ref, send_ref, first, half, sems):
            copy.start()

    @pl.when(slot < 0)
    def _():
        keep_ref[first : first + half, :] = jnp.zeros((half, keep_ref.shape[1]), F32)
        send_ref[first : first + half, :] = jnp.zeros((half, keep_ref.shape[1]), F32)

    def finish():
        @pl.when(slot >= 0)
        def _():
            for copy in band_copies(where_ref, factor_ref, slot, column, keep_ref, send_ref, first, half, sems):
                copy.wait()

    return finish


def first_band(where, slot_row, factor_rows):
    _, _, band, width = factor_rows.shape
    half = band // 2

    def body(where_ref, rows_ref, factor_ref, keep_ref, send_ref, sems):
        put_band(where_ref, rows_ref, factor_ref, 1, 1, keep_ref, send_ref, 0, half, sems)()

    out = (shape(half, width), shape(half, width))
    scratch = [pltpu.SemaphoreType.DMA((2,))]
    return call(body, out, (SMEM, SMEM, HBM), (where, slot_row, factor_rows), "first_band", scratch)


def front(where, slot_row, factor_rows, known, members):
    slots, _, band, width = factor_rows.shape
    total = known.shape[2]
    one, rest = shape(total // 2, width), shape(band // 2 + total // 2, width)
    scratch = [
        pltpu.VMEM(factor_rows.shape, F32),
        pltpu.VMEM(known.shape, F32),
        pltpu.VMEM((total, width), F32),
        pltpu.SemaphoreType.DMA((3, slots)),
        pltpu.SemaphoreType.DMA((2,)),
    ]
    body = functools.partial(front_kernel, tables=send_tables(members))
    args = (where, slot_row, factor_rows, known)
    return call(body, (one, one, rest, rest), (SMEM, SMEM, HBM, HBM), args, "front", scratch)


def top_band(where, slot_row, factor_rows):
    slots, _, band, width = factor_rows.shape
    half = band // 2

    def body(where_ref, rows_ref, factor_ref, keep_ref, send_ref, tile_ref, sem):
        slot = owned_slot(where_ref, rows_ref, 0, slots)
        core = where_ref[0] & 1

        @pl.when(slot >= 0)
        def _():
            copy = pltpu.make_async_copy(factor_ref.at[slot, 0], tile_ref, sem)
            copy.start()
            copy.wait()
            invert_diagonal(tile_ref, where_ref[1], range(width // band), band)
            keep_ref[...] = tile_ref[pl.ds(pl.multiple_of(core * half, half), half), :]
            send_ref[...] = tile_ref[pl.ds(pl.multiple_of((1 - core) * half, half), half), :]

        @pl.when(slot < 0)
        def _():
            keep_ref[...] = jnp.zeros_like(keep_ref)
            send_ref[...] = jnp.zeros_like(send_ref)

    out = (shape(half, width), shape(half, width))
    scratch = [pltpu.VMEM((band, width), F32), pltpu.SemaphoreType.DMA(())]
    return call(body, out, (SMEM, SMEM, HBM), (where, slot_row, factor_rows), "top_band", scratch)


def finish_sum(where, value, got, rhs, bands):
    columns, width = got.shape
    band = width // bands

    def body(where_ref, value_ref, got_ref, rhs_ref, total_ref, base_ref, *piece_refs):
        total_ref[...] = value_ref[:columns, :] + got_ref[...]
        place = where_ref[1]

        def own(spot):
            return total_ref[:, pl.ds(pl.multiple_of(spot * band, band), band)]

        base_ref[...] = rhs_ref[1] - own(place)
        for shift, piece_ref in enumerate(piece_refs, 1):
            piece_ref[...] = own(jnp.minimum(place + shift, bands - 1))

    out = (shape(columns, width),) + (shape(columns, band),) * bands
    total, base, *pieces = call(body, out, (SMEM,) + (VMEM,) * 3, (where, value, got, rhs), "finish_sum")
    return total, base, pieces


def finish_plain(where, value, got, rhs, bands):
    total = value[: got.shape[0]] + got
    band = total.shape[1] // bands
    spots = [jnp.minimum(where[1] + shift, bands - 1) for shift in range(bands)]
    base, *pieces = [own_band(total, spot, band) for spot in spots]
    return total, rhs[1] - base, pieces


def after(value, *others):
    return lax.optimization_barrier((value,) + others)[0]


def pack_parts(sums, skip, got, tile_rows, final):
    width = got.shape[1]
    count = got.shape[0] - tile_rows
    go = count if final else count // 2

    def add(tiles_ref, sums_ref, got_ref, out_ref, keep_ref):
        out_ref[:tile_rows, :] = tiles_ref[:tile_rows, :] + got_ref[:tile_rows, :]
        keep_ref[...] = sums_ref[skip : skip + go, :] + got_ref[tile_rows : tile_rows + go, :]
        if not final:
            out_ref[tile_rows:, :] = sums_ref[skip + go : skip + count, :] + got_ref[tile_rows + go :, :]

    def add_tile(tiles_ref, got_ref, out_ref):
        out_ref[...] = tiles_ref[...] + got_ref[...]

    if sums is None:
        return add_tile, (shape(tile_rows, width),)
    return add, (shape(tile_rows + count - go, width), shape(go, width))


def pack_inputs(tiles, sums, skip, got, tile_rows, final):
    return (tiles, got) if sums is None else (tiles, sums, got)


def pack_step(*pack):
    add, out = pack_parts(*pack[1:])
    args = pack_inputs(*pack)
    return call(add, out, (VMEM,) * len(args), args, "pack_step")


def inverse_of(block):
    size = block.shape[0]
    base = min(size, 64)
    row = lax.broadcasted_iota(jnp.int32, (base, base), 0)
    col = lax.broadcasted_iota(jnp.int32, (base, base), 1)
    pair = (row - col == 1) & (row & 1 == 1)
    starts = range(0, size, base)
    blocks = [block[at : at + base, at : at + base] for at in starts]
    inverses = []
    for part in blocks:
        diag = jnp.where(row == col, part, 0.0)
        recip_row = 1.0 / jnp.sum(diag, axis=0, keepdims=True)
        recip_col = 1.0 / jnp.sum(diag, axis=1, keepdims=True)
        off = -(part * recip_row) * recip_col
        inverses.append(jnp.where(row == col, recip_row, jnp.where(pair, off, 0.0)))
    step = 2
    while step < base:
        half = lax.div(row, step)
        below = (half - lax.div(col, step) == 1) & (half & 1 == 1)
        parts = [split(inverse) for inverse in inverses]
        middle = [dot_split(split(jnp.where(below, b, 0.0)), p, ((1,), (0,))) for b, p in zip(blocks, parts)]
        inverses = [i - dot_split(p, split(m), ((1,), (0,))) for i, p, m in zip(inverses, parts, middle)]
        step *= 2
    width = base
    while len(inverses) > 1:
        merged = []
        for index in range(0, len(inverses), 2):
            first, second = inverses[index : index + 2]
            lower = block[(index + 1) * width : (index + 2) * width, index * width : (index + 1) * width]
            corner = -dot3(second, dot3(lower, first))
            top = jnp.concatenate([first, jnp.zeros_like(first)], 1)
            merged.append(jnp.concatenate([top, jnp.concatenate([corner, second], 1)], 0))
        inverses = merged
        width *= 2
    return inverses[0]


def invert_diagonal(tile_ref, place, chosen, band):
    for spot in chosen:

        @pl.when(place == spot)
        def _():
            here = slice(spot * band, (spot + 1) * band)
            tile_ref[:, here] = inverse_of(tile_ref[:, here])


def join_halves(where, mine, other, first, half, chosen):
    width = mine.shape[1]

    def body(where_ref, mine_ref, other_ref, tile_ref):
        core = where_ref[0] & 1
        tile_ref[pl.ds(pl.multiple_of(core * half, half), half), :] = mine_ref[first : first + half, :]
        tile_ref[pl.ds(pl.multiple_of((1 - core) * half, half), half), :] = other_ref[first : first + half, :]
        invert_diagonal(tile_ref, where_ref[1], chosen, 2 * half)

    return call(body, shape(2 * half, width), (SMEM, VMEM, VMEM), (where, mine, other), "join")


def run_stage(where, base, tile, add, near, far, held, stage, packs=(), ups=(), other=None):
    columns, band = base.shape
    left = stage * band
    wide = far is None
    first = 0 if wide else max(left - band, 0)
    width = max(left, band) - first
    inputs = [pack_inputs(*pack) for pack in packs]
    more = [pack_parts(*pack[1:]) for pack in packs]
    count = sum(len(args) for args in inputs)
    come = (near,) if wide else (near, far)
    stacked = other is not None
    extra = ups + ((other,) if stacked else ())

    def body(where_ref, base_ref, tile_ref, add_ref, held_ref, *refs):
        come_refs, refs = refs[: len(come)], refs[len(come) :]
        extra_refs, refs = refs[: len(extra)], refs[len(extra) :]
        ins, (solved_ref, update_ref), outs = refs[:count], refs[count : count + 2], refs[count + 2 :]
        if stacked:
            solved_ref[1] = extra_refs[-1][...]
            solved_ref = solved_ref.at[0]

        @pl.when(where_ref[1] == stage)
        def _():
            if wide:
                right = base_ref[...] - come_refs[0][:, left:]
            else:
                right = base_ref[...] - come_refs[0][...] - come_refs[1][:, left : left + band]
            for up_ref in extra_refs[: len(ups)]:
                right = right - up_ref[...]
            solved = dot3(right, tile_ref[:, left : left + band])
            solved_ref[...] = solved
            if stage > 0:
                here = slice(first, left)
                passed = come_refs[-1][:, here] + add_ref[:, here]
                update_ref[...] = passed + dot3(solved, tile_ref[:, here])

        @pl.when(where_ref[1] != stage)
        def _():
            solved_ref[...] = held_ref[...]

        for args, (add_pack, out) in zip(inputs, more):
            add_pack(*ins[: len(args)], *outs[: len(out)])
            ins, outs = ins[len(args) :], outs[len(out) :]

    answer = shape(2, columns, band) if stacked else shape(columns, band)
    out = (answer, shape(columns, width)) + sum((out for _, out in more), ())
    args = (where, base, tile, add, held) + come + extra + sum(inputs, ())
    return call(body, out, (SMEM,) + (VMEM,) * (len(args) - 1), args, "stage")


def run_rest(where, tile, add, far, solved, stage):
    columns, band = solved.shape
    last = (stage - 1) * band

    def body(where_ref, tile_ref, add_ref, far_ref, solved_ref, rest_ref):
        @pl.when(where_ref[1] == stage)
        def _():
            rest_ref[...] = far_ref[:, :last] + add_ref[:, :last] + dot3(solved_ref[...], tile_ref[:, :last])

    return call(body, shape(columns, last), (SMEM,) + (VMEM,) * 4, (where, tile, add, far, solved), "rest")


def run_stage_plain(where, base, tile, add, near, far, held, stage, packs=(), ups=(), other=None):
    high = lax.Precision.HIGHEST
    band = base.shape[1]
    left = stage * band
    here = slice(max(left - band, 0), max(left, band))
    solved = jnp.dot(base - near - far[:, left : left + band] - sum(ups), tile[:, left : left + band], precision=high)
    update = jnp.dot(solved, tile[:, here], precision=high) + add[:, here] + far[:, here]
    more = sum((tuple(pack_step(*pack)) for pack in packs), ())
    solved = jnp.where(where[1] == stage, solved, held)
    return (solved if other is None else jnp.stack([solved, other]), update) + more


def run_rest_plain(where, tile, add, far, solved, stage):
    last = (stage - 1) * solved.shape[1]
    return far[:, :last] + add[:, :last] + jnp.dot(solved, tile[:, :last], precision=lax.Precision.HIGHEST)


def sweep(where, base, tile, add, bands, packs=None, ups=(), other=None):
    columns, band = base.shape
    aligned = band % 128 == 0
    wide = packs is not None and aligned
    stage_of, rest_of = (run_stage, run_rest) if aligned else (run_stage_plain, run_rest_plain)
    near = jnp.zeros((columns, bands * band if wide else band), F32)
    held = jnp.zeros((columns, band), F32)
    fars = [None] * bands if wide else [jnp.zeros((columns, bands * band), F32)] * 2
    for stage in range(bands - 1, -1, -1):
        far = fars.pop(0)
        taken = packs.take(bands - 1 - stage) if packs else ()
        last = other if stage == 0 else None
        held, update, *more = stage_of(where, base, tile, add, near, far, held, stage, taken, ups, last)
        if stage > 0:
            near = lax.ppermute(update, "ct", [(stage, stage - 1)])
        if stage > 1 and not wide:
            rest = rest_of(where, tile, add, far, held, stage)
            fars.append(lax.ppermute(rest, "ct", [(stage, stage - 2)]))
        if more:
            packs.put(*more)
        if packs:
            near = packs.loose(held, near)
    return held


class Packs:
    def __init__(self, pack, got, top, got_top, steps, bands, members):
        self.pack, self.got, self.top, self.got_top = pack, got, top, got_top
        self.steps, self.members = steps, members
        self.low_at = [bands - 2 - 2 * (steps - 1 - step) for step in range(steps - 1)]
        self.loose_at = bands - 2
        self.top_at = [bands - steps + step for step in range(steps)]

    def take(self, index):
        taken = ()
        if index in self.low_at:
            tiles, sums, rows = self.pack
            taken += ((tiles, sums, 0, self.got, rows, False),)
        if index in self.top_at:
            taken += ((self.top, None, 0, self.got_top, self.top.shape[0], True),)
        self.index = index
        return taken

    def loose(self, held, near):
        if self.index != self.loose_at:
            return near
        tiles, sums, rows = self.pack
        tiles, sums = pack_step(tiles, sums, 0, after(self.got, held), rows, True)
        self.pack = (tiles, sums, rows)
        self.got = swap_core(tiles, self.members)
        return after(near, tiles)

    def put(self, *outs):
        if self.index in self.low_at:
            tiles, sums, *outs = outs
            self.pack = (tiles, sums, self.pack[2])
            step = self.low_at.index(self.index) + 1
            if step < self.steps:
                self.got = swap_chip(tiles, self.members, step)
            else:
                self.got = swap_core(tiles, self.members)
        if self.index in self.top_at:
            (self.top,) = outs
            step = self.top_at.index(self.index) + 1
            if step < self.steps:
                self.got_top = swap_chip(self.top, self.members, step)
            else:
                self.got_top = swap_core(self.top, self.members)


def couple(where, sums, solved, mine, other, rhs, bands):
    columns, band = solved.shape
    half, width = mine.shape

    def body(where_ref, sums_ref, solved_ref, mine_ref, other_ref, rhs_ref, *refs):
        outs, (tile_ref, whole_ref) = refs[:bands], refs[bands:]
        core = where_ref[0] & 1
        tile_ref[pl.ds(pl.multiple_of(core * half, half), half), :] = mine_ref[...]
        tile_ref[pl.ds(pl.multiple_of((1 - core) * half, half), half), :] = other_ref[...]
        whole_ref[...] = sums_ref[...] + dot3(solved_ref[...], tile_ref[...])
        for mask, out_ref in enumerate(outs):
            start = pl.multiple_of((where_ref[1] ^ mask) * band, band)
            piece = whole_ref[:, pl.ds(start, band)]
            out_ref[...] = piece if mask else rhs_ref[0] - piece

    scratch = [pltpu.VMEM((band, width), F32), pltpu.VMEM((columns, width), F32)]
    args = (where, sums, solved, mine, other, rhs)
    return call(body, (shape(columns, band),) * bands, (SMEM,) + (VMEM,) * 5, args, "couple", scratch)


def couple_plain(where, sums, solved, mine, other, rhs, bands):
    band = solved.shape[1]
    tile = join_halves(where, mine, other, 0, band // 2, ())
    whole = sums + jnp.dot(solved, tile, precision=lax.Precision.HIGHEST)
    pieces = [own_band(whole, where[1] ^ mask, band) for mask in range(bands)]
    return [rhs[0] - pieces[0]] + pieces[1:]


def own_band(value, spot, band):
    return lax.dynamic_slice(value, (0, spot * band), (value.shape[0], band))


def shards(factor_rows, slot_row, known, rhs, *, members, bands):
    slots, _, band, width = factor_rows.shape
    half = band // 2
    columns = rhs.shape[2]
    stages = len(stage_orders(members)[0])
    aligned = band % 128 == 0
    place = lax.axis_index("ct")
    where = jnp.stack([lax.axis_index("rt"), place]).astype(jnp.int32)
    factor_rows = pltpu.with_memory_space_constraint(factor_rows, pltpu.HBM)
    known = pltpu.with_memory_space_constraint(known, pltpu.HBM)
    rhs = jnp.swapaxes(rhs, 1, 2)

    keep, send = first_band(where, slot_row, factor_rows)
    tile_one = keep + swap_core(send, members)
    got_tile = swap_chip(tile_one, members, 0)
    keep_one, send_one, keep, send = front(after(where, tile_one), slot_row, factor_rows, known, members)
    got_sum = swap_core(send_one, members)
    tile_one = tile_one + after(got_tile, keep_one)
    got_tile = swap_chip(tile_one, members, 1)
    sum_one = keep_one + after(got_sum, tile_one)
    got_pack = got_top = top = None
    for stage in range(stages):
        rows = sum_one.shape[0] // 2
        got_sum = swap_chip(sum_one[rows:], members, stage)
        if stage == 0:
            got_pack = swap_core(after(send, sum_one), members)
            top, send_top = top_band(after(where, sum_one), slot_row, factor_rows)
            got_sum = after(got_sum, top)
        if stage < stages - 1:
            sum_one = sum_one[:rows] + got_sum
        else:
            finish = finish_sum if aligned else finish_plain
            sum_one, base, pieces = finish(where, sum_one, got_sum, rhs, bands)
        if stage == 0:
            got_top = swap_core(after(send_top, sum_one), members)
        if stage < stages - 1:
            tile_one = tile_one + after(got_tile, sum_one)
            got_tile = swap_chip(tile_one, members, stage + 2) if stage < stages - 2 else None

    got_up = []
    for shift in range(bands - 1, 0, -1):
        got_up.append(lax.ppermute(pieces[shift - 1], "ct", [(i, i + shift) for i in range(bands - shift)]))

    other = swap_core(tile_one, members)

    tiles, sums = pack_step(keep, keep, half, after(got_pack, sum_one), half, False)
    got_pack = swap_chip(tiles, members, 0)
    (top,) = pack_step(top, None, 0, after(got_top, other), half, True)
    got_top = swap_chip(top, members, 0)

    tile_one = join_halves(after(where, sum_one, top), tile_one, other, 0, half, range(bands))
    packs = Packs((tiles, sums, half), got_pack, top, got_top, stages, bands, members)
    ups = tuple(after(piece, tile_one) for piece in got_up)
    solved_one = sweep(where, base, tile_one, sum_one, bands, packs, ups)

    low, sums, _ = packs.pack
    base, *pieces = (couple if aligned else couple_plain)(where, sums, solved_one, low, packs.got, rhs, bands)
    tile_zero = join_halves(where, packs.top, packs.got_top, 0, half, ())
    ups = ()
    for mask in range(bands - 1, 0, -1):
        got = lax.ppermute(pieces[mask - 1], "ct", [(i, i ^ mask) for i in range(bands)])
        ups += (after(got, tile_zero),)

    nothing = jnp.zeros((columns, width), F32)
    answer = sweep(where, base, tile_zero, nothing, bands, None, ups, solved_one)
    return jnp.swapaxes(answer, 1, 2)


def solution(mesh):
    members, bands = mesh.shape["rt"], mesh.shape["ct"]
    in_specs = (P("rt", None, "ct", None), P(), P("rt", "ct", None), P(None, "ct", "rt"))
    out_specs = P(None, "ct", "rt")
    body = functools.partial(shards, members=members, bands=bands)
    return jax.shard_map(body, mesh=mesh, in_specs=in_specs, out_specs=out_specs, check_vma=False)
```
